32 devices in a mesh: groups: 2 (over y), seq: 16 (over z, x, core).
Axes of the slice: x: 2, y: 2, z: 4, core: 2. Of those that a mesh axis runs over, the one named last changes fastest.
Arguments:
- queries: bfloat16 [4, 128, 128, 128], P('groups', 'seq'), parts along dimension 0, may hold values from -64 to 64
- new_k: bfloat16 [4, 128, 8, 128], P('groups', 'seq'), parts along dimension 0, may hold values from -15 to 15
- new_v: bfloat16 [4, 128, 8, 128], P('groups', 'seq'), parts along dimension 0, may hold values from -6 to 6
- cache_k: bfloat16 [4, 8192, 8, 128], P('groups', 'seq'), parts along dimension 0, may hold values from -12 to 12
- cache_v: bfloat16 [4, 8192, 8, 128], P('groups', 'seq'), parts along dimension 0, may hold values from -6 to 6
- cache_len: int32 [4], P('groups'), parts along dimension 0, may hold values from 2048 to 8192
Outputs:
- attended: bfloat16 [4, 128, 128, 128], P('groups', 'seq'), parts along dimension 0
The draws below stay inside these ranges and needn't reach their ends.
There are 2 independent parts, one for each index of `groups`. The reference program is written for one: setup_inputs(seed, part) draws one part's arguments, and reference() takes and returns one part's arrays. A program takes and returns all parts, laid end to end along the dimension named above; each array names one. Nothing has to cross between parts.
Inputs may be any that keep to these rules, and one draw needn't show every extreme that they name: The first cache_len[r] of the 8192 cache slots of request r hold keys and values; the rest are to be ignored.
All inputs are finite; a program needn't handle non-finite values.
Results may differ from the reference program's by a relative error of at most 0.004.
Values may be sent and summed in bfloat16 or wider, within the bound.
No kernel may reach another device: no remote copies, remote signals or barrier semaphores. Data moves between devices by JAX's collectives and lax.ppermute only.
A program may use at most 128 MiB of HBM per device.

```python
import math
import jax
import jax.numpy as jnp
from jax import lax

H = 128
KVH = 8
HD = 128
REQS = 2
NEW = 128
CTX_DEV = 512
CTX = 8192
N_SEQ = 16


def attention_field(key):
    seeded = jax.random.fold_in(key, 7)
    key_field = 2.0 * jnp.clip(jax.random.normal(jax.random.fold_in(seeded, 1), (REQS, CTX, KVH, HD), jnp.float32), -6.0, 6.0)
    query_field = 2.0 * jnp.clip(jax.random.normal(jax.random.fold_in(seeded, 2), (REQS, NEW, H, HD), jnp.float32), -6.0, 6.0)
    return (key_field, query_field)


def draw_queries(key, part):
    return attention_field(key)[1].astype(jnp.bfloat16)


def draw_cache_k(key, part):
    return attention_field(key)[0].astype(jnp.bfloat16)


def block_scale(key, dims, shards, smallest, top_value):
    def one(dim, shards_of):
        steps = jax.random.uniform(jax.random.fold_in(jax.random.fold_in(key, 6), dim), (shards_of,), jnp.float32, smallest / len(shards), top_value / len(shards))
        return jnp.repeat(jnp.exp(steps), dims[dim] // shards_of).reshape((-1,) + (1,) * (len(dims) - dim - 1))

    gain = one(*shards[0])
    for cut in shards[1:]:
        gain = gain * one(*cut)
    return gain


def centred(key, extent, scale, limit, pieces=(), held_as=jnp.bfloat16):
    result = scale * jax.random.normal(key, extent, jnp.float32)
    if pieces:
        result = result * block_scale(key, extent, pieces, -0.22, 0.18)
    return jnp.clip(result, -limit, limit).astype(held_as)


def setup_inputs(seed: int = 0, part: int = 0) -> dict:
    key_of = jax.random.split(jax.random.key(seed), 7)
    own_keys = jax.random.split(jax.random.fold_in(key_of[6], part), 7)
    return {
        "queries": draw_queries(jax.random.fold_in(jax.random.fold_in(key_of[6], part), 71), part),
        "new_k": centred(own_keys[1], (REQS, NEW, KVH, HD), 2.5, 15.0, ((1, 16),)),
        "new_v": centred(own_keys[2], (REQS, NEW, KVH, HD), 1.0, 6.0, ((1, 16),)),
        "cache_k": draw_cache_k(jax.random.fold_in(jax.random.fold_in(key_of[6], part), 71), part),
        "cache_v": centred(own_keys[4], (REQS, CTX, KVH, HD), 1.0, 6.0, ((1, 16),)),
        "cache_len": jax.random.randint(own_keys[5], (REQS,), CTX // 4, CTX + 1).astype(jnp.int32),
    }


def reference(queries, new_k, new_v, cache_k, cache_v, cache_len):
    group_size = H // KVH
    scaling = 1.0 / math.sqrt(HD)
    query_f32 = queries.astype(jnp.float32).reshape(REQS, NEW, KVH, group_size, HD)
    key_blocks = jnp.moveaxis(cache_k.reshape(REQS, N_SEQ, CTX_DEV, KVH, HD), 1, 0)
    value_blocks = jnp.moveaxis(cache_v.reshape(REQS, N_SEQ, CTX_DEV, KVH, HD), 1, 0)

    def absorb(state, scores, valid, values):
        row_max, row_sum, partial_value = state
        scores = jnp.where(valid, scores, -1e+30)
        new_max = jnp.maximum(row_max, lax.optimization_barrier(jnp.max(scores, axis=-1)))
        weights = jnp.where(valid, jnp.exp(scores - new_max[..., None]), 0.0)
        rescale = jnp.exp(row_max - new_max)
        row_sum = row_sum * rescale + lax.optimization_barrier(jnp.sum(weights, axis=-1))
        rounded = weights.astype(jnp.bfloat16).astype(jnp.float32)
        partial_value = partial_value * rescale[..., None] + jnp.einsum('rnkgc,rckd->rnkgd', rounded, values.astype(jnp.float32))
        return (new_max, row_sum, partial_value)

    def step(state, inputs):
        key_block, value_block, block_index = inputs
        scores = jnp.einsum('rnkgd,rckd->rnkgc', query_f32, key_block.astype(jnp.float32)) * scaling
        slot_pos = block_index * CTX_DEV + jnp.arange(CTX_DEV, dtype=jnp.int32)
        valid = (slot_pos[None, :] < cache_len[:, None])[:, None, None, None, :]
        return (absorb(state, scores, valid, value_block), None)
    start_state = (jnp.full((REQS, NEW, KVH, group_size), -1e+30, jnp.float32), jnp.zeros((REQS, NEW, KVH, group_size), jnp.float32), jnp.zeros((REQS, NEW, KVH, group_size, HD), jnp.float32))
    state, _ = lax.scan(step, start_state, (key_blocks, value_blocks, jnp.arange(N_SEQ, dtype=jnp.int32)))
    fresh_scores = jnp.einsum('rnkgd,rukd->rnkgu', query_f32, new_k.astype(jnp.float32)) * scaling
    positions = jnp.arange(NEW, dtype=jnp.int32)
    fresh_valid = (positions[None, :] <= positions[:, None])[None, :, None, None, :]
    row_max, row_sum, partial_value = absorb(state, fresh_scores, fresh_valid, new_v)
    merged = partial_value / row_sum[..., None]
    return merged.reshape(REQS, NEW, H, HD).astype(jnp.bfloat16)
```

```python
import functools
import math

import jax
import jax.numpy as jnp
from jax import lax
from jax.experimental import pallas as pl
from jax.experimental.pallas import tpu as pltpu
from jax.sharding import PartitionSpec as P

NEG = -1e30
STAT_ROWS = 8
VMEM_BYTES = 58 * 2**20


def attend_kernel(
    info_ref, q_ref, k_ref, v_ref, fk_ref, fv_ref, out_ref, vals, fvals, s0, s1, m0, m1, *, chunk, tile, group_size
):
    sources, per_source, dim = q_ref.shape
    slots = k_ref.shape[0] * k_ref.shape[1]
    per_chunk = chunk // k_ref.shape[1]
    fresh = fk_ref.shape[0]
    rows = sources * per_source
    tiles = rows // tile
    span = tile // per_source
    scale = math.log2(math.e) / math.sqrt(dim)
    valid = info_ref[0]
    fresh_shift = info_ref[1]

    vals[:, :dim] = v_ref[...].reshape(slots, dim)
    vals[:, dim:] = jnp.ones((slots, dim), jnp.bfloat16)
    fvals[:, :dim] = fv_ref[...]
    fvals[:, dim:] = jnp.ones((fresh, dim), jnp.bfloat16)

    def product(a, b):
        return lax.dot_general(a, b, (((1,), (1,)), ((), ())), preferred_element_type=jnp.float32)

    def lane_max(scores, best):
        for lane in range(scores.shape[1] // dim):
            part = scores[:, lane * dim : (lane + 1) * dim]
            best = part if best is None else jnp.maximum(best, part)
        return best

    def score_chunk(t, j, count, s_ref, best):
        q = q_ref[pl.ds(t * span, span)].reshape(tile, dim)
        if j < count:
            keys = k_ref[j * per_chunk : (j + 1) * per_chunk].reshape(chunk, dim)
            scores = product(q, keys)
            if j == count - 1:
                pos = j * chunk + lax.broadcasted_iota(jnp.int32, (1, chunk), 1)
                scores = scores + jnp.where(pos < valid, 0.0, NEG)
            s_ref[:, j * chunk : (j + 1) * chunk] = scores
            return lane_max(scores, best)
        scores = product(q, fk_ref[...])
        token = (t * tile + lax.broadcasted_iota(jnp.int32, (tile, 1), 0)) // group_size
        unit = lax.broadcasted_iota(jnp.int32, (tile, fresh), 1)
        scores = jnp.where(unit <= token + fresh_shift, scores, NEG)
        s_ref[:, slots : slots + fresh] = scores
        return lane_max(scores, best)

    def value_chunk(j, count, s_ref, top, acc):
        if j < count:
            scores = s_ref[:, j * chunk : (j + 1) * chunk]
            values = vals[j * chunk : (j + 1) * chunk, :]
        else:
            scores = s_ref[:, slots : slots + fresh]
            values = fvals[...]
        weights = jnp.exp2((scores - top) * scale).astype(jnp.bfloat16)
        part = jnp.dot(weights, values, preferred_element_type=jnp.float32)
        return part if acc is None else acc + part

    def stage(t_next, s_next, m_next, t_now, s_now, m_now, count):
        best = None
        acc = None
        if t_now is not None:
            top = jnp.max(m_now[...], axis=1, keepdims=True)
        for j in range(count + 1):
            if t_next is not None:
                best = score_chunk(t_next, j, count, s_next, best)
            if t_now is not None:
                acc = value_chunk(j, count, s_now, top, acc)
        if t_next is not None:
            m_next[...] = best
        if t_now is not None:
            total = acc[:, dim:]
            out = (acc[:, :dim] / total).astype(jnp.bfloat16)
            out_ref[pl.ds(t_now * span, span), :per_source, :] = out.reshape(span, per_source, dim)
            level = top * scale + jnp.log2(total)
            for first in range(0, tile, dim):
                flat = jnp.transpose(level[first : first + dim, :])[:STAT_ROWS]
                high = flat.astype(jnp.bfloat16)
                rest = flat - high.astype(jnp.float32)
                mid = rest.astype(jnp.bfloat16)
                low = (rest - mid.astype(jnp.float32)).astype(jnp.bfloat16)
                which = lax.broadcasted_iota(jnp.int32, flat.shape, 0)
                stats = jnp.where(
                    which == 0,
                    high.astype(jnp.float32),
                    jnp.where(which == 1, mid.astype(jnp.float32), low.astype(jnp.float32)),
                ).astype(jnp.bfloat16)
                width = min(per_source, dim)
                for part in range(dim // width):
                    row = first + part * width
                    out_ref[
                        t_now * span + row // per_source, per_source:, :width
                    ] = stats[:, part * width : (part + 1) * width]

    for count in range(slots // chunk + 1):

        @pl.when((valid > (count - 1) * chunk) & (valid <= count * chunk))
        def _(count=count):
            stage(0, s0, m0, None, None, None, count)

            def pair(i, carry):
                stage(2 * i + 1, s1, m1, 2 * i, s0, m0, count)
                stage(jnp.minimum(2 * i + 2, tiles - 1), s0, m0, 2 * i + 1, s1, m1, count)
                return carry

            lax.fori_loop(0, tiles // 2, pair, 0)


def attend(request, info, head_q, keys, values, fresh_k, fresh_v, per_source, group_size):
    sources, _, dim = head_q.shape
    slots = keys.shape[0] * keys.shape[1]
    rows = sources * per_source
    fresh = fresh_k.shape[0]
    tile = min(256, rows // 2)
    chunk = min(1024, slots)

    def whole(array):
        return pl.BlockSpec(array.shape, lambda i, s: (0,) * array.ndim)

    return pl.pallas_call(
        functools.partial(attend_kernel, chunk=chunk, tile=tile, group_size=group_size),
        grid_spec=pltpu.PrefetchScalarGridSpec(
            num_scalar_prefetch=1,
            grid=(1,),
            in_specs=[
                pl.BlockSpec((sources, per_source, dim), lambda i, s: (0, request, 0)),
                whole(keys),
                whole(values),
                whole(fresh_k),
                whole(fresh_v),
            ],
            out_specs=pl.BlockSpec((sources, per_source + STAT_ROWS, dim), lambda i, s: (0, 0, 0)),
            scratch_shapes=[
                pltpu.VMEM((slots, 2 * dim), jnp.bfloat16),
                pltpu.VMEM((fresh, 2 * dim), jnp.bfloat16),
                pltpu.VMEM((tile, slots + fresh), jnp.float32),
                pltpu.VMEM((tile, slots + fresh), jnp.float32),
                pltpu.VMEM((tile, dim), jnp.float32),
                pltpu.VMEM((tile, dim), jnp.float32),
            ],
        ),
        out_shape=jax.ShapeDtypeStruct((sources, per_source + STAT_ROWS, dim), jnp.bfloat16),
        compiler_params=pltpu.CompilerParams(vmem_limit_bytes=VMEM_BYTES),
        cost_estimate=pl.CostEstimate(
            flops=4 * rows * slots * dim,
            bytes_accessed=4 * slots * dim + 4 * rows * dim,
            transcendentals=rows * slots,
        ),
    )(info, head_q, keys, values, fresh_k, fresh_v)


def merge_kernel(part_ref, out_ref, *, group_size):
    spread, heads, _, dim = part_ref.shape
    local_rows = out_ref.shape[0]
    per_source = local_rows * group_size
    for h in range(heads):
        levels = []
        for b in range(spread):
            stats = part_ref[b, h, per_source : per_source + STAT_ROWS, :].astype(jnp.float32)
            level = stats[0:1] + stats[1:2] + stats[2:3]
            levels.append(jnp.transpose(jnp.broadcast_to(level, (dim, dim)))[:per_source])
        top = functools.reduce(jnp.maximum, levels)
        weights = [jnp.exp2(level - top) for level in levels]
        total = functools.reduce(jnp.add, weights)
        mixed = functools.reduce(
            jnp.add,
            [w * part_ref[b, h, :per_source, :].astype(jnp.float32) for b, w in enumerate(weights)],
        )
        out = (mixed / total).astype(jnp.bfloat16)
        out_ref[:, h * group_size : (h + 1) * group_size, :] = out.reshape(local_rows, group_size, dim)


def merge(parts, local_rows, group_size):
    spread, heads, _, dim = parts.shape
    return pl.pallas_call(
        functools.partial(merge_kernel, group_size=group_size),
        out_shape=jax.ShapeDtypeStruct((local_rows, heads * group_size, dim), jnp.bfloat16),
        compiler_params=pltpu.CompilerParams(vmem_limit_bytes=VMEM_BYTES),
    )(parts)


def shards(queries, new_k, new_v, cache_k, cache_v, cache_len):
    requests, local_rows, heads, head_dim = queries.shape
    slots = cache_k.shape[1]
    kv_heads = cache_k.shape[2]
    group_size = heads // kv_heads
    devices_seq = lax.axis_size("seq")
    seq_index = lax.axis_index("seq")
    spread = devices_seq // kv_heads
    block = seq_index // kv_heads
    per_source = local_rows * group_size
    blocks = [[b * kv_heads + h for h in range(kv_heads)] for b in range(spread)]

    grouped = jnp.transpose(
        queries.reshape(requests, local_rows, kv_heads, group_size, head_dim), (2, 0, 1, 3, 4)
    ).reshape(kv_heads, requests * per_source, head_dim)
    fresh = jnp.transpose(jnp.stack([new_k, new_v]), (3, 0, 1, 2, 4)).reshape(
        kv_heads, 2 * requests * local_rows, head_dim
    )
    sent = jnp.concatenate([grouped, fresh], axis=1)
    sent = jnp.broadcast_to(sent[None], (spread,) + sent.shape).reshape((devices_seq,) + sent.shape[1:])
    head_q = lax.all_to_all(sent, "seq", split_axis=0, concat_axis=0, tiled=True)
    head_fresh = head_q[:, requests * per_source :, :].reshape(
        devices_seq, 2, requests, local_rows, head_dim
    )
    head_fresh = jnp.transpose(head_fresh, (1, 2, 0, 3, 4)).reshape(
        2, requests, devices_seq * local_rows, head_dim
    )

    def to_heads(cache):
        return lax.all_to_all(
            jnp.transpose(cache, (1, 0, 2)), "seq", split_axis=0, concat_axis=0, axis_index_groups=blocks, tiled=True
        )

    outs = []
    for r in range(requests):
        keys = to_heads(cache_k[r])
        values = to_heads(cache_v[r])
        held = kv_heads * slots
        valid = jnp.clip(cache_len[r] - block * held, 0, held)
        fresh_shift = jnp.where(block == spread - 1, 0, -devices_seq * local_rows)
        info = jnp.stack([valid, fresh_shift]).astype(jnp.int32)
        part = attend(r, info, head_q, keys, values, head_fresh[0, r], head_fresh[1, r], per_source, group_size)
        part = lax.all_to_all(part, "seq", split_axis=0, concat_axis=0, tiled=True)
        outs.append(merge(part.reshape(spread, kv_heads, per_source + STAT_ROWS, head_dim), local_rows, group_size))
    return jnp.stack(outs)


def solution(mesh):
    in_specs = (
        P("groups", "seq", None, None),
        P("groups", "seq", None, None),
        P("groups", "seq", None, None),
        P("groups", "seq", None, None),
        P("groups", "seq", None, None),
        P("groups"),
    )
    out_specs = P("groups", "seq", None, None)
    return jax.shard_map(shards, mesh=mesh, in_specs=in_specs, out_specs=out_specs, check_vma=False)
```

```python
import functools
import math

import jax
import jax.numpy as jnp
from jax import lax
from jax.experimental import pallas as pl
from jax.experimental.pallas import tpu as pltpu
from jax.sharding import PartitionSpec as P

NEG = -1e30
STAT_ROWS = 8
VMEM_BYTES = 58 * 2**20


def attend_kernel(
    info_ref, q_ref, kv_ref, fk_ref, fv_ref, out_ref, vals, fvals, s0, s1, m0, m1, *, chunk, tile, group_size
):
    sources, per_source, dim = q_ref.shape
    slots = kv_ref.shape[0] * kv_ref.shape[2]
    per_chunk = chunk // kv_ref.shape[2]
    fresh = fk_ref.shape[0]
    local_rows = per_source // group_size
    rows = sources * per_source
    tiles = rows // tile
    span = tile // per_source
    scale = math.log2(math.e) / math.sqrt(dim)
    valid = info_ref[0]
    fresh_shift = info_ref[1]
    me = info_ref[2]

    vals[:, :dim] = kv_ref[:, 1].reshape(slots, dim)
    vals[:, dim:] = jnp.ones((slots, dim), jnp.bfloat16)
    fvals[:, :dim] = fv_ref[...]
    fvals[:, dim:] = jnp.ones((fresh, dim), jnp.bfloat16)

    def position(order):
        return ((order // local_rows) ^ me) * local_rows + order % local_rows

    def product(a, b):
        return lax.dot_general(a, b, (((1,), (1,)), ((), ())), preferred_element_type=jnp.float32)

    def lane_max(scores, best):
        for lane in range(scores.shape[1] // dim):
            part = scores[:, lane * dim : (lane + 1) * dim]
            best = part if best is None else jnp.maximum(best, part)
        return best

    def score_chunk(t, j, count, s_ref, best):
        q = q_ref[pl.ds(t * span, span)].reshape(tile, dim)
        if j < count:
            keys = kv_ref[j * per_chunk : (j + 1) * per_chunk, 0].reshape(chunk, dim)
            scores = product(q, keys)
            if j == count - 1:
                pos = j * chunk + lax.broadcasted_iota(jnp.int32, (1, chunk), 1)
                scores = scores + jnp.where(pos < valid, 0.0, NEG)
            s_ref[:, j * chunk : (j + 1) * chunk] = scores
            return lane_max(scores, best)
        scores = product(q, fk_ref[...])
        token = position((t * tile + lax.broadcasted_iota(jnp.int32, (tile, 1), 0)) // group_size)
        unit = position(lax.broadcasted_iota(jnp.int32, (1, fresh), 1))
        scores = jnp.where(unit <= token + fresh_shift, scores, NEG)
        s_ref[:, slots : slots + fresh] = scores
        return lane_max(scores, best)

    def value_chunk(j, count, s_ref, top, acc):
        if j < count:
            scores = s_ref[:, j * chunk : (j + 1) * chunk]
            values = vals[j * chunk : (j + 1) * chunk, :]
        else:
            scores = s_ref[:, slots : slots + fresh]
            values = fvals[...]
        weights = jnp.exp2((scores - top) * scale).astype(jnp.bfloat16)
        part = jnp.dot(weights, values, preferred_element_type=jnp.float32)
        return part if acc is None else acc + part

    def stage(t_next, s_next, m_next, t_now, s_now, m_now, count):
        best = None
        acc = None
        if t_now is not None:
            top = jnp.max(m_now[...], axis=1, keepdims=True)
        for j in range(count + 1):
            if t_next is not None:
                best = score_chunk(t_next, j, count, s_next, best)
            if t_now is not None:
                acc = value_chunk(j, count, s_now, top, acc)
        if t_next is not None:
            m_next[...] = best
        if t_now is not None:
            total = acc[:, dim:]
            out = (acc[:, :dim] / total).astype(jnp.bfloat16)
            for part in range(span):
                out_ref[(t_now * span + part) ^ me, :per_source, :] = out[
                    part * per_source : (part + 1) * per_source
                ]
            level = top * scale + jnp.log2(total)
            for first in range(0, tile, dim):
                flat = jnp.transpose(level[first : first + dim, :])[:STAT_ROWS]
                high = flat.astype(jnp.bfloat16)
                rest = flat - high.astype(jnp.float32)
                mid = rest.astype(jnp.bfloat16)
                low = (rest - mid.astype(jnp.float32)).astype(jnp.bfloat16)
                which = lax.broadcasted_iota(jnp.int32, flat.shape, 0)
                stats = jnp.where(
                    which == 0,
                    high.astype(jnp.float32),
                    jnp.where(which == 1, mid.astype(jnp.float32), low.astype(jnp.float32)),
                ).astype(jnp.bfloat16)
                width = min(per_source, dim)
                for part in range(dim // width):
                    row = first + part * width
                    out_ref[(t_now * span + row // per_source) ^ me, per_source:, :width] = stats[
                        :, part * width : (part + 1) * width
                    ]

    for count in range(slots // chunk + 1):

        @pl.when((valid > (count - 1) * chunk) & (valid <= count * chunk))
        def _(count=count):
            stage(0, s0, m0, None, None, None, count)

            def pair(i, carry):
                stage(2 * i + 1, s1, m1, 2 * i, s0, m0, count)
                stage(jnp.minimum(2 * i + 2, tiles - 1), s0, m0, 2 * i + 1, s1, m1, count)
                return carry

            lax.fori_loop(0, tiles // 2, pair, 0)


def attend(request, info, head_q, keys_values, fresh_k, fresh_v, per_source, group_size):
    sources, _, dim = head_q.shape
    slots = keys_values.shape[0] * keys_values.shape[2]
    rows = sources * per_source
    fresh = fresh_k.shape[0]
    tile = min(256, rows // 2)
    chunk = min(1024, slots)

    def whole(array):
        return pl.BlockSpec(array.shape, lambda i, s: (0,) * array.ndim)

    return pl.pallas_call(
        functools.partial(attend_kernel, chunk=chunk, tile=tile, group_size=group_size),
        grid_spec=pltpu.PrefetchScalarGridSpec(
            num_scalar_prefetch=1,
            grid=(1,),
            in_specs=[
                pl.BlockSpec((sources, per_source, dim), lambda i, s: (0, request, 0)),
                whole(keys_values),
                whole(fresh_k),
                whole(fresh_v),
            ],
            out_specs=pl.BlockSpec((sources, per_source + STAT_ROWS, dim), lambda i, s: (0, 0, 0)),
            scratch_shapes=[
                pltpu.VMEM((slots, 2 * dim), jnp.bfloat16),
                pltpu.VMEM((fresh, 2 * dim), jnp.bfloat16),
                pltpu.VMEM((tile, slots + fresh), jnp.float32),
                pltpu.VMEM((tile, slots + fresh), jnp.float32),
                pltpu.VMEM((tile, dim), jnp.float32),
                pltpu.VMEM((tile, dim), jnp.float32),
            ],
        ),
        out_shape=jax.ShapeDtypeStruct((sources, per_source + STAT_ROWS, dim), jnp.bfloat16),
        compiler_params=pltpu.CompilerParams(vmem_limit_bytes=VMEM_BYTES),
        cost_estimate=pl.CostEstimate(
            flops=4 * rows * slots * dim,
            bytes_accessed=4 * slots * dim + 4 * rows * dim,
            transcendentals=rows * slots,
        ),
    )(info, head_q, keys_values, fresh_k, fresh_v)


def merge_kernel(part_ref, *refs, group_size):
    out_ref = refs[-1]
    spread, heads, _, dim = part_ref.shape
    local_rows = out_ref.shape[1]
    per_source = local_rows * group_size
    for h in range(heads):
        levels = []
        for b in range(spread):
            stats = part_ref[b, h, per_source : per_source + STAT_ROWS, :].astype(jnp.float32)
            level = stats[0:1] + stats[1:2] + stats[2:3]
            levels.append(jnp.transpose(jnp.broadcast_to(level, (dim, dim)))[:per_source])
        top = functools.reduce(jnp.maximum, levels)
        weights = [jnp.exp2(level - top) for level in levels]
        total = functools.reduce(jnp.add, weights)
        mixed = functools.reduce(
            jnp.add,
            [w * part_ref[b, h, :per_source, :].astype(jnp.float32) for b, w in enumerate(weights)],
        )
        out = (mixed / total).astype(jnp.bfloat16)
        out_ref[0, :, h * group_size : (h + 1) * group_size, :] = out.reshape(local_rows, group_size, dim)


def merge(parts, request, requests, local_rows, group_size, earlier):
    heads, dim = parts.shape[1], parts.shape[3]
    rest = [] if earlier is None else [earlier]
    return pl.pallas_call(
        functools.partial(merge_kernel, group_size=group_size),
        grid=(1,),
        in_specs=[pl.BlockSpec(parts.shape, lambda i: (0, 0, 0, 0))]
        + [pl.BlockSpec(memory_space=pl.ANY) for _ in rest],
        out_specs=pl.BlockSpec((1, local_rows, heads * group_size, dim), lambda i: (request, 0, 0, 0)),
        out_shape=jax.ShapeDtypeStruct((requests, local_rows, heads * group_size, dim), jnp.bfloat16),
        input_output_aliases={1: 0} if rest else {},
        compiler_params=pltpu.CompilerParams(vmem_limit_bytes=VMEM_BYTES),
    )(parts, *rest)


def pack_kernel(me_ref, q_ref, fresh_ref, out_ref):
    requests, local_rows, group_size, dim = q_ref.shape
    rows = requests * local_rows * group_size
    out_ref[0, :rows, :] = q_ref[...].reshape(rows, dim)
    out_ref[0, rows:, :] = fresh_ref[0]


def pack(queries, fresh, me, kv_heads):
    requests, local_rows, heads, dim = queries.shape
    group_size = heads // kv_heads
    rows = requests * local_rows * group_size + fresh.shape[1]
    return pl.pallas_call(
        pack_kernel,
        grid_spec=pltpu.PrefetchScalarGridSpec(
            num_scalar_prefetch=1,
            grid=(kv_heads,),
            in_specs=[
                pl.BlockSpec((requests, local_rows, group_size, dim), lambda d, me: (0, 0, d ^ me[0], 0)),
                pl.BlockSpec((1,) + fresh.shape[1:], lambda d, me: (d ^ me[0], 0, 0)),
            ],
            out_specs=pl.BlockSpec((1, rows, dim), lambda d, me: (d, 0, 0)),
        ),
        out_shape=jax.ShapeDtypeStruct((kv_heads, rows, dim), jnp.bfloat16),
    )(me, queries, fresh)


def shards(queries, new_k, new_v, cache_k, cache_v, cache_len):
    requests, local_rows, heads, head_dim = queries.shape
    slots = cache_k.shape[1]
    kv_heads = cache_k.shape[2]
    group_size = heads // kv_heads
    devices_seq = lax.axis_size("seq")
    seq_index = lax.axis_index("seq")
    spread = devices_seq // kv_heads
    block = seq_index // kv_heads
    per_source = local_rows * group_size
    blocks = [[b * kv_heads + h for h in range(kv_heads)] for b in range(spread)]

    def partner(bit):
        return [(i, i ^ bit) for i in range(devices_seq)]

    fresh = jnp.transpose(jnp.stack([new_k, new_v]), (3, 0, 1, 2, 4)).reshape(
        kv_heads, 2 * requests * local_rows, head_dim
    )
    own_head = (seq_index % kv_heads).astype(jnp.int32)[None]
    head_q = pack(queries, fresh, own_head, kv_heads)[None]
    bit = 1
    while bit < kv_heads:
        halves = head_q.reshape((head_q.shape[0], -1, 2) + head_q.shape[2:])
        received = lax.ppermute(halves[:, :, 1], "seq", partner(bit))
        head_q = jnp.concatenate([halves[:, :, 0], received], axis=0)
        bit *= 2
    head_q = head_q[:, 0]
    in_block = head_q
    while bit < devices_seq:
        head_q = jnp.concatenate([head_q, lax.ppermute(head_q, "seq", partner(bit))], axis=0)
        bit *= 2
    head_fresh = head_q[:, requests * per_source :, :].reshape(
        devices_seq, 2, requests, local_rows, head_dim
    )
    head_fresh = jnp.transpose(head_fresh, (1, 2, 0, 3, 4)).reshape(
        2, requests, devices_seq * local_rows, head_dim
    )

    out = None
    for r in range(requests):
        keys_values = jnp.transpose(jnp.stack([cache_k[r], cache_v[r]]), (2, 0, 1, 3))
        if r > 0:
            keys_values, _ = lax.optimization_barrier((keys_values, in_block))
        keys_values = lax.all_to_all(
            keys_values, "seq", split_axis=0, concat_axis=0, axis_index_groups=blocks, tiled=True
        )
        held = kv_heads * slots
        valid = jnp.clip(cache_len[r] - block * held, 0, held)
        fresh_shift = jnp.where(block == spread - 1, 0, -devices_seq * local_rows)
        info = jnp.stack([valid, fresh_shift, seq_index]).astype(jnp.int32)
        part = attend(r, info, head_q, keys_values, head_fresh[0, r], head_fresh[1, r], per_source, group_size)
        part = lax.all_to_all(part, "seq", split_axis=0, concat_axis=0, tiled=True)
        part = part.reshape(spread, kv_heads, per_source + STAT_ROWS, head_dim)
        out = merge(part, r, requests, local_rows, group_size, out)
    return out


def solution(mesh):
    in_specs = (
        P("groups", "seq", None, None),
        P("groups", "seq", None, None),
        P("groups", "seq", None, None),
        P("groups", "seq", None, None),
        P("groups", "seq", None, None),
        P("groups"),
    )
    out_specs = P("groups", "seq", None, None)
    return jax.shard_map(shards, mesh=mesh, in_specs=in_specs, out_specs=out_specs, check_vma=False)
```

```python
import functools
import math

import jax
import jax.numpy as jnp
from jax import lax
from jax.experimental import pallas as pl
from jax.experimental.pallas import tpu as pltpu
from jax.sharding import PartitionSpec as P


NEG = -1e30
STAT_ROWS = 8
SMALL_VMEM = 8 * 2**20


def attend_kernel(
    info_ref, q_ref, kv_ref, fk_ref, fv_ref, out_ref, vals, fvals, s0, s1, m0, m1, *, chunk, tile, group_size
):
    sources, per_source, dim = q_ref.shape
    slots = kv_ref.shape[0] * kv_ref.shape[2]
    per_chunk = chunk // kv_ref.shape[2]
    fresh = fk_ref.shape[0]
    local_rows = per_source // group_size
    rows = sources * per_source
    tiles = rows // tile
    span = tile // per_source
    scale = math.log2(math.e) / math.sqrt(dim)
    valid = info_ref[0]
    fresh_shift = info_ref[1]
    me = info_ref[2]

    vals[:, :dim] = kv_ref[:, 1].reshape(slots, dim)
    vals[:, dim:] = jnp.ones((slots, dim), jnp.bfloat16)
    fvals[:, :dim] = fv_ref[...]
    fvals[:, dim:] = jnp.ones((fresh, dim), jnp.bfloat16)

    def position(order):
        return ((order // local_rows) ^ me) * local_rows + order % local_rows

    def product(a, b):
        return lax.dot_general(a, b, (((1,), (1,)), ((), ())), preferred_element_type=jnp.float32)

    def lane_max(scores, best):
        for lane in range(scores.shape[1] // dim):
            part = scores[:, lane * dim : (lane + 1) * dim]
            best = part if best is None else jnp.maximum(best, part)
        return best

    def score_chunk(t, j, count, s_ref, best):
        q = q_ref[pl.ds(t * span, span)].reshape(tile, dim)
        if j < count:
            keys = kv_ref[j * per_chunk : (j + 1) * per_chunk, 0].reshape(chunk, dim)
            scores = product(q, keys)
            if j == count - 1:
                pos = j * chunk + lax.broadcasted_iota(jnp.int32, (1, chunk), 1)
                scores = scores + jnp.where(pos < valid, 0.0, NEG)
            s_ref[:, j * chunk : (j + 1) * chunk] = scores
            return lane_max(scores, best)
        scores = product(q, fk_ref[...])
        token = position((t * tile + lax.broadcasted_iota(jnp.int32, (tile, 1), 0)) // group_size)
        unit = position(lax.broadcasted_iota(jnp.int32, (1, fresh), 1))
        scores = jnp.where(unit <= token + fresh_shift, scores, NEG)
        s_ref[:, slots : slots + fresh] = scores
        return lane_max(scores, best)

    def value_chunk(j, count, s_ref, top, acc):
        if j < count:
            scores = s_ref[:, j * chunk : (j + 1) * chunk]
            values = vals[j * chunk : (j + 1) * chunk, :]
        else:
            scores = s_ref[:, slots : slots + fresh]
            values = fvals[...]
        weights = jnp.exp2((scores - top) * scale).astype(jnp.bfloat16)
        part = jnp.dot(weights, values, preferred_element_type=jnp.float32)
        return part if acc is None else acc + part

    def stage(t_next, s_next, m_next, t_now, s_now, m_now, count):
        best = None
        acc = None
        if t_now is not None:
            top = jnp.max(m_now[...], axis=1, keepdims=True)
        for j in range(count + 1):
            if t_next is not None:
                best = score_chunk(t_next, j, count, s_next, best)
            if t_now is not None:
                acc = value_chunk(j, count, s_now, top, acc)
        if t_next is not None:
            m_next[...] = best
        if t_now is not None:
            total = acc[:, dim:]
            out = (acc[:, :dim] / total).astype(jnp.bfloat16)
            for part in range(span):
                out_ref[(t_now * span + part) ^ me, :per_source, :] = out[
                    part * per_source : (part + 1) * per_source
                ]
            level = top * scale + jnp.log2(total)
            for first in range(0, tile, dim):
                flat = jnp.transpose(level[first : first + dim, :STAT_ROWS])
                high = flat.astype(jnp.bfloat16)
                rest = flat - high.astype(jnp.float32)
                mid = rest.astype(jnp.bfloat16)
                low = (rest - mid.astype(jnp.float32)).astype(jnp.bfloat16)
                which = lax.broadcasted_iota(jnp.int32, flat.shape, 0)
                stats = jnp.where(
                    which == 0,
                    high.astype(jnp.float32),
                    jnp.where(which == 1, mid.astype(jnp.float32), low.astype(jnp.float32)),
                ).astype(jnp.bfloat16)
                width = min(per_source, dim)
                for part in range(dim // width):
                    row = first + part * width
                    out_ref[(t_now * span + row // per_source) ^ me, per_source:, :width] = stats[
                        :, part * width : (part + 1) * width
                    ]

    for count in range(slots // chunk + 1):

        @pl.when((valid > (count - 1) * chunk) & (valid <= count * chunk))
        def _(count=count):
            stage(0, s0, m0, None, None, None, count)

            def pair(i, carry):
                stage(2 * i + 1, s1, m1, 2 * i, s0, m0, count)
                stage(jnp.minimum(2 * i + 2, tiles - 1), s0, m0, 2 * i + 1, s1, m1, count)
                return carry

            lax.fori_loop(0, tiles // 2, pair, 0)


def attend(request, info, head_q, keys_values, fresh_k, fresh_v, per_source, group_size):
    sources, _, dim = head_q.shape
    slots = keys_values.shape[0] * keys_values.shape[2]
    rows = sources * per_source
    fresh = fresh_k.shape[0]
    tile = min(256, rows // 2)
    chunk = min(1024, slots)

    grant = 4 * (2 * tile * (slots + fresh) + slots * dim + 2 * slots * dim + 2 * rows * dim) + SMALL_VMEM

    def whole():
        return pl.BlockSpec(memory_space=pltpu.VMEM)

    return pl.pallas_call(
        functools.partial(attend_kernel, chunk=chunk, tile=tile, group_size=group_size),
        grid_spec=pltpu.PrefetchScalarGridSpec(
            num_scalar_prefetch=1,
            grid=(1,),
            in_specs=[
                pl.BlockSpec((sources, per_source, dim), lambda i, s: (0, request, 0)), whole(), whole(), whole()
            ],
            out_specs=pl.BlockSpec((sources, per_source + STAT_ROWS, dim), lambda i, s: (0, 0, 0)),
            scratch_shapes=[
                pltpu.VMEM((slots, 2 * dim), jnp.bfloat16),
                pltpu.VMEM((fresh, 2 * dim), jnp.bfloat16),
                pltpu.VMEM((tile, slots + fresh), jnp.float32),
                pltpu.VMEM((tile, slots + fresh), jnp.float32),
                pltpu.VMEM((tile, dim), jnp.float32),
                pltpu.VMEM((tile, dim), jnp.float32),
            ],
        ),
        out_shape=jax.ShapeDtypeStruct((sources, per_source + STAT_ROWS, dim), jnp.bfloat16),
        compiler_params=pltpu.CompilerParams(vmem_limit_bytes=grant),
        cost_estimate=pl.CostEstimate(
            flops=4 * rows * slots * dim,
            bytes_accessed=4 * slots * dim + 4 * rows * dim,
            transcendentals=rows * slots,
        ),
    )(info, head_q, keys_values, fresh_k, fresh_v)


def merge_kernel(part_ref, *refs, group_size):
    out_ref = refs[-1]
    spread, heads, _, dim = part_ref.shape
    local_rows = out_ref.shape[1]
    per_source = local_rows * group_size
    levels = []
    for b in range(spread):
        stats = [
            part_ref[b, h, per_source : per_source + STAT_ROWS, :].astype(jnp.float32) for h in range(heads)
        ]
        levels.append(jnp.concatenate([x[0:1] + x[1:2] + x[2:3] for x in stats], axis=0))
    top = functools.reduce(jnp.maximum, levels)
    weights = [jnp.exp2(level - top) for level in levels]
    total = functools.reduce(jnp.add, weights)
    weights = [jnp.transpose(w / total) for w in weights]
    for h in range(heads):
        mixed = functools.reduce(
            jnp.add,
            [
                w[:per_source, h : h + 1] * part_ref[b, h, :per_source, :].astype(jnp.float32)
                for b, w in enumerate(weights)
            ],
        ).astype(jnp.bfloat16)
        out_ref[0, :, h * group_size : (h + 1) * group_size, :] = mixed.reshape(local_rows, group_size, dim)


def merge(parts, request, requests, local_rows, group_size, earlier):
    heads, dim = parts.shape[1], parts.shape[3]
    rest = [] if earlier is None else [earlier]
    return pl.pallas_call(
        functools.partial(merge_kernel, group_size=group_size),
        grid=(1,),
        in_specs=[pl.BlockSpec(parts.shape, lambda i: (0, 0, 0, 0))]
        + [pl.BlockSpec(memory_space=pl.ANY) for _ in rest],
        out_specs=pl.BlockSpec((1, local_rows, heads * group_size, dim), lambda i: (request, 0, 0, 0)),
        out_shape=jax.ShapeDtypeStruct((requests, local_rows, heads * group_size, dim), jnp.bfloat16),
        input_output_aliases={1: 0} if rest else {},
        compiler_params=pltpu.CompilerParams(vmem_limit_bytes=SMALL_VMEM),
    )(parts, *rest)


def pack_kernel(me_ref, q_ref, fresh_ref, out_ref):
    requests, local_rows, heads, dim = q_ref.shape
    kv_heads = out_ref.shape[0]
    group_size = heads // kv_heads
    rows = requests * local_rows * group_size
    for d in range(kv_heads):
        head = d ^ me_ref[0]
        first = pl.multiple_of(head * group_size, group_size)
        out_ref[d, :rows, :] = q_ref[:, :, pl.ds(first, group_size), :].reshape(rows, dim)
        out_ref[d, rows:, :] = fresh_ref[head]


def pack(queries, fresh, me, kv_heads):
    requests, local_rows, heads, dim = queries.shape
    rows = requests * local_rows * (heads // kv_heads) + fresh.shape[1]
    return pl.pallas_call(
        pack_kernel,
        in_specs=[
            pl.BlockSpec(memory_space=pltpu.SMEM),
            pl.BlockSpec(memory_space=pltpu.VMEM),
            pl.BlockSpec(memory_space=pltpu.VMEM),
        ],
        out_specs=pl.BlockSpec(memory_space=pltpu.VMEM),
        out_shape=jax.ShapeDtypeStruct((kv_heads, rows, dim), jnp.bfloat16),
        compiler_params=pltpu.CompilerParams(vmem_limit_bytes=SMALL_VMEM),
    )(me, queries, fresh)


def attention(queries, new_k, new_v, cache_k, cache_v, cache_len):
    requests, local_rows, heads, head_dim = queries.shape
    slots = cache_k.shape[1]
    kv_heads = cache_k.shape[2]
    group_size = heads // kv_heads
    devices_seq = lax.axis_size("seq")
    seq_index = lax.axis_index("seq")
    spread = devices_seq // kv_heads
    block = seq_index // kv_heads
    per_source = local_rows * group_size
    blocks = [[b * kv_heads + h for h in range(kv_heads)] for b in range(spread)]

    def partner(bit):
        return [(i, i ^ bit) for i in range(devices_seq)]

    fresh = jnp.transpose(jnp.stack([new_k, new_v]), (3, 0, 1, 2, 4)).reshape(
        kv_heads, 2 * requests * local_rows, head_dim
    )
    own_head = (seq_index % kv_heads).astype(jnp.int32)[None]
    head_q = pack(queries, fresh, own_head, kv_heads)[None]
    bit = 1
    while bit < kv_heads:
        halves = head_q.reshape((head_q.shape[0], -1, 2) + head_q.shape[2:])
        if 2 * bit == kv_heads:
            before_last = halves
        received = lax.ppermute(halves[:, :, 1], "seq", partner(bit))
        head_q = jnp.concatenate([halves[:, :, 0], received], axis=0)
        bit *= 2
    head_q = head_q[:, 0]
    in_block = head_q
    while bit < devices_seq:
        received = lax.ppermute(head_q, "seq", partner(bit))
        head_q = jnp.concatenate([head_q, received], axis=0)
        bit *= 2
    head_fresh = head_q[:, requests * per_source :, :].reshape(
        devices_seq, 2, requests, local_rows, head_dim
    )
    head_fresh = jnp.transpose(head_fresh, (1, 2, 0, 3, 4)).reshape(
        2, requests, devices_seq * local_rows, head_dim
    )

    out = None
    for r in range(requests):
        keys_values = jnp.transpose(jnp.stack([cache_k[r], cache_v[r]]), (2, 0, 1, 3))
        keys_values, _ = lax.optimization_barrier((keys_values, before_last if r == 0 else in_block))
        keys_values = lax.all_to_all(
            keys_values, "seq", split_axis=0, concat_axis=0, axis_index_groups=blocks, tiled=True
        )
        held = kv_heads * slots
        valid = jnp.clip(cache_len[r] - block * held, 0, held)
        fresh_shift = jnp.where(block == spread - 1, 0, -devices_seq * local_rows)
        info = jnp.stack([valid, fresh_shift, seq_index]).astype(jnp.int32)
        part = attend(r, info, head_q, keys_values, head_fresh[0, r], head_fresh[1, r], per_source, group_size)
        part = lax.all_to_all(part, "seq", split_axis=0, concat_axis=0, tiled=True)
        part = part.reshape(spread, kv_heads, per_source + STAT_ROWS, head_dim)
        out = merge(part, r, requests, local_rows, group_size, out)
    return out


def solution(mesh):
    in_specs = (
        P("groups", "seq", None, None),
        P("groups", "seq", None, None),
        P("groups", "seq", None, None),
        P("groups", "seq", None, None),
        P("groups", "seq", None, None),
        P("groups"),
    )
    out_specs = P("groups", "seq", None, None)
    return jax.shard_map(attention, mesh=mesh, in_specs=in_specs, out_specs=out_specs, check_vma=False)
```

```python
import functools
import math

import jax
import jax.numpy as jnp
from jax import lax
from jax.experimental import pallas as pl
from jax.experimental.pallas import tpu as pltpu
from jax.sharding import PartitionSpec as P


NEG = -1e30
STAT_ROWS = 8
SMALL_VMEM = 12 * 2**20


VMEM_SPEC = pl.BlockSpec(memory_space=pltpu.VMEM)
HBM_SPEC = pl.BlockSpec(memory_space=pltpu.HBM)
SMEM_SPEC = pl.BlockSpec(memory_space=pltpu.SMEM)


def attend_kernel(*refs, blocks, chunk, tile, group_size, row_start, row_count):
    info_ref, q_hbm = refs[:2]
    kv_refs = refs[2 : 2 + blocks]
    fk_ref, fv_ref, out_hbm, q_ref, out_ref, keys, vals, fvals, s0, s1, m0, m1, in_sems, q_sem, out_sem = refs[
        2 + blocks :
    ]
    per_source, dim = row_count, q_ref.shape[2]
    block_slots = kv_refs[0].shape[1]
    slots = blocks * block_slots
    fresh = fk_ref.shape[0]
    rows = q_ref.shape[0] * per_source
    tiles = rows // tile
    span = tile // per_source
    scale = math.log2(math.e) / math.sqrt(dim)
    valid = info_ref[0]
    fresh_shift = info_ref[1]
    own = info_ref[2]

    copies = [
        pltpu.make_async_copy(q_hbm.at[:, row_start : row_start + row_count, :], q_ref, q_sem),
    ]
    for k, kv_ref in enumerate(kv_refs):
        at = pl.ds(pl.multiple_of((own ^ k) * block_slots, block_slots), block_slots)
        copies.append(pltpu.make_async_copy(kv_ref.at[0], keys.at[at, :], in_sems.at[k, 0]))
        copies.append(pltpu.make_async_copy(kv_ref.at[1], vals.at[at, :dim], in_sems.at[k, 1]))
    for copy in copies:
        copy.start()
    vals[:, dim:] = jnp.ones((slots, dim), jnp.bfloat16)
    fvals[:, :dim] = fv_ref[...]
    fvals[:, dim:] = jnp.ones((fresh, dim), jnp.bfloat16)
    for copy in copies:
        copy.wait()

    def product(a, b):
        return lax.dot_general(a, b, (((1,), (1,)), ((), ())), preferred_element_type=jnp.float32)

    def lane_max(scores, best):
        for lane in range(scores.shape[1] // dim):
            part = scores[:, lane * dim : (lane + 1) * dim]
            best = part if best is None else jnp.maximum(best, part)
        return best

    def score_chunk(t, j, count, s_ref, best):
        q = q_ref[pl.ds(t * span, span)].reshape(tile, dim)
        if j < count:
            scores = product(q, keys[j * chunk : (j + 1) * chunk, :])
            if j == count - 1:
                pos = j * chunk + lax.broadcasted_iota(jnp.int32, (1, chunk), 1)
                scores = scores + jnp.where(pos < valid, 0.0, NEG)
            s_ref[:, j * chunk : (j + 1) * chunk] = scores
            return lane_max(scores, best)
        scores = product(q, fk_ref[...])
        token = (t * tile + lax.broadcasted_iota(jnp.int32, (tile, 1), 0)) // group_size
        unit = lax.broadcasted_iota(jnp.int32, (1, fresh), 1)
        scores = jnp.where(unit <= token + fresh_shift, scores, NEG)
        s_ref[:, slots : slots + fresh] = scores
        return lane_max(scores, best)

    def value_chunk(j, count, s_ref, top, acc):
        if j < count:
            scores = s_ref[:, j * chunk : (j + 1) * chunk]
            values = vals[j * chunk : (j + 1) * chunk, :]
        else:
            scores = s_ref[:, slots : slots + fresh]
            values = fvals[...]
        weights = jnp.exp2((scores - top) * scale).astype(jnp.bfloat16)
        part = jnp.dot(weights, values, preferred_element_type=jnp.float32)
        return part if acc is None else acc + part

    def stage(t_next, s_next, m_next, t_now, s_now, m_now, count):
        best = None
        acc = None
        if t_now is not None:
            top = jnp.max(m_now[...], axis=1, keepdims=True)
        for j in range(count + 1):
            if t_next is not None:
                best = score_chunk(t_next, j, count, s_next, best)
            if t_now is not None:
                acc = value_chunk(j, count, s_now, top, acc)
        if t_next is not None:
            m_next[...] = best
        if t_now is not None:
            total = acc[:, dim:]
            out = (acc[:, :dim] / total).astype(jnp.bfloat16)
            out_ref[pl.ds(t_now * span, span), :per_source, :] = out.reshape(span, per_source, dim)
            level = top * scale + jnp.log2(total)
            for first in range(0, tile, dim):
                flat = jnp.transpose(level[first : first + dim, :STAT_ROWS])
                high = flat.astype(jnp.bfloat16).astype(jnp.float32)
                mid = (flat - high).astype(jnp.bfloat16).astype(jnp.float32)
                low = flat - high - mid
                which = lax.broadcasted_iota(jnp.int32, flat.shape, 0)
                stats = jnp.where(which == 0, high, jnp.where(which == 1, mid, low)).astype(jnp.bfloat16)
                width = min(per_source, dim)
                for part in range(dim // width):
                    row = first + part * width
                    out_ref[t_now * span + row // per_source, per_source:, :width] = stats[
                        :, part * width : (part + 1) * width
                    ]

    for count in range(slots // chunk + 1):

        @pl.when((valid > (count - 1) * chunk) & (valid <= count * chunk))
        def _(count=count):
            stage(0, s0, m0, None, None, None, count)

            def pair(i, carry):
                stage(2 * i + 1, s1, m1, 2 * i, s0, m0, count)
                stage(jnp.minimum(2 * i + 2, tiles - 1), s0, m0, 2 * i + 1, s1, m1, count)
                return carry

            lax.fori_loop(0, tiles // 2, pair, 0)

    result = pltpu.make_async_copy(out_ref, out_hbm, out_sem)
    result.start()
    result.wait()


def attend(info, head_q, kv_blocks, fresh_k, fresh_v, row_start, row_count, group_size):
    sources, _, dim = head_q.shape
    slots = len(kv_blocks) * kv_blocks[0].shape[1]
    rows = sources * row_count
    fresh = fresh_k.shape[0]
    tile = min(256, rows // 2)
    chunk = min(1024, slots)
    grant = 4 * (2 * tile * (slots + fresh) + 4 * slots * dim + 2 * rows * dim) + SMALL_VMEM
    return pl.pallas_call(
        functools.partial(
            attend_kernel,
            blocks=len(kv_blocks),
            chunk=chunk,
            tile=tile,
            group_size=group_size,
            row_start=row_start,
            row_count=row_count,
        ),
        in_specs=[SMEM_SPEC] + [HBM_SPEC] * (1 + len(kv_blocks)) + [VMEM_SPEC] * 2,
        out_specs=HBM_SPEC,
        scratch_shapes=[
            pltpu.VMEM((sources, row_count, dim), jnp.bfloat16),
            pltpu.VMEM((sources, row_count + STAT_ROWS, dim), jnp.bfloat16),
            pltpu.VMEM((slots, dim), jnp.bfloat16),
            pltpu.VMEM((slots, 2 * dim), jnp.bfloat16),
            pltpu.VMEM((fresh, 2 * dim), jnp.bfloat16),
            pltpu.VMEM((tile, slots + fresh), jnp.float32),
            pltpu.VMEM((tile, slots + fresh), jnp.float32),
            pltpu.VMEM((tile, dim), jnp.float32),
            pltpu.VMEM((tile, dim), jnp.float32),
            pltpu.SemaphoreType.DMA((len(kv_blocks), 2)),
            pltpu.SemaphoreType.DMA,
            pltpu.SemaphoreType.DMA,
        ],
        out_shape=jax.ShapeDtypeStruct((sources, row_count + STAT_ROWS, dim), jnp.bfloat16),
        compiler_params=pltpu.CompilerParams(vmem_limit_bytes=grant),
        cost_estimate=pl.CostEstimate(
            flops=4 * rows * slots * dim,
            bytes_accessed=4 * slots * dim + 4 * rows * dim,
            transcendentals=rows * slots,
        ),
    )(info, head_q, *kv_blocks, fresh_k, fresh_v)


def merge_kernel(part_ref, *refs, group_size):
    out_ref = refs[-1]
    spread, heads, _, dim = part_ref.shape
    local_rows = out_ref.shape[1]
    per_source = local_rows * group_size
    levels = []
    for b in range(spread):
        stats = [
            part_ref[b, h, per_source : per_source + STAT_ROWS, :].astype(jnp.float32) for h in range(heads)
        ]
        levels.append(jnp.concatenate([x[0:1] + x[1:2] + x[2:3] for x in stats], axis=0))
    top = functools.reduce(jnp.maximum, levels)
    weights = [jnp.exp2(level - top) for level in levels]
    total = functools.reduce(jnp.add, weights)
    weights = [jnp.transpose(w / total) for w in weights]
    for h in range(heads):
        mixed = functools.reduce(
            jnp.add,
            [
                w[:per_source, h : h + 1] * part_ref[b, h, :per_source, :].astype(jnp.float32)
                for b, w in enumerate(weights)
            ],
        ).astype(jnp.bfloat16)
        out_ref[0, :, h * group_size : (h + 1) * group_size, :] = mixed.reshape(local_rows, group_size, dim)


def merge(parts, request, requests, local_rows, group_size, earlier):
    heads, dim = parts.shape[1], parts.shape[3]
    rest = [] if earlier is None else [earlier]
    return pl.pallas_call(
        functools.partial(merge_kernel, group_size=group_size),
        grid=(1,),
        in_specs=[pl.BlockSpec(parts.shape, lambda i: (0, 0, 0, 0))]
        + [pl.BlockSpec(memory_space=pl.ANY) for _ in rest],
        out_specs=pl.BlockSpec((1, local_rows, heads * group_size, dim), lambda i: (request, 0, 0, 0)),
        out_shape=jax.ShapeDtypeStruct((requests, local_rows, heads * group_size, dim), jnp.bfloat16),
        input_output_aliases={1: 0} if rest else {},
        compiler_params=pltpu.CompilerParams(vmem_limit_bytes=SMALL_VMEM),
    )(parts, *rest)


def pack_kernel(q_ref, fresh_ref, out_ref):
    requests, local_rows, heads, dim = q_ref.shape
    kv_heads = fresh_ref.shape[0]
    group_size = heads // kv_heads
    rows = requests * local_rows * group_size
    for d in range(out_ref.shape[0]):
        head = d % kv_heads
        out_ref[d, :rows, :] = q_ref[:, :, head * group_size : (head + 1) * group_size, :].reshape(rows, dim)
        out_ref[d, rows:, :] = fresh_ref[head]


def pack(queries, fresh, devices):
    requests, local_rows, heads, dim = queries.shape
    rows = requests * local_rows * (heads // fresh.shape[0]) + fresh.shape[1]
    return pl.pallas_call(
        pack_kernel,
        in_specs=[VMEM_SPEC, VMEM_SPEC],
        out_specs=VMEM_SPEC,
        out_shape=jax.ShapeDtypeStruct((devices, rows, dim), jnp.bfloat16),
        compiler_params=pltpu.CompilerParams(vmem_limit_bytes=SMALL_VMEM),
    )(queries, fresh)


def split_kernel(own_ref, k_ref, v_ref, *refs):
    held = refs[-1]
    held[:, 0] = jnp.swapaxes(k_ref[0], 0, 1)
    held[:, 1] = jnp.swapaxes(v_ref[0], 0, 1)
    for k, out_ref in enumerate(refs[:-1]):
        out_ref[...] = held[own_ref[0] ^ k]


def split_heads(own, cache_k, cache_v, request):
    _, slots, kv_heads, dim = cache_k.shape
    return pl.pallas_call(
        split_kernel,
        grid=(1,),
        in_specs=[SMEM_SPEC] + [pl.BlockSpec((1, slots, kv_heads, dim), lambda i: (request, 0, 0, 0))] * 2,
        out_specs=[pl.BlockSpec((2, slots, dim), lambda i: (0, 0, 0))] * kv_heads,
        out_shape=[jax.ShapeDtypeStruct((2, slots, dim), jnp.bfloat16)] * kv_heads,
        scratch_shapes=[pltpu.VMEM((kv_heads, 2, slots, dim), jnp.bfloat16)],
        compiler_params=pltpu.CompilerParams(vmem_limit_bytes=2 * SMALL_VMEM),
    )(own, cache_k, cache_v)


def attention(queries, new_k, new_v, cache_k, cache_v, cache_len):
    requests, local_rows, heads, head_dim = queries.shape
    slots = cache_k.shape[1]
    kv_heads = cache_k.shape[2]
    group_size = heads // kv_heads
    devices_seq = lax.axis_size("seq")
    seq_index = lax.axis_index("seq")
    spread = devices_seq // kv_heads
    block = seq_index // kv_heads
    own = (seq_index % kv_heads).astype(jnp.int32)
    per_source = local_rows * group_size

    fresh = jnp.transpose(jnp.stack([new_k, new_v]), (3, 0, 1, 2, 4)).reshape(
        kv_heads, 2 * requests * local_rows, head_dim
    )
    head_q = lax.all_to_all(
        pack(queries, fresh, devices_seq), "seq", split_axis=0, concat_axis=0, tiled=True
    )
    head_fresh = head_q[:, requests * per_source :, :].reshape(
        devices_seq, 2, requests, local_rows, head_dim
    )
    head_fresh = jnp.transpose(head_fresh, (1, 2, 0, 3, 4)).reshape(
        2, requests, devices_seq * local_rows, head_dim
    )

    kv_blocks = []
    for r in range(requests):
        parts = split_heads(own[None], cache_k, cache_v, r)
        moved = [lax.ppermute(parts[k], "seq", [(i, i ^ k) for i in range(devices_seq)]) for k in range(1, kv_heads)]
        kv_blocks.append([parts[0]] + moved)

    out = None
    for r in range(requests):
        held = kv_heads * slots
        valid = jnp.clip(cache_len[r] - block * held, 0, held)
        fresh_shift = jnp.where(block == spread - 1, 0, -devices_seq * local_rows)
        info = jnp.stack([valid, fresh_shift, own]).astype(jnp.int32)
        part = attend(
            info, head_q, kv_blocks[r], head_fresh[0, r], head_fresh[1, r], r * per_source, per_source, group_size
        )
        part = lax.all_to_all(part, "seq", split_axis=0, concat_axis=0, tiled=True)
        part = part.reshape(spread, kv_heads, per_source + STAT_ROWS, head_dim)
        out = merge(part, r, requests, local_rows, group_size, out)
    return out


def solution(mesh):
    in_specs = (
        P("groups", "seq", None, None),
        P("groups", "seq", None, None),
        P("groups", "seq", None, None),
        P("groups", "seq", None, None),
        P("groups", "seq", None, None),
        P("groups"),
    )
    out_specs = P("groups", "seq", None, None)
    return jax.shard_map(attention, mesh=mesh, in_specs=in_specs, out_specs=out_specs, check_vma=False)
```

```python
import functools
import math

import jax
import jax.numpy as jnp
from jax import lax
from jax.experimental import pallas as pl
from jax.experimental.pallas import tpu as pltpu
from jax.sharding import PartitionSpec as P


NEG = -1e30
STAT_ROWS = 8
SMALL_VMEM = 12 * 2**20


VMEM_SPEC = pl.BlockSpec(memory_space=pltpu.VMEM)
HBM_SPEC = pl.BlockSpec(memory_space=pltpu.HBM)
SMEM_SPEC = pl.BlockSpec(memory_space=pltpu.SMEM)


def attend_kernel(*refs, order, total_blocks, tile, group_size, row_start, with_fresh, with_state, final):
    refs = list(refs)
    info_ref, q_hbm = refs.pop(0), refs.pop(0)
    kv_refs = [refs.pop(0) for _ in order]
    if with_fresh:
        fk_ref, fv_ref = refs.pop(0), refs.pop(0)
    if with_state:
        acc_in, top_in = refs.pop(0), refs.pop(0)
    if final:
        out_hbm = refs.pop(0)
    else:
        acc_out, top_out = refs.pop(0), refs.pop(0)
    if final:
        out_ref, out_sem = refs.pop(), refs.pop()
    if with_fresh:
        fvals = refs.pop()
    q_ref, keys, vals, s0, s1, m0, m1, in_sems, q_sem = refs
    per_source, dim = q_ref.shape[1:]
    block_slots = kv_refs[0].shape[1]
    chunk = 2 * block_slots
    chunks = len(order) // 2
    slots = chunks * chunk
    rows = q_ref.shape[0] * per_source
    tiles = rows // tile
    span = tile // per_source
    scale = math.log2(math.e) / math.sqrt(dim)
    valid = info_ref[0]
    fresh_shift = info_ref[1]
    own = info_ref[2]

    held = sorted({k // 2 for k in order})
    absent = [c for c in range(total_blocks // 2) if c not in held]

    def rank_of(index):
        rank = index
        for c in absent:
            rank = rank - jnp.where((own // 2) ^ c < index, 1, 0)
        return rank

    copies = [pltpu.make_async_copy(q_hbm.at[:, row_start : row_start + per_source, :], q_ref, q_sem)]
    for i, k in enumerate(order):
        first = rank_of((own // 2) ^ (k // 2)) * chunk + ((own % 2) ^ (k % 2)) * block_slots
        at = pl.ds(pl.multiple_of(first, block_slots), block_slots)
        copies.append(pltpu.make_async_copy(kv_refs[i].at[0], keys.at[at, :], in_sems.at[i, 0]))
        copies.append(pltpu.make_async_copy(kv_refs[i].at[1], vals.at[at, :dim], in_sems.at[i, 1]))
    for copy in copies:
        copy.start()
    vals[:, dim:] = jnp.ones((slots, dim), jnp.bfloat16)
    if with_fresh:
        fresh = fk_ref.shape[0]
        fvals[:, :dim] = fv_ref[...]
        fvals[:, dim:] = jnp.ones((fresh, dim), jnp.bfloat16)

    filled = jnp.int32(0)
    last_valid = jnp.int32(0)
    for c in held:
        left = valid - ((own // 2) ^ c) * chunk
        filled = filled + jnp.where(left > 0, 1, 0)
        last_valid = jnp.where((left > 0) & (left < chunk), left, last_valid)
    last_valid = jnp.where(last_valid == 0, chunk, last_valid)
    for copy in copies:
        copy.wait()

    def product(a, b):
        return lax.dot_general(a, b, (((1,), (1,)), ((), ())), preferred_element_type=jnp.float32)

    def lane_max(scores, best):
        for lane in range(scores.shape[1] // dim):
            part = scores[:, lane * dim : (lane + 1) * dim]
            best = part if best is None else jnp.maximum(best, part)
        return best

    def score_chunk(t, j, count, s_ref, best):
        q = q_ref[pl.ds(t * span, span)].reshape(tile, dim)
        if j < count:
            scores = product(q, keys[j * chunk : (j + 1) * chunk, :])
            if j == count - 1:
                pos = lax.broadcasted_iota(jnp.int32, (1, chunk), 1)
                scores = scores + jnp.where(pos < last_valid, 0.0, NEG)
            s_ref[:, j * chunk : (j + 1) * chunk] = scores
            return lane_max(scores, best)
        scores = product(q, fk_ref[...])
        token = (t * tile + lax.broadcasted_iota(jnp.int32, (tile, 1), 0)) // group_size
        unit = lax.broadcasted_iota(jnp.int32, (1, fresh), 1)
        scores = jnp.where(unit <= token + fresh_shift, scores, NEG)
        s_ref[:, slots : slots + fresh] = scores
        return lane_max(scores, best)

    def value_chunk(j, count, s_ref, top, acc):
        if j < count:
            scores = s_ref[:, j * chunk : (j + 1) * chunk]
            values = vals[j * chunk : (j + 1) * chunk, :]
        else:
            scores = s_ref[:, slots : slots + fresh]
            values = fvals[...]
        weights = jnp.exp2((scores - top) * scale).astype(jnp.bfloat16)
        part = jnp.dot(weights, values, preferred_element_type=jnp.float32)
        return part if acc is None else acc + part

    def finish(t, top, acc):
        total = acc[:, dim:]
        out = (acc[:, :dim] / total).astype(jnp.bfloat16)
        out_ref[pl.ds(t * span, span), :per_source, :] = out.reshape(span, per_source, dim)
        level = top * scale + jnp.log2(total)
        for first in range(0, tile, dim):
            flat = jnp.transpose(level[first : first + dim, :STAT_ROWS])
            high = flat.astype(jnp.bfloat16).astype(jnp.float32)
            mid = (flat - high).astype(jnp.bfloat16).astype(jnp.float32)
            low = flat - high - mid
            which = lax.broadcasted_iota(jnp.int32, flat.shape, 0)
            stats = jnp.where(which == 0, high, jnp.where(which == 1, mid, low)).astype(jnp.bfloat16)
            width = min(per_source, dim)
            for part in range(dim // width):
                row = first + part * width
                out_ref[t * span + row // per_source, per_source:, :width] = stats[
                    :, part * width : (part + 1) * width
                ]

    def stage(t_next, s_next, m_next, t_now, s_now, m_now, count):
        pieces = count + (1 if with_fresh else 0)
        best = None
        acc = None
        if t_now is not None:
            at = pl.ds(pl.multiple_of(t_now * tile, tile), tile)
            top = jnp.max(m_now[...], axis=1, keepdims=True) if pieces else None
            if with_state:
                before = top_in[at, :1]
                top = before if top is None else jnp.maximum(top, before)
                acc = acc_in[at, :] * jnp.exp2((before - top) * scale)
        for j in range(pieces):
            if t_next is not None:
                best = score_chunk(t_next, j, count, s_next, best)
            if t_now is not None:
                acc = value_chunk(j, count, s_now, top, acc)
        if t_next is not None and pieces:
            m_next[...] = best
        if t_now is not None:
            if final:
                finish(t_now, top, acc)
            else:
                acc_out[at, :] = acc
                top_out[at, :] = jnp.broadcast_to(top, (tile, dim))

    for count in range(chunks + 1):

        @pl.when(filled == count)
        def _(count=count):
            stage(0, s0, m0, None, None, None, count)

            def pair(i, carry):
                stage(2 * i + 1, s1, m1, 2 * i, s0, m0, count)
                stage(jnp.minimum(2 * i + 2, tiles - 1), s0, m0, 2 * i + 1, s1, m1, count)
                return carry

            lax.fori_loop(0, tiles // 2, pair, 0)

    if final:
        result = pltpu.make_async_copy(out_ref, out_hbm, out_sem)
        result.start()
        result.wait()


def attend(info, head_q, kv_blocks, order, fresh, state, final, row_start, row_count, group_size):
    sources, _, dim = head_q.shape
    slots = len(order) * kv_blocks[0].shape[1]
    rows = sources * row_count
    units = 0 if fresh is None else fresh[0].shape[0]
    tile = min(256, rows // 2)
    operands = [info, head_q] + [kv_blocks[k] for k in order]
    in_specs = [SMEM_SPEC] + [HBM_SPEC] * (1 + len(order))
    scratch = [
        pltpu.VMEM((sources, row_count, dim), jnp.bfloat16),
        pltpu.VMEM((slots, dim), jnp.bfloat16),
        pltpu.VMEM((slots, 2 * dim), jnp.bfloat16),
        pltpu.VMEM((tile, slots + units), jnp.float32),
        pltpu.VMEM((tile, slots + units), jnp.float32),
        pltpu.VMEM((tile, dim), jnp.float32),
        pltpu.VMEM((tile, dim), jnp.float32),
        pltpu.SemaphoreType.DMA((len(order), 2)),
        pltpu.SemaphoreType.DMA,
    ]
    if fresh is not None:
        operands += list(fresh)
        in_specs += [VMEM_SPEC] * 2
        scratch.append(pltpu.VMEM((units, 2 * dim), jnp.bfloat16))
    if state is not None:
        operands += list(state)
        in_specs += [VMEM_SPEC] * 2
    if final:
        out_shape = jax.ShapeDtypeStruct((sources, row_count + STAT_ROWS, dim), jnp.bfloat16)
        out_specs = HBM_SPEC
        scratch += [pltpu.SemaphoreType.DMA, pltpu.VMEM(out_shape.shape, jnp.bfloat16)]
    else:
        out_shape = [
            jax.ShapeDtypeStruct((rows, 2 * dim), jnp.float32),
            jax.ShapeDtypeStruct((rows, dim), jnp.float32),
        ]
        out_specs = [VMEM_SPEC] * 2
    grant = 8 * tile * (slots + units) + 6 * slots * dim + 24 * rows * dim + SMALL_VMEM
    return pl.pallas_call(
        functools.partial(
            attend_kernel,
            order=order,
            total_blocks=len(kv_blocks),
            tile=tile,
            group_size=group_size,
            row_start=row_start,
            with_fresh=fresh is not None,
            with_state=state is not None,
            final=final,
        ),
        in_specs=in_specs,
        out_specs=out_specs,
        scratch_shapes=scratch,
        out_shape=out_shape,
        compiler_params=pltpu.CompilerParams(vmem_limit_bytes=grant),
        cost_estimate=pl.CostEstimate(
            flops=4 * rows * slots * dim,
            bytes_accessed=4 * slots * dim + 4 * rows * dim,
            transcendentals=rows * slots,
        ),
    )(*operands)


def merge_kernel(part_ref, *refs, group_size):
    out_ref = refs[-1]
    spread, heads, _, dim = part_ref.shape
    local_rows = out_ref.shape[1]
    per_source = local_rows * group_size
    levels = []
    for b in range(spread):
        stats = [
            part_ref[b, h, per_source : per_source + STAT_ROWS, :].astype(jnp.float32) for h in range(heads)
        ]
        levels.append(jnp.concatenate([x[0:1] + x[1:2] + x[2:3] for x in stats], axis=0))
    top = functools.reduce(jnp.maximum, levels)
    weights = [jnp.exp2(level - top) for level in levels]
    total = functools.reduce(jnp.add, weights)
    weights = [jnp.transpose(w / total) for w in weights]
    for h in range(heads):
        mixed = functools.reduce(
            jnp.add,
            [
                w[:per_source, h : h + 1] * part_ref[b, h, :per_source, :].astype(jnp.float32)
                for b, w in enumerate(weights)
            ],
        ).astype(jnp.bfloat16)
        out_ref[0, :, h * group_size : (h + 1) * group_size, :] = mixed.reshape(local_rows, group_size, dim)


def merge(parts, request, requests, local_rows, group_size, earlier):
    heads, dim = parts.shape[1], parts.shape[3]
    rest = [] if earlier is None else [earlier]
    return pl.pallas_call(
        functools.partial(merge_kernel, group_size=group_size),
        grid=(1,),
        in_specs=[pl.BlockSpec(parts.shape, lambda i: (0, 0, 0, 0))]
        + [pl.BlockSpec(memory_space=pl.ANY) for _ in rest],
        out_specs=pl.BlockSpec((1, local_rows, heads * group_size, dim), lambda i: (request, 0, 0, 0)),
        out_shape=jax.ShapeDtypeStruct((requests, local_rows, heads * group_size, dim), jnp.bfloat16),
        input_output_aliases={1: 0} if rest else {},
        compiler_params=pltpu.CompilerParams(vmem_limit_bytes=SMALL_VMEM),
    )(parts, *rest)


def pack_kernel(q_ref, fresh_ref, out_ref):
    requests, local_rows, heads, dim = q_ref.shape
    kv_heads = fresh_ref.shape[0]
    group_size = heads // kv_heads
    rows = requests * local_rows * group_size
    for d in range(out_ref.shape[0]):
        head = d % kv_heads
        out_ref[d, :rows, :] = q_ref[:, :, head * group_size : (head + 1) * group_size, :].reshape(rows, dim)
        out_ref[d, rows:, :] = fresh_ref[head]


def pack(queries, fresh, devices):
    requests, local_rows, heads, dim = queries.shape
    rows = requests * local_rows * (heads // fresh.shape[0]) + fresh.shape[1]
    return pl.pallas_call(
        pack_kernel,
        in_specs=[VMEM_SPEC, VMEM_SPEC],
        out_specs=VMEM_SPEC,
        out_shape=jax.ShapeDtypeStruct((devices, rows, dim), jnp.bfloat16),
        compiler_params=pltpu.CompilerParams(vmem_limit_bytes=SMALL_VMEM),
    )(queries, fresh)


def split_kernel(own_ref, k_hbm, v_hbm, *refs, request):
    loaded, held, sems = refs[-3:]
    copies = [
        pltpu.make_async_copy(hbm.at[request], loaded.at[i], sems.at[i]) for i, hbm in enumerate((k_hbm, v_hbm))
    ]
    for copy in copies:
        copy.start()
    for i, copy in enumerate(copies):
        copy.wait()
        held[:, i] = jnp.swapaxes(loaded[i], 0, 1)
    for k, out_ref in enumerate(refs[:-3]):
        out_ref[...] = held[own_ref[0] ^ k]


def split_heads(own, cache_k, cache_v, request):
    _, slots, kv_heads, dim = cache_k.shape
    return pl.pallas_call(
        functools.partial(split_kernel, request=request),
        in_specs=[SMEM_SPEC, HBM_SPEC, HBM_SPEC],
        out_specs=[VMEM_SPEC] * kv_heads,
        out_shape=[jax.ShapeDtypeStruct((2, slots, dim), jnp.bfloat16)] * kv_heads,
        scratch_shapes=[
            pltpu.VMEM((2, slots, kv_heads, dim), jnp.bfloat16),
            pltpu.VMEM((kv_heads, 2, slots, dim), jnp.bfloat16),
            pltpu.SemaphoreType.DMA((2,)),
        ],
        compiler_params=pltpu.CompilerParams(vmem_limit_bytes=2 * SMALL_VMEM),
    )(own, cache_k, cache_v)


def attention(queries, new_k, new_v, cache_k, cache_v, cache_len):
    requests, local_rows, heads, head_dim = queries.shape
    slots = cache_k.shape[1]
    kv_heads = cache_k.shape[2]
    group_size = heads // kv_heads
    devices_seq = lax.axis_size("seq")
    seq_index = lax.axis_index("seq")
    spread = devices_seq // kv_heads
    block = seq_index // kv_heads
    own = (seq_index % kv_heads).astype(jnp.int32)
    per_source = local_rows * group_size

    fresh = jnp.transpose(jnp.stack([new_k, new_v]), (3, 0, 1, 2, 4)).reshape(
        kv_heads, 2 * requests * local_rows, head_dim
    )
    head_q = lax.all_to_all(
        pack(queries, fresh, devices_seq), "seq", split_axis=0, concat_axis=0, tiled=True
    )
    head_fresh = head_q[:, requests * per_source :, :].reshape(
        devices_seq, 2, requests, local_rows, head_dim
    )
    head_fresh = jnp.transpose(head_fresh, (1, 2, 0, 3, 4)).reshape(
        2, requests, devices_seq * local_rows, head_dim
    )

    early = kv_heads - 2
    kv_blocks = []
    for r in range(requests):
        parts = split_heads(own[None], cache_k, cache_v, r)
        moved = [parts[0]]
        for k in range(1, kv_heads):
            moved.append(lax.ppermute(parts[k], "seq", [(i, i ^ k) for i in range(devices_seq)]))
        kv_blocks.append(moved)

    out = None
    for r in range(requests):
        held = kv_heads * slots
        valid = jnp.clip(cache_len[r] - block * held, 0, held)
        fresh_shift = jnp.where(block == spread - 1, 0, -devices_seq * local_rows)
        info = jnp.stack([valid, fresh_shift, own]).astype(jnp.int32)
        rows = (r * per_source, per_source, group_size)
        state = attend(
            info, head_q, kv_blocks[r], tuple(range(early)), (head_fresh[0, r], head_fresh[1, r]), None, False, *rows
        )
        part = attend(info, head_q, kv_blocks[r], tuple(range(early, kv_heads)), None, state, True, *rows)
        part = lax.all_to_all(part, "seq", split_axis=0, concat_axis=0, tiled=True)
        part = part.reshape(spread, kv_heads, per_source + STAT_ROWS, head_dim)
        out = merge(part, r, requests, local_rows, group_size, out)
    return out


def solution(mesh):
    in_specs = (
        P("groups", "seq", None, None),
        P("groups", "seq", None, None),
        P("groups", "seq", None, None),
        P("groups", "seq", None, None),
        P("groups", "seq", None, None),
        P("groups"),
    )
    out_specs = P("groups", "seq", None, None)
    return jax.shard_map(attention, mesh=mesh, in_specs=in_specs, out_specs=out_specs, check_vma=False)
```

```python
import functools
import math

import jax
import jax.numpy as jnp
from jax import lax
from jax.experimental import pallas as pl
from jax.experimental.pallas import tpu as pltpu
from jax.sharding import PartitionSpec as P


NEG = -1e30
STAT_ROWS = 8
SMALL_VMEM = 12 * 2**20
LARGE_VMEM = 56 * 2**20


VMEM_SPEC = pl.BlockSpec(memory_space=pltpu.VMEM)
HBM_SPEC = pl.BlockSpec(memory_space=pltpu.HBM)
SMEM_SPEC = pl.BlockSpec(memory_space=pltpu.SMEM)


def attend_kernel(
    *refs, q_count, order, total_blocks, tile, group_size, row_start, with_fresh, with_state, final, out_count
):
    refs = list(refs)
    info_ref = refs.pop(0)
    q_hbm = [refs.pop(0) for _ in range(q_count)]
    kv_refs = [refs.pop(0) for _ in order]
    if with_fresh:
        fk_ref, fv_ref = refs.pop(0), refs.pop(0)
    if with_state:
        acc_in, top_in = refs.pop(0), refs.pop(0)
    if final:
        out_hbm = [refs.pop(0) for _ in range(out_count)]
    else:
        acc_out, top_out = refs.pop(0), refs.pop(0)
    if final:
        out_ref, out_sems = refs.pop(), refs.pop()
    if with_fresh:
        fvals = refs.pop()
    q_ref, keys, vals, s0, s1, m0, m1, in_sems, q_sems = refs
    per_source, dim = q_ref.shape[1:]
    block_slots = kv_refs[0].shape[1]
    chunk = 2 * block_slots
    chunks = len(order) // 2
    slots = chunks * chunk
    rows = q_ref.shape[0] * per_source
    tiles = rows // tile
    span = tile // per_source
    scale = math.log2(math.e) / math.sqrt(dim)
    valid = info_ref[0]
    fresh_shift = info_ref[1]
    own = info_ref[2]
    me = info_ref[3]

    held = sorted({k // 2 for k in order})
    absent = [c for c in range(total_blocks // 2) if c not in held]

    def rank_of(index):
        rank = index
        for c in absent:
            rank = rank - jnp.where((own // 2) ^ c < index, 1, 0)
        return rank

    q_rows = pl.ds(row_start, per_source)
    if q_count == 1:
        copies = [pltpu.make_async_copy(q_hbm[0].at[:, q_rows, :], q_ref, q_sems.at[0])]
    else:
        copies = [
            pltpu.make_async_copy(hbm.at[q_rows, :], q_ref.at[me ^ k], q_sems.at[k]) for k, hbm in enumerate(q_hbm)
        ]
    for i, k in enumerate(order):
        first = rank_of((own // 2) ^ (k // 2)) * chunk + ((own % 2) ^ (k % 2)) * block_slots
        at = pl.ds(pl.multiple_of(first, block_slots), block_slots)
        copies.append(pltpu.make_async_copy(kv_refs[i].at[0], keys.at[at, :], in_sems.at[i, 0]))
        copies.append(pltpu.make_async_copy(kv_refs[i].at[1], vals.at[at, :dim], in_sems.at[i, 1]))
    for copy in copies:
        copy.start()
    vals[:, dim:] = jnp.ones((slots, dim), jnp.bfloat16)
    if with_fresh:
        fresh = fk_ref.shape[0]
        fvals[:, :dim] = fv_ref[...]
        fvals[:, dim:] = jnp.ones((fresh, dim), jnp.bfloat16)

    filled = jnp.int32(0)
    last_valid = jnp.int32(0)
    for c in held:
        left = valid - ((own // 2) ^ c) * chunk
        filled = filled + jnp.where(left > 0, 1, 0)
        last_valid = jnp.where((left > 0) & (left < chunk), left, last_valid)
    last_valid = jnp.where(last_valid == 0, chunk, last_valid)
    for copy in copies:
        copy.wait()

    def product(a, b):
        return lax.dot_general(a, b, (((1,), (1,)), ((), ())), preferred_element_type=jnp.float32)

    def lane_max(scores, best):
        for lane in range(scores.shape[1] // dim):
            part = scores[:, lane * dim : (lane + 1) * dim]
            best = part if best is None else jnp.maximum(best, part)
        return best

    def score_chunk(t, j, count, s_ref, best):
        q = q_ref[pl.ds(t * span, span)].reshape(tile, dim)
        if j < count:
            scores = product(q, keys[j * chunk : (j + 1) * chunk, :])
            if j == count - 1:
                pos = lax.broadcasted_iota(jnp.int32, (1, chunk), 1)
                scores = scores + jnp.where(pos < last_valid, 0.0, NEG)
            s_ref[:, j * chunk : (j + 1) * chunk] = scores
            return lane_max(scores, best)
        scores = product(q, fk_ref[...])
        token = (t * tile + lax.broadcasted_iota(jnp.int32, (tile, 1), 0)) // group_size
        unit = lax.broadcasted_iota(jnp.int32, (1, fresh), 1)
        if q_count > 1:
            local_rows = per_source // group_size
            unit = ((unit // local_rows) ^ me) * local_rows + unit % local_rows
        scores = jnp.where(unit <= token + fresh_shift, scores, NEG)
        s_ref[:, slots : slots + fresh] = scores
        return lane_max(scores, best)

    def value_chunk(j, count, s_ref, top, acc):
        if j < count:
            scores = s_ref[:, j * chunk : (j + 1) * chunk]
            values = vals[j * chunk : (j + 1) * chunk, :]
        else:
            scores = s_ref[:, slots : slots + fresh]
            values = fvals[...]
        weights = jnp.exp2((scores - top) * scale).astype(jnp.bfloat16)
        part = jnp.dot(weights, values, preferred_element_type=jnp.float32)
        return part if acc is None else acc + part

    def finish(t, top, acc):
        total = acc[:, dim:]
        out = (acc[:, :dim] / total).astype(jnp.bfloat16)
        out_ref[pl.ds(t * span, span), :per_source, :] = out.reshape(span, per_source, dim)
        level = top * scale + jnp.log2(total)
        for first in range(0, tile, dim):
            flat = jnp.transpose(level[first : first + dim, :STAT_ROWS])
            high = flat.astype(jnp.bfloat16).astype(jnp.float32)
            mid = (flat - high).astype(jnp.bfloat16).astype(jnp.float32)
            low = flat - high - mid
            which = lax.broadcasted_iota(jnp.int32, flat.shape, 0)
            stats = jnp.where(which == 0, high, jnp.where(which == 1, mid, low)).astype(jnp.bfloat16)
            width = min(per_source, dim)
            for part in range(dim // width):
                row = first + part * width
                out_ref[t * span + row // per_source, per_source:, :width] = stats[
                    :, part * width : (part + 1) * width
                ]

    def stage(t_next, s_next, m_next, t_now, s_now, m_now, count):
        pieces = count + (1 if with_fresh else 0)
        best = None
        acc = None
        if t_now is not None:
            at = pl.ds(pl.multiple_of(t_now * tile, tile), tile)
            top = jnp.max(m_now[...], axis=1, keepdims=True) if pieces else None
            if with_state:
                before = top_in[at, :1]
                top = before if top is None else jnp.maximum(top, before)
                acc = acc_in[at, :] * jnp.exp2((before - top) * scale)
        for j in range(pieces):
            if t_next is not None:
                best = score_chunk(t_next, j, count, s_next, best)
            if t_now is not None:
                acc = value_chunk(j, count, s_now, top, acc)
        if t_next is not None and pieces:
            m_next[...] = best
        if t_now is not None:
            if final:
                finish(t_now, top, acc)
            else:
                acc_out[at, :] = acc
                top_out[at, :] = jnp.broadcast_to(top, (tile, dim))

    for count in range(chunks + 1):

        @pl.when(filled == count)
        def _(count=count):
            stage(0, s0, m0, None, None, None, count)

            def pair(i, carry):
                stage(2 * i + 1, s1, m1, 2 * i, s0, m0, count)
                stage(jnp.minimum(2 * i + 2, tiles - 1), s0, m0, 2 * i + 1, s1, m1, count)
                return carry

            lax.fori_loop(0, tiles // 2, pair, 0)

    if final:
        if out_count == 1:
            results = [pltpu.make_async_copy(out_ref, out_hbm[0], out_sems.at[0])]
        else:
            results = [
                pltpu.make_async_copy(out_ref.at[me ^ k], hbm, out_sems.at[k]) for k, hbm in enumerate(out_hbm)
            ]
        for result in results:
            result.start()
        for result in results:
            result.wait()


def attend(info, head_q, kv_blocks, order, fresh, state, final, out_count, sources, row_start, row_count, group_size):
    dim = head_q[0].shape[-1]
    slots = len(order) * kv_blocks[0].shape[1]
    rows = sources * row_count
    units = 0 if fresh is None else fresh[0].shape[0]
    tile = min(256, rows // 2)
    operands = [info] + head_q + [kv_blocks[k] for k in order]
    in_specs = [SMEM_SPEC] + [HBM_SPEC] * (len(head_q) + len(order))
    scratch = [
        pltpu.VMEM((sources, row_count, dim), jnp.bfloat16),
        pltpu.VMEM((slots, dim), jnp.bfloat16),
        pltpu.VMEM((slots, 2 * dim), jnp.bfloat16),
        pltpu.VMEM((tile, slots + units), jnp.float32),
        pltpu.VMEM((tile, slots + units), jnp.float32),
        pltpu.VMEM((tile, dim), jnp.float32),
        pltpu.VMEM((tile, dim), jnp.float32),
        pltpu.SemaphoreType.DMA((len(order), 2)),
        pltpu.SemaphoreType.DMA((len(head_q),)),
    ]
    if fresh is not None:
        operands += list(fresh)
        in_specs += [VMEM_SPEC] * 2
        scratch.append(pltpu.VMEM((units, 2 * dim), jnp.bfloat16))
    if state is not None:
        operands += list(state)
        in_specs += [VMEM_SPEC] * 2
    if final:
        whole = (sources, row_count + STAT_ROWS, dim)
        each = whole if out_count == 1 else whole[1:]
        out_shape = [jax.ShapeDtypeStruct(each, jnp.bfloat16)] * out_count
        out_specs = [HBM_SPEC] * out_count
        scratch += [pltpu.SemaphoreType.DMA((out_count,)), pltpu.VMEM(whole, jnp.bfloat16)]
    else:
        out_shape = [
            jax.ShapeDtypeStruct((rows, 2 * dim), jnp.float32),
            jax.ShapeDtypeStruct((rows, dim), jnp.float32),
        ]
        out_specs = [VMEM_SPEC] * 2
    grant = 8 * tile * (slots + units) + 6 * slots * dim + 24 * rows * dim + SMALL_VMEM
    return pl.pallas_call(
        functools.partial(
            attend_kernel,
            q_count=len(head_q),
            out_count=out_count,
            order=order,
            total_blocks=len(kv_blocks),
            tile=tile,
            group_size=group_size,
            row_start=row_start,
            with_fresh=fresh is not None,
            with_state=state is not None,
            final=final,
        ),
        in_specs=in_specs,
        out_specs=out_specs,
        scratch_shapes=scratch,
        out_shape=out_shape,
        compiler_params=pltpu.CompilerParams(vmem_limit_bytes=grant),
        cost_estimate=pl.CostEstimate(
            flops=4 * rows * slots * dim,
            bytes_accessed=4 * slots * dim + 4 * rows * dim,
            transcendentals=rows * slots,
        ),
    )(*operands)


def merge_kernel(own_ref, *refs, count, spread, heads, group_size):
    parts, out_ref = refs[:count], refs[-1]
    _, local_rows, _, dim = out_ref.shape
    per_source = local_rows * group_size

    def part(b, h):
        return parts[0].at[b * heads + h] if count == 1 else parts[b * heads + h]

    levels = []
    for b in range(spread):
        stats = [part(b, h)[per_source : per_source + STAT_ROWS, :].astype(jnp.float32) for h in range(heads)]
        levels.append(jnp.concatenate([x[0:1] + x[1:2] + x[2:3] for x in stats], axis=0))
    top = functools.reduce(jnp.maximum, levels)
    weights = [jnp.exp2(level - top) for level in levels]
    total = functools.reduce(jnp.add, weights)
    weights = [jnp.transpose(w / total) for w in weights]
    for h in range(heads):
        mixed = functools.reduce(
            jnp.add,
            [
                w[:per_source, h : h + 1] * part(b, h)[:per_source, :].astype(jnp.float32)
                for b, w in enumerate(weights)
            ],
        ).astype(jnp.bfloat16)
        first = h * group_size if count == 1 else pl.multiple_of((own_ref[0] ^ h) * group_size, group_size)
        out_ref[0, :, pl.ds(first, group_size), :] = mixed.reshape(local_rows, group_size, dim)


def merge(own, parts, kv_heads, spread, request, requests, local_rows, group_size, earlier):
    dim = parts[0].shape[-1]
    rest = [] if earlier is None else [earlier]

    def whole(array):
        return pl.BlockSpec(array.shape, lambda i: (0,) * array.ndim)

    return pl.pallas_call(
        functools.partial(merge_kernel, count=len(parts), spread=spread, heads=kv_heads, group_size=group_size),
        grid=(1,),
        in_specs=[SMEM_SPEC] + [whole(x) for x in parts] + [pl.BlockSpec(memory_space=pl.ANY) for _ in rest],
        out_specs=pl.BlockSpec((1, local_rows, kv_heads * group_size, dim), lambda i: (request, 0, 0, 0)),
        out_shape=jax.ShapeDtypeStruct((requests, local_rows, kv_heads * group_size, dim), jnp.bfloat16),
        input_output_aliases={1 + len(parts): 0} if rest else {},
        compiler_params=pltpu.CompilerParams(vmem_limit_bytes=SMALL_VMEM),
    )(own, *parts, *rest)


def pack_kernel(own_ref, q_ref, fresh_ref, *out_refs):
    requests, local_rows, heads, dim = q_ref.shape
    kv_heads = fresh_ref.shape[0]
    group_size = heads // kv_heads
    rows = requests * local_rows * group_size
    for d, out_ref in enumerate(out_refs):
        head = own_ref[0] ^ d
        first = pl.multiple_of(head * group_size, group_size)
        out_ref[:rows, :] = q_ref[:, :, pl.ds(first, group_size), :].reshape(rows, dim)
        out_ref[rows:, :] = fresh_ref[head]


def pack(own, queries, fresh):
    requests, local_rows, heads, dim = queries.shape
    kv_heads = fresh.shape[0]
    rows = requests * local_rows * (heads // kv_heads) + fresh.shape[1]
    return pl.pallas_call(
        pack_kernel,
        in_specs=[SMEM_SPEC, VMEM_SPEC, VMEM_SPEC],
        out_specs=[VMEM_SPEC] * kv_heads,
        out_shape=[jax.ShapeDtypeStruct((rows, dim), jnp.bfloat16)] * kv_heads,
        compiler_params=pltpu.CompilerParams(vmem_limit_bytes=SMALL_VMEM),
    )(own, queries, fresh)


def split_kernel(own_ref, k_hbm, v_hbm, *refs, request):
    loaded, held, sems = refs[-3:]
    copies = [
        pltpu.make_async_copy(hbm.at[request], loaded.at[i], sems.at[i]) for i, hbm in enumerate((k_hbm, v_hbm))
    ]
    for copy in copies:
        copy.start()
    for i, copy in enumerate(copies):
        copy.wait()
        held[:, i] = jnp.swapaxes(loaded[i], 0, 1)
    for k, out_ref in enumerate(refs[:-3]):
        out_ref[...] = held[own_ref[0] ^ k]


def split_heads(own, cache_k, cache_v, request):
    _, slots, kv_heads, dim = cache_k.shape
    return pl.pallas_call(
        functools.partial(split_kernel, request=request),
        in_specs=[SMEM_SPEC, HBM_SPEC, HBM_SPEC],
        out_specs=[VMEM_SPEC] * kv_heads,
        out_shape=[jax.ShapeDtypeStruct((2, slots, dim), jnp.bfloat16)] * kv_heads,
        scratch_shapes=[
            pltpu.VMEM((2, slots, kv_heads, dim), jnp.bfloat16),
            pltpu.VMEM((kv_heads, 2, slots, dim), jnp.bfloat16),
            pltpu.SemaphoreType.DMA((2,)),
        ],
        compiler_params=pltpu.CompilerParams(vmem_limit_bytes=LARGE_VMEM),
    )(own, cache_k, cache_v)


def attention(queries, new_k, new_v, cache_k, cache_v, cache_len):
    requests, local_rows, heads, head_dim = queries.shape
    slots = cache_k.shape[1]
    kv_heads = cache_k.shape[2]
    group_size = heads // kv_heads
    devices_seq = lax.axis_size("seq")
    seq_index = lax.axis_index("seq")
    spread = devices_seq // kv_heads
    block = seq_index // kv_heads
    own = (seq_index % kv_heads).astype(jnp.int32)
    per_source = local_rows * group_size

    devices = range(devices_seq)
    direct = spread <= 2
    fresh = jnp.transpose(jnp.stack([new_k, new_v]), (3, 0, 1, 2, 4)).reshape(
        kv_heads, 2 * requests * local_rows, head_dim
    )

    def to_partner(array, k):
        return lax.ppermute(array, "seq", [(i, i ^ k) for i in devices])

    if direct:
        packed = pack(own[None], queries, fresh)
        head_q = [packed[0]]
        for k in range(1, devices_seq):
            head_q.append(to_partner(packed[k % kv_heads], k))
        head_fresh = jnp.stack([x[requests * per_source :, :] for x in head_q])
    else:
        packed = jnp.stack(pack(jnp.zeros((1,), jnp.int32), queries, fresh))
        packed = jnp.broadcast_to(packed[None], (spread,) + packed.shape).reshape((devices_seq,) + packed.shape[1:])
        head_q = lax.all_to_all(packed, "seq", split_axis=0, concat_axis=0, tiled=True)
        head_fresh = head_q[:, requests * per_source :, :]
        head_q = [head_q]
    head_fresh = head_fresh.reshape(devices_seq, 2, requests, local_rows, head_dim)
    head_fresh = jnp.transpose(head_fresh, (1, 2, 0, 3, 4)).reshape(
        2, requests, devices_seq * local_rows, head_dim
    )

    early = kv_heads - 2
    kv_blocks = []
    for r in range(requests):
        parts = split_heads(own[None], cache_k, cache_v, r)
        moved = [parts[0]]
        for k in range(1, kv_heads):
            moved.append(to_partner(parts[k], k))
        kv_blocks.append(moved)

    out = None
    for r in range(requests):
        held = kv_heads * slots
        valid = jnp.clip(cache_len[r] - block * held, 0, held)
        fresh_shift = jnp.where(block == spread - 1, 0, -devices_seq * local_rows)
        info = jnp.stack([valid, fresh_shift, own, seq_index]).astype(jnp.int32)
        rows = (devices_seq, r * per_source, per_source, group_size)
        separate = direct and r == requests - 1
        out_count = devices_seq if separate else 1
        state = attend(
            info,
            head_q,
            kv_blocks[r],
            tuple(range(early)),
            (head_fresh[0, r], head_fresh[1, r]),
            None,
            False,
            1,
            *rows,
        )
        parts = attend(info, head_q, kv_blocks[r], tuple(range(early, kv_heads)), None, state, True, out_count, *rows)
        if separate:
            parts = [parts[0]] + [to_partner(parts[k], k) for k in range(1, devices_seq)]
        else:
            parts = [lax.all_to_all(parts[0], "seq", split_axis=0, concat_axis=0, tiled=True)]
        out = merge(own[None], parts, kv_heads, spread, r, requests, local_rows, group_size, out)
    return out


def solution(mesh):
    in_specs = (
        P("groups", "seq", None, None),
        P("groups", "seq", None, None),
        P("groups", "seq", None, None),
        P("groups", "seq", None, None),
        P("groups", "seq", None, None),
        P("groups"),
    )
    out_specs = P("groups", "seq", None, None)
    return jax.shard_map(attention, mesh=mesh, in_specs=in_specs, out_specs=out_specs, check_vma=False)
```

```python
import functools
import math

import jax
import jax.numpy as jnp
from jax import lax
from jax.experimental import pallas as pl
from jax.experimental.pallas import tpu as pltpu
from jax.sharding import PartitionSpec as P


NEG = -1e30
STAT_ROWS = 8
SMALL_VMEM = 12 * 2**20
LARGE_VMEM = 56 * 2**20


VMEM_SPEC = pl.BlockSpec(memory_space=pltpu.VMEM)
HBM_SPEC = pl.BlockSpec(memory_space=pltpu.HBM)
SMEM_SPEC = pl.BlockSpec(memory_space=pltpu.SMEM)


def attend_kernel(*refs, order, total_blocks, tile, group_size, row_start, with_fresh, with_state, final):
    refs = list(refs)
    info_ref, q_hbm = refs.pop(0), refs.pop(0)
    kv_refs = [refs.pop(0) for _ in order]
    if with_fresh:
        fk_ref, fv_ref = refs.pop(0), refs.pop(0)
    if with_state:
        acc_in, top_in = refs.pop(0), refs.pop(0)
    if final:
        out_hbm = refs.pop(0)
    else:
        acc_out, top_out = refs.pop(0), refs.pop(0)
    if final:
        out_ref, out_sem = refs.pop(), refs.pop()
    if with_fresh:
        fvals = refs.pop()
    q_ref, keys, vals, s0, s1, m0, m1, in_sems, q_sem = refs
    per_source, dim = q_ref.shape[1:]
    block_slots = kv_refs[0].shape[1]
    chunk = 2 * block_slots
    chunks = len(order) // 2
    slots = chunks * chunk
    rows = q_ref.shape[0] * per_source
    tiles = rows // tile
    span = tile // per_source
    scale = math.log2(math.e) / math.sqrt(dim)
    valid = info_ref[0]
    fresh_shift = info_ref[1]
    own = info_ref[2]

    held = sorted({k // 2 for k in order})
    absent = [c for c in range(total_blocks // 2) if c not in held]

    def rank_of(index):
        rank = index
        for c in absent:
            rank = rank - jnp.where((own // 2) ^ c < index, 1, 0)
        return rank

    copies = [pltpu.make_async_copy(q_hbm.at[:, row_start : row_start + per_source, :], q_ref, q_sem)]
    for i, k in enumerate(order):
        first = rank_of((own // 2) ^ (k // 2)) * chunk + ((own % 2) ^ (k % 2)) * block_slots
        at = pl.ds(pl.multiple_of(first, block_slots), block_slots)
        copies.append(pltpu.make_async_copy(kv_refs[i].at[0], keys.at[at, :], in_sems.at[i, 0]))
        copies.append(pltpu.make_async_copy(kv_refs[i].at[1], vals.at[at, :dim], in_sems.at[i, 1]))
    for copy in copies:
        copy.start()
    vals[:, dim:] = jnp.ones((slots, dim), jnp.bfloat16)
    if with_fresh:
        fresh = fk_ref.shape[0]
        fvals[:, :dim] = fv_ref[...]
        fvals[:, dim:] = jnp.ones((fresh, dim), jnp.bfloat16)

    filled = jnp.int32(0)
    last_valid = jnp.int32(0)
    for c in held:
        left = valid - ((own // 2) ^ c) * chunk
        filled = filled + jnp.where(left > 0, 1, 0)
        last_valid = jnp.where((left > 0) & (left < chunk), left, last_valid)
    last_valid = jnp.where(last_valid == 0, chunk, last_valid)
    for copy in copies:
        copy.wait()

    def product(a, b):
        return lax.dot_general(a, b, (((1,), (1,)), ((), ())), preferred_element_type=jnp.float32)

    def lane_max(scores, best):
        for lane in range(scores.shape[1] // dim):
            part = scores[:, lane * dim : (lane + 1) * dim]
            best = part if best is None else jnp.maximum(best, part)
        return best

    def score_chunk(t, j, count, s_ref, best):
        q = q_ref[pl.ds(t * span, span)].reshape(tile, dim)
        if j < count:
            scores = product(q, keys[j * chunk : (j + 1) * chunk, :])
            if j == count - 1:
                pos = lax.broadcasted_iota(jnp.int32, (1, chunk), 1)
                scores = scores + jnp.where(pos < last_valid, 0.0, NEG)
            s_ref[:, j * chunk : (j + 1) * chunk] = scores
            return lane_max(scores, best)
        scores = product(q, fk_ref[...])
        token = (t * tile + lax.broadcasted_iota(jnp.int32, (tile, 1), 0)) // group_size
        unit = lax.broadcasted_iota(jnp.int32, (1, fresh), 1)
        scores = jnp.where(unit <= token + fresh_shift, scores, NEG)
        s_ref[:, slots : slots + fresh] = scores
        return lane_max(scores, best)

    def value_chunk(j, count, s_ref, top, acc):
        if j < count:
            scores = s_ref[:, j * chunk : (j + 1) * chunk]
            values = vals[j * chunk : (j + 1) * chunk, :]
        else:
            scores = s_ref[:, slots : slots + fresh]
            values = fvals[...]
        weights = jnp.exp2((scores - top) * scale).astype(jnp.bfloat16)
        part = jnp.dot(weights, values, preferred_element_type=jnp.float32)
        return part if acc is None else acc + part

    def finish(t, top, acc):
        total = acc[:, dim:]
        out = (acc[:, :dim] / total).astype(jnp.bfloat16)
        out_ref[pl.ds(t * span, span), :per_source, :] = out.reshape(span, per_source, dim)
        level = top * scale + jnp.log2(total)
        for first in range(0, tile, dim):
            flat = jnp.transpose(level[first : first + dim, :STAT_ROWS])
            high = flat.astype(jnp.bfloat16).astype(jnp.float32)
            mid = (flat - high).astype(jnp.bfloat16).astype(jnp.float32)
            low = flat - high - mid
            which = lax.broadcasted_iota(jnp.int32, flat.shape, 0)
            stats = jnp.where(which == 0, high, jnp.where(which == 1, mid, low)).astype(jnp.bfloat16)
            width = min(per_source, dim)
            for part in range(dim // width):
                row = first + part * width
                out_ref[t * span + row // per_source, per_source:, :width] = stats[
                    :, part * width : (part + 1) * width
                ]

    def stage(t_next, s_next, m_next, t_now, s_now, m_now, count):
        pieces = count + (1 if with_fresh else 0)
        best = None
        acc = None
        if t_now is not None:
            at = pl.ds(pl.multiple_of(t_now * tile, tile), tile)
            top = jnp.max(m_now[...], axis=1, keepdims=True) if pieces else None
            if with_state:
                before = top_in[at, :1]
                top = before if top is None else jnp.maximum(top, before)
                acc = acc_in[at, :] * jnp.exp2((before - top) * scale)
        for j in range(pieces):
            if t_next is not None:
                best = score_chunk(t_next, j, count, s_next, best)
            if t_now is not None:
                acc = value_chunk(j, count, s_now, top, acc)
        if t_next is not None and pieces:
            m_next[...] = best
        if t_now is not None:
            if final:
                finish(t_now, top, acc)
            else:
                acc_out[at, :] = acc
                top_out[at, :] = jnp.broadcast_to(top, (tile, dim))

    for count in range(chunks + 1):

        @pl.when(filled == count)
        def _(count=count):
            stage(0, s0, m0, None, None, None, count)

            def pair(i, carry):
                stage(2 * i + 1, s1, m1, 2 * i, s0, m0, count)
                stage(jnp.minimum(2 * i + 2, tiles - 1), s0, m0, 2 * i + 1, s1, m1, count)
                return carry

            lax.fori_loop(0, tiles // 2, pair, 0)

    if final:
        result = pltpu.make_async_copy(out_ref, out_hbm, out_sem)
        result.start()
        result.wait()


def attend(info, head_q, kv_blocks, order, fresh, state, final, row_start, row_count, group_size):
    sources, _, dim = head_q.shape
    slots = len(order) * kv_blocks[0].shape[1]
    rows = sources * row_count
    units = 0 if fresh is None else fresh[0].shape[0]
    tile = min(256, rows // 2)
    operands = [info, head_q] + [kv_blocks[k] for k in order]
    in_specs = [SMEM_SPEC] + [HBM_SPEC] * (1 + len(order))
    scratch = [
        pltpu.VMEM((sources, row_count, dim), jnp.bfloat16),
        pltpu.VMEM((slots, dim), jnp.bfloat16),
        pltpu.VMEM((slots, 2 * dim), jnp.bfloat16),
        pltpu.VMEM((tile, slots + units), jnp.float32),
        pltpu.VMEM((tile, slots + units), jnp.float32),
        pltpu.VMEM((tile, dim), jnp.float32),
        pltpu.VMEM((tile, dim), jnp.float32),
        pltpu.SemaphoreType.DMA((len(order), 2)),
        pltpu.SemaphoreType.DMA,
    ]
    if fresh is not None:
        operands += list(fresh)
        in_specs += [VMEM_SPEC] * 2
        scratch.append(pltpu.VMEM((units, 2 * dim), jnp.bfloat16))
    if state is not None:
        operands += list(state)
        in_specs += [VMEM_SPEC] * 2
    if final:
        out_shape = jax.ShapeDtypeStruct((sources, row_count + STAT_ROWS, dim), jnp.bfloat16)
        out_specs = HBM_SPEC
        scratch += [pltpu.SemaphoreType.DMA, pltpu.VMEM(out_shape.shape, jnp.bfloat16)]
    else:
        out_shape = [
            jax.ShapeDtypeStruct((rows, 2 * dim), jnp.float32),
            jax.ShapeDtypeStruct((rows, dim), jnp.float32),
        ]
        out_specs = [VMEM_SPEC] * 2
    grant = 8 * tile * (slots + units) + 6 * slots * dim + 24 * rows * dim + SMALL_VMEM
    return pl.pallas_call(
        functools.partial(
            attend_kernel,
            order=order,
            total_blocks=len(kv_blocks),
            tile=tile,
            group_size=group_size,
            row_start=row_start,
            with_fresh=fresh is not None,
            with_state=state is not None,
            final=final,
        ),
        in_specs=in_specs,
        out_specs=out_specs,
        scratch_shapes=scratch,
        out_shape=out_shape,
        compiler_params=pltpu.CompilerParams(vmem_limit_bytes=grant),
        cost_estimate=pl.CostEstimate(
            flops=4 * rows * slots * dim,
            bytes_accessed=4 * slots * dim + 4 * rows * dim,
            transcendentals=rows * slots,
        ),
    )(*operands)


def merge_kernel(part_ref, *refs, group_size):
    out_ref = refs[-1]
    spread, heads, _, dim = part_ref.shape
    local_rows = out_ref.shape[1]
    per_source = local_rows * group_size
    levels = []
    for b in range(spread):
        stats = [
            part_ref[b, h, per_source : per_source + STAT_ROWS, :].astype(jnp.float32) for h in range(heads)
        ]
        levels.append(jnp.concatenate([x[0:1] + x[1:2] + x[2:3] for x in stats], axis=0))
    top = functools.reduce(jnp.maximum, levels)
    weights = [jnp.exp2(level - top) for level in levels]
    total = functools.reduce(jnp.add, weights)
    weights = [jnp.transpose(w / total) for w in weights]
    for h in range(heads):
        mixed = functools.reduce(
            jnp.add,
            [
                w[:per_source, h : h + 1] * part_ref[b, h, :per_source, :].astype(jnp.float32)
                for b, w in enumerate(weights)
            ],
        ).astype(jnp.bfloat16)
        out_ref[0, :, h * group_size : (h + 1) * group_size, :] = mixed.reshape(local_rows, group_size, dim)


def merge(parts, request, requests, local_rows, group_size, earlier):
    heads, dim = parts.shape[1], parts.shape[3]
    rest = [] if earlier is None else [earlier]
    return pl.pallas_call(
        functools.partial(merge_kernel, group_size=group_size),
        grid=(1,),
        in_specs=[pl.BlockSpec(parts.shape, lambda i: (0, 0, 0, 0))]
        + [pl.BlockSpec(memory_space=pl.ANY) for _ in rest],
        out_specs=pl.BlockSpec((1, local_rows, heads * group_size, dim), lambda i: (request, 0, 0, 0)),
        out_shape=jax.ShapeDtypeStruct((requests, local_rows, heads * group_size, dim), jnp.bfloat16),
        input_output_aliases={1: 0} if rest else {},
        compiler_params=pltpu.CompilerParams(vmem_limit_bytes=SMALL_VMEM),
    )(parts, *rest)


def pack_kernel(q_ref, fresh_ref, out_ref):
    requests, local_rows, heads, dim = q_ref.shape
    kv_heads = fresh_ref.shape[0]
    group_size = heads // kv_heads
    rows = requests * local_rows * group_size
    for d in range(out_ref.shape[0]):
        head = d % kv_heads
        out_ref[d, :rows, :] = q_ref[:, :, head * group_size : (head + 1) * group_size, :].reshape(rows, dim)
        out_ref[d, rows:, :] = fresh_ref[head]


def pack(queries, fresh, devices):
    requests, local_rows, heads, dim = queries.shape
    rows = requests * local_rows * (heads // fresh.shape[0]) + fresh.shape[1]
    return pl.pallas_call(
        pack_kernel,
        in_specs=[VMEM_SPEC, VMEM_SPEC],
        out_specs=VMEM_SPEC,
        out_shape=jax.ShapeDtypeStruct((devices, rows, dim), jnp.bfloat16),
        compiler_params=pltpu.CompilerParams(vmem_limit_bytes=SMALL_VMEM),
    )(queries, fresh)


def split_kernel(own_ref, k_hbm, v_hbm, *refs, request):
    loaded, held, sems = refs[-3:]
    copies = [
        pltpu.make_async_copy(hbm.at[request], loaded.at[i], sems.at[i]) for i, hbm in enumerate((k_hbm, v_hbm))
    ]
    for copy in copies:
        copy.start()
    for i, copy in enumerate(copies):
        copy.wait()
        held[:, i] = jnp.swapaxes(loaded[i], 0, 1)
    for k, out_ref in enumerate(refs[:-3]):
        out_ref[...] = held[own_ref[0] ^ k]


def split_heads(own, cache_k, cache_v, request, grant):
    _, slots, kv_heads, dim = cache_k.shape
    return pl.pallas_call(
        functools.partial(split_kernel, request=request),
        in_specs=[SMEM_SPEC, HBM_SPEC, HBM_SPEC],
        out_specs=[VMEM_SPEC] * kv_heads,
        out_shape=[jax.ShapeDtypeStruct((2, slots, dim), jnp.bfloat16)] * kv_heads,
        scratch_shapes=[
            pltpu.VMEM((2, slots, kv_heads, dim), jnp.bfloat16),
            pltpu.VMEM((kv_heads, 2, slots, dim), jnp.bfloat16),
            pltpu.SemaphoreType.DMA((2,)),
        ],
        compiler_params=pltpu.CompilerParams(vmem_limit_bytes=grant),
    )(own, cache_k, cache_v)


def attention(queries, new_k, new_v, cache_k, cache_v, cache_len):
    requests, local_rows, heads, head_dim = queries.shape
    slots = cache_k.shape[1]
    kv_heads = cache_k.shape[2]
    group_size = heads // kv_heads
    devices_seq = lax.axis_size("seq")
    seq_index = lax.axis_index("seq")
    spread = devices_seq // kv_heads
    block = seq_index // kv_heads
    own = (seq_index % kv_heads).astype(jnp.int32)
    per_source = local_rows * group_size

    fresh = jnp.transpose(jnp.stack([new_k, new_v]), (3, 0, 1, 2, 4)).reshape(
        kv_heads, 2 * requests * local_rows, head_dim
    )
    head_q = lax.all_to_all(
        pack(queries, fresh, devices_seq), "seq", split_axis=0, concat_axis=0, tiled=True
    )
    head_fresh = head_q[:, requests * per_source :, :].reshape(
        devices_seq, 2, requests, local_rows, head_dim
    )
    head_fresh = jnp.transpose(head_fresh, (1, 2, 0, 3, 4)).reshape(
        2, requests, devices_seq * local_rows, head_dim
    )

    kv_blocks = []
    for r in range(requests):
        parts = split_heads(own[None], cache_k, cache_v, r, LARGE_VMEM if r == 0 else 2 * SMALL_VMEM)
        moved = [parts[0]]
        for k in range(1, kv_heads):
            moved.append(lax.ppermute(parts[k], "seq", [(i, i ^ k) for i in range(devices_seq)]))
        kv_blocks.append(moved)

    out = None
    for r in range(requests):
        held = kv_heads * slots
        valid = jnp.clip(cache_len[r] - block * held, 0, held)
        fresh_shift = jnp.where(block == spread - 1, 0, -devices_seq * local_rows)
        info = jnp.stack([valid, fresh_shift, own]).astype(jnp.int32)
        rows = (r * per_source, per_source, group_size)
        part = attend(
            info, head_q, kv_blocks[r], tuple(range(kv_heads)), (head_fresh[0, r], head_fresh[1, r]), None, True, *rows
        )
        part = lax.all_to_all(part, "seq", split_axis=0, concat_axis=0, tiled=True)
        part = part.reshape(spread, kv_heads, per_source + STAT_ROWS, head_dim)
        out = merge(part, r, requests, local_rows, group_size, out)
    return out


def solution(mesh):
    in_specs = (
        P("groups", "seq", None, None),
        P("groups", "seq", None, None),
        P("groups", "seq", None, None),
        P("groups", "seq", None, None),
        P("groups", "seq", None, None),
        P("groups"),
    )
    out_specs = P("groups", "seq", None, None)
    return jax.shard_map(attention, mesh=mesh, in_specs=in_specs, out_specs=out_specs, check_vma=False)
```

```python
import functools
import math

import jax
import jax.numpy as jnp
from jax import lax
from jax.experimental import pallas as pl
from jax.experimental.pallas import tpu as pltpu
from jax.sharding import PartitionSpec as P


NEG = -1e30
STAT_ROWS = 8
SMALL_VMEM = 12 * 2**20
LARGE_VMEM = 56 * 2**20


VMEM_SPEC = pl.BlockSpec(memory_space=pltpu.VMEM)
HBM_SPEC = pl.BlockSpec(memory_space=pltpu.HBM)
SMEM_SPEC = pl.BlockSpec(memory_space=pltpu.SMEM)


def attend_kernel(
    *refs, q_count, order, total_blocks, tile, group_size, row_start, with_fresh, with_state, final, out_count
):
    refs = list(refs)
    length_ref, place_ref = refs.pop(0), refs.pop(0)
    q_hbm = [refs.pop(0) for _ in range(q_count)]
    kv_refs = [refs.pop(0) for _ in order]
    if with_fresh:
        fk_ref, fv_ref = refs.pop(0), refs.pop(0)
    if with_state:
        acc_in, top_in = refs.pop(0), refs.pop(0)
    if final:
        out_hbm = [refs.pop(0) for _ in range(out_count)]
    else:
        acc_out, top_out = refs.pop(0), refs.pop(0)
    if final:
        out_ref, out_sems = refs.pop(), refs.pop()
    if with_fresh:
        fvals = refs.pop()
    q_ref, keys, vals, s0, s1, m0, m1, in_sems, q_sems = refs
    per_source, dim = q_ref.shape[1:]
    block_slots = kv_refs[0].shape[1]
    chunk = 2 * block_slots
    chunks = len(order) // 2
    slots = chunks * chunk
    rows = q_ref.shape[0] * per_source
    tiles = rows // tile
    span = tile // per_source
    scale = math.log2(math.e) / math.sqrt(dim)
    own, device_block, me = place_ref[0], place_ref[1], place_ref[2]
    valid = jnp.clip(length_ref[0] - device_block * total_blocks * block_slots, 0, total_blocks * block_slots)
    fresh_shift = jnp.where(device_block == q_ref.shape[0] // total_blocks - 1, 0, -rows)

    held = sorted({k // 2 for k in order})
    absent = [c for c in range(total_blocks // 2) if c not in held]

    def rank_of(index):
        rank = index
        for c in absent:
            rank = rank - jnp.where((own // 2) ^ c < index, 1, 0)
        return rank

    q_rows = pl.ds(row_start, per_source)
    if q_count == 1:
        copies = [pltpu.make_async_copy(q_hbm[0].at[:, q_rows, :], q_ref, q_sems.at[0])]
    else:
        copies = [
            pltpu.make_async_copy(hbm.at[q_rows, :], q_ref.at[me ^ k], q_sems.at[k]) for k, hbm in enumerate(q_hbm)
        ]
    for i, k in enumerate(order):
        first = rank_of((own // 2) ^ (k // 2)) * chunk + ((own % 2) ^ (k % 2)) * block_slots
        at = pl.ds(pl.multiple_of(first, block_slots), block_slots)
        copies.append(pltpu.make_async_copy(kv_refs[i].at[0], keys.at[at, :], in_sems.at[i, 0]))
        copies.append(pltpu.make_async_copy(kv_refs[i].at[1], vals.at[at, :dim], in_sems.at[i, 1]))
    for copy in copies:
        copy.start()
    vals[:, dim:] = jnp.ones((slots, dim), jnp.bfloat16)
    if with_fresh:
        fresh = fk_ref.shape[0]
        fvals[:, :dim] = fv_ref[...]
        fvals[:, dim:] = jnp.ones((fresh, dim), jnp.bfloat16)

    filled = jnp.int32(0)
    last_valid = jnp.int32(0)
    for c in held:
        left = valid - ((own // 2) ^ c) * chunk
        filled = filled + jnp.where(left > 0, 1, 0)
        last_valid = jnp.where((left > 0) & (left < chunk), left, last_valid)
    last_valid = jnp.where(last_valid == 0, chunk, last_valid)
    for copy in copies:
        copy.wait()

    def product(a, b):
        return lax.dot_general(a, b, (((1,), (1,)), ((), ())), preferred_element_type=jnp.float32)

    def lane_max(scores, best):
        for lane in range(scores.shape[1] // dim):
            part = scores[:, lane * dim : (lane + 1) * dim]
            best = part if best is None else jnp.maximum(best, part)
        return best

    def score_chunk(t, j, count, s_ref, best):
        q = q_ref[pl.ds(t * span, span)].reshape(tile, dim)
        if j < count:
            scores = product(q, keys[j * chunk : (j + 1) * chunk, :])
            if j == count - 1:
                pos = lax.broadcasted_iota(jnp.int32, (1, chunk), 1)
                scores = scores + jnp.where(pos < last_valid, 0.0, NEG)
            s_ref[:, j * chunk : (j + 1) * chunk] = scores
            return lane_max(scores, best)
        scores = product(q, fk_ref[...])
        token = (t * tile + lax.broadcasted_iota(jnp.int32, (tile, 1), 0)) // group_size
        unit = lax.broadcasted_iota(jnp.int32, (1, fresh), 1)
        if q_count > 1:
            local_rows = per_source // group_size
            unit = ((unit // local_rows) ^ me) * local_rows + unit % local_rows
        scores = jnp.where(unit <= token + fresh_shift, scores, NEG)
        s_ref[:, slots : slots + fresh] = scores
        return lane_max(scores, best)

    def value_chunk(j, count, s_ref, top, acc):
        if j < count:
            scores = s_ref[:, j * chunk : (j + 1) * chunk]
            values = vals[j * chunk : (j + 1) * chunk, :]
        else:
            scores = s_ref[:, slots : slots + fresh]
            values = fvals[...]
        weights = jnp.exp2((scores - top) * scale).astype(jnp.bfloat16)
        part = jnp.dot(weights, values, preferred_element_type=jnp.float32)
        return part if acc is None else acc + part

    def finish(t, top, acc):
        total = acc[:, dim:]
        out = (acc[:, :dim] / total).astype(jnp.bfloat16)
        out_ref[pl.ds(t * span, span), :per_source, :] = out.reshape(span, per_source, dim)
        level = top * scale + jnp.log2(total)
        for first in range(0, tile, dim):
            flat = jnp.transpose(level[first : first + dim, :STAT_ROWS])
            high = flat.astype(jnp.bfloat16).astype(jnp.float32)
            mid = (flat - high).astype(jnp.bfloat16).astype(jnp.float32)
            low = flat - high - mid
            which = lax.broadcasted_iota(jnp.int32, flat.shape, 0)
            stats = jnp.where(which == 0, high, jnp.where(which == 1, mid, low)).astype(jnp.bfloat16)
            width = min(per_source, dim)
            for part in range(dim // width):
                row = first + part * width
                out_ref[t * span + row // per_source, per_source:, :width] = stats[
                    :, part * width : (part + 1) * width
                ]

    def stage(t_next, s_next, m_next, t_now, s_now, m_now, count):
        pieces = count + (1 if with_fresh else 0)
        best = None
        acc = None
        if t_now is not None:
            at = pl.ds(pl.multiple_of(t_now * tile, tile), tile)
            top = jnp.max(m_now[...], axis=1, keepdims=True) if pieces else None
            if with_state:
                before = top_in[at, :1]
                top = before if top is None else jnp.maximum(top, before)
                acc = acc_in[at, :] * jnp.exp2((before - top) * scale)
        for j in range(pieces):
            if t_next is not None:
                best = score_chunk(t_next, j, count, s_next, best)
            if t_now is not None:
                acc = value_chunk(j, count, s_now, top, acc)
        if t_next is not None and pieces:
            m_next[...] = best
        if t_now is not None:
            if final:
                finish(t_now, top, acc)
            else:
                acc_out[at, :] = acc
                top_out[at, :] = jnp.broadcast_to(top, (tile, dim))

    for count in range(chunks + 1):

        @pl.when(filled == count)
        def _(count=count):
            stage(0, s0, m0, None, None, None, count)

            def pair(i, carry):
                stage(2 * i + 1, s1, m1, 2 * i, s0, m0, count)
                stage(jnp.minimum(2 * i + 2, tiles - 1), s0, m0, 2 * i + 1, s1, m1, count)
                return carry

            lax.fori_loop(0, tiles // 2, pair, 0)

    if final:
        if out_count == 1:
            results = [pltpu.make_async_copy(out_ref, out_hbm[0], out_sems.at[0])]
        else:
            results = [
                pltpu.make_async_copy(out_ref.at[me ^ k], hbm, out_sems.at[k]) for k, hbm in enumerate(out_hbm)
            ]
        for result in results:
            result.start()
        for result in results:
            result.wait()


def attend(length, place, head_q, kv_blocks, order, fresh, state, final, out_count, sources, row_start, row_count, group_size):
    dim = head_q[0].shape[-1]
    slots = len(order) * kv_blocks[0].shape[1]
    rows = sources * row_count
    units = 0 if fresh is None else fresh[0].shape[0]
    tile = min(256, rows // 2)
    operands = [length, place] + head_q + [kv_blocks[k] for k in order]
    in_specs = [SMEM_SPEC] * 2 + [HBM_SPEC] * (len(head_q) + len(order))
    scratch = [
        pltpu.VMEM((sources, row_count, dim), jnp.bfloat16),
        pltpu.VMEM((slots, dim), jnp.bfloat16),
        pltpu.VMEM((slots, 2 * dim), jnp.bfloat16),
        pltpu.VMEM((tile, slots + units), jnp.float32),
        pltpu.VMEM((tile, slots + units), jnp.float32),
        pltpu.VMEM((tile, dim), jnp.float32),
        pltpu.VMEM((tile, dim), jnp.float32),
        pltpu.SemaphoreType.DMA((len(order), 2)),
        pltpu.SemaphoreType.DMA((len(head_q),)),
    ]
    if fresh is not None:
        operands += list(fresh)
        in_specs += [VMEM_SPEC] * 2
        scratch.append(pltpu.VMEM((units, 2 * dim), jnp.bfloat16))
    if state is not None:
        operands += list(state)
        in_specs += [VMEM_SPEC] * 2
    if final:
        whole = (sources, row_count + STAT_ROWS, dim)
        each = whole if out_count == 1 else whole[1:]
        out_shape = [jax.ShapeDtypeStruct(each, jnp.bfloat16)] * out_count
        out_specs = [HBM_SPEC] * out_count
        scratch += [pltpu.SemaphoreType.DMA((out_count,)), pltpu.VMEM(whole, jnp.bfloat16)]
    else:
        out_shape = [
            jax.ShapeDtypeStruct((rows, 2 * dim), jnp.float32),
            jax.ShapeDtypeStruct((rows, dim), jnp.float32),
        ]
        out_specs = [VMEM_SPEC] * 2
    grant = 8 * tile * (slots + units) + 6 * slots * dim + 24 * rows * dim + SMALL_VMEM
    return pl.pallas_call(
        functools.partial(
            attend_kernel,
            q_count=len(head_q),
            out_count=out_count,
            order=order,
            total_blocks=len(kv_blocks),
            tile=tile,
            group_size=group_size,
            row_start=row_start,
            with_fresh=fresh is not None,
            with_state=state is not None,
            final=final,
        ),
        in_specs=in_specs,
        out_specs=out_specs,
        scratch_shapes=scratch,
        out_shape=out_shape,
        compiler_params=pltpu.CompilerParams(vmem_limit_bytes=grant),
        cost_estimate=pl.CostEstimate(
            flops=4 * rows * slots * dim,
            bytes_accessed=4 * slots * dim + 4 * rows * dim,
            transcendentals=rows * slots,
        ),
    )(*operands)


def merge_kernel(own_ref, *refs, count, spread, heads, group_size):
    parts, out_ref = refs[:count], refs[-1]
    _, local_rows, _, dim = out_ref.shape
    per_source = local_rows * group_size

    def part(b, h):
        return parts[0].at[b * heads + h] if count == 1 else parts[b * heads + h]

    levels = []
    for b in range(spread):
        stats = [part(b, h)[per_source : per_source + STAT_ROWS, :].astype(jnp.float32) for h in range(heads)]
        levels.append(jnp.concatenate([x[0:1] + x[1:2] + x[2:3] for x in stats], axis=0))
    top = functools.reduce(jnp.maximum, levels)
    weights = [jnp.exp2(level - top) for level in levels]
    total = functools.reduce(jnp.add, weights)
    weights = [jnp.transpose(w / total) for w in weights]
    for h in range(heads):
        mixed = functools.reduce(
            jnp.add,
            [
                w[:per_source, h : h + 1] * part(b, h)[:per_source, :].astype(jnp.float32)
                for b, w in enumerate(weights)
            ],
        ).astype(jnp.bfloat16)
        first = h * group_size if count == 1 else pl.multiple_of((own_ref[0] ^ h) * group_size, group_size)
        out_ref[0, :, pl.ds(first, group_size), :] = mixed.reshape(local_rows, group_size, dim)


def merge(own, parts, kv_heads, spread, request, requests, local_rows, group_size, earlier):
    dim = parts[0].shape[-1]
    rest = [] if earlier is None else [earlier]

    def whole(array):
        return pl.BlockSpec(array.shape, lambda i: (0,) * array.ndim)

    return pl.pallas_call(
        functools.partial(merge_kernel, count=len(parts), spread=spread, heads=kv_heads, group_size=group_size),
        grid=(1,),
        in_specs=[SMEM_SPEC] + [whole(x) for x in parts] + [pl.BlockSpec(memory_space=pl.ANY) for _ in rest],
        out_specs=pl.BlockSpec((1, local_rows, kv_heads * group_size, dim), lambda i: (request, 0, 0, 0)),
        out_shape=jax.ShapeDtypeStruct((requests, local_rows, kv_heads * group_size, dim), jnp.bfloat16),
        input_output_aliases={1 + len(parts): 0} if rest else {},
        compiler_params=pltpu.CompilerParams(vmem_limit_bytes=SMALL_VMEM),
    )(own, *parts, *rest)


def pack_kernel(own_ref, q_ref, fresh_ref, *out_refs):
    requests, local_rows, heads, dim = q_ref.shape
    kv_heads = fresh_ref.shape[0]
    group_size = heads // kv_heads
    rows = requests * local_rows * group_size
    for d, out_ref in enumerate(out_refs):
        head = own_ref[0] ^ d
        first = pl.multiple_of(head * group_size, group_size)
        out_ref[:rows, :] = q_ref[:, :, pl.ds(first, group_size), :].reshape(rows, dim)
        out_ref[rows:, :] = fresh_ref[head]


def pack(own, queries, fresh):
    requests, local_rows, heads, dim = queries.shape
    kv_heads = fresh.shape[0]
    rows = requests * local_rows * (heads // kv_heads) + fresh.shape[1]
    return pl.pallas_call(
        pack_kernel,
        in_specs=[SMEM_SPEC, VMEM_SPEC, VMEM_SPEC],
        out_specs=[VMEM_SPEC] * kv_heads,
        out_shape=[jax.ShapeDtypeStruct((rows, dim), jnp.bfloat16)] * kv_heads,
        compiler_params=pltpu.CompilerParams(vmem_limit_bytes=SMALL_VMEM),
    )(own, queries, fresh)


def split_kernel(own_ref, k_hbm, v_hbm, *refs, request):
    loaded, held, sems = refs[-3:]
    copies = [
        pltpu.make_async_copy(hbm.at[request], loaded.at[i], sems.at[i]) for i, hbm in enumerate((k_hbm, v_hbm))
    ]
    for copy in copies:
        copy.start()
    for i, copy in enumerate(copies):
        copy.wait()
        held[:, i] = jnp.swapaxes(loaded[i], 0, 1)
    for k, out_ref in enumerate(refs[:-3]):
        out_ref[...] = held[own_ref[0] ^ k]


def split_heads(own, cache_k, cache_v, request, grant):
    _, slots, kv_heads, dim = cache_k.shape
    return pl.pallas_call(
        functools.partial(split_kernel, request=request),
        in_specs=[SMEM_SPEC, HBM_SPEC, HBM_SPEC],
        out_specs=[VMEM_SPEC] * kv_heads,
        out_shape=[jax.ShapeDtypeStruct((2, slots, dim), jnp.bfloat16)] * kv_heads,
        scratch_shapes=[
            pltpu.VMEM((2, slots, kv_heads, dim), jnp.bfloat16),
            pltpu.VMEM((kv_heads, 2, slots, dim), jnp.bfloat16),
            pltpu.SemaphoreType.DMA((2,)),
        ],
        compiler_params=pltpu.CompilerParams(vmem_limit_bytes=grant),
    )(own, cache_k, cache_v)


def attention(queries, new_k, new_v, cache_k, cache_v, cache_len):
    requests, local_rows, heads, head_dim = queries.shape
    kv_heads = cache_k.shape[2]
    group_size = heads // kv_heads
    devices_seq = lax.axis_size("seq")
    seq_index = lax.axis_index("seq")
    spread = devices_seq // kv_heads
    block = seq_index // kv_heads
    own = (seq_index % kv_heads).astype(jnp.int32)
    per_source = local_rows * group_size

    devices = range(devices_seq)
    direct = spread <= 2
    fresh = jnp.transpose(jnp.stack([new_k, new_v]), (3, 0, 1, 2, 4)).reshape(
        kv_heads, 2 * requests * local_rows, head_dim
    )

    def to_partner(array, k):
        return lax.ppermute(array, "seq", [(i, i ^ k) for i in devices])

    if direct:
        packed = pack(own[None], queries, fresh)
        head_q = [packed[0]]
        for k in range(1, devices_seq):
            head_q.append(to_partner(packed[k % kv_heads], k))
        head_fresh = jnp.stack([x[requests * per_source :, :] for x in head_q])
    else:
        packed = jnp.stack(pack(jnp.zeros((1,), jnp.int32), queries, fresh))
        packed = jnp.broadcast_to(packed[None], (spread,) + packed.shape).reshape((devices_seq,) + packed.shape[1:])
        head_q = lax.all_to_all(packed, "seq", split_axis=0, concat_axis=0, tiled=True)
        head_fresh = head_q[:, requests * per_source :, :]
        head_q = [head_q]
    head_fresh = head_fresh.reshape(devices_seq, 2, requests, local_rows, head_dim)
    head_fresh = jnp.transpose(head_fresh, (1, 2, 0, 3, 4)).reshape(
        2, requests, devices_seq * local_rows, head_dim
    )

    kv_blocks = []
    for r in range(requests):
        parts = split_heads(own[None], cache_k, cache_v, r, LARGE_VMEM if r == 0 else 2 * SMALL_VMEM)
        moved = [parts[0]]
        for k in range(1, kv_heads):
            moved.append(to_partner(parts[k], k))
        kv_blocks.append(moved)

    place = jnp.stack([own, block, seq_index]).astype(jnp.int32)
    out = None
    for r in range(requests):
        rows = (devices_seq, r * per_source, per_source, group_size)
        parts = attend(
            cache_len[r : r + 1],
            place,
            head_q,
            kv_blocks[r],
            tuple(range(kv_heads)),
            (head_fresh[0, r], head_fresh[1, r]),
            None,
            True,
            1,
            *rows,
        )
        parts = [lax.all_to_all(parts[0], "seq", split_axis=0, concat_axis=0, tiled=True)]
        out = merge(own[None], parts, kv_heads, spread, r, requests, local_rows, group_size, out)
    return out


def solution(mesh):
    in_specs = (
        P("groups", "seq", None, None),
        P("groups", "seq", None, None),
        P("groups", "seq", None, None),
        P("groups", "seq", None, None),
        P("groups", "seq", None, None),
        P("groups"),
    )
    out_specs = P("groups", "seq", None, None)
    return jax.shard_map(attention, mesh=mesh, in_specs=in_specs, out_specs=out_specs, check_vma=False)
```

```python
import functools
import math

import jax
import jax.numpy as jnp
from jax import lax
from jax.experimental import pallas as pl
from jax.experimental.pallas import tpu as pltpu
from jax.sharding import PartitionSpec as P


NEG = -1e30
STAT_ROWS = 8
SMALL_VMEM = 12 * 2**20
LARGE_VMEM = 56 * 2**20


VMEM_SPEC = pl.BlockSpec(memory_space=pltpu.VMEM)
HBM_SPEC = pl.BlockSpec(memory_space=pltpu.HBM)
SMEM_SPEC = pl.BlockSpec(memory_space=pltpu.SMEM)


def attend_kernel(*refs, blocks, tile, group_size, row_start):
    length_ref, place_ref, q_hbm = refs[:3]
    kv_refs = refs[3 : 3 + blocks]
    (
        fk_ref,
        fv_ref,
        out_hbm,
        q_ref,
        out_ref,
        keys,
        loaded,
        vals,
        bias,
        s0,
        s1,
        m0,
        m1,
        in_sems,
        q_sem,
        out_sem,
    ) = refs[3 + blocks :]
    per_source, dim = q_ref.shape[1:]
    block_slots = kv_refs[0].shape[1]
    chunk = bias.shape[0]
    slots = blocks * block_slots
    fresh = fk_ref.shape[0]
    rows = q_ref.shape[0] * per_source
    tiles = rows // tile
    span = tile // per_source
    ones = vals.shape[0] - dim
    scale = math.log2(math.e) / math.sqrt(dim)
    own, device_block = place_ref[0], place_ref[1]
    valid = jnp.clip(length_ref[0] - device_block * slots, 0, slots)
    fresh_shift = jnp.where(device_block == q_ref.shape[0] // blocks - 1, 0, -rows)

    copies = []
    for k, kv_ref in enumerate(kv_refs):
        at = pl.ds(pl.multiple_of((own ^ k) * block_slots, block_slots), block_slots)
        copies.append(pltpu.make_async_copy(kv_ref.at[1], loaded.at[at, :], in_sems.at[k, 1]))
    for k, kv_ref in enumerate(kv_refs):
        at = pl.ds(pl.multiple_of((own ^ k) * block_slots, block_slots), block_slots)
        copies.append(pltpu.make_async_copy(kv_ref.at[0], keys.at[at, :], in_sems.at[k, 0]))
    copies.append(pltpu.make_async_copy(q_hbm.at[:, row_start : row_start + per_source, :], q_ref, q_sem))
    for copy in copies:
        copy.start()

    vals[dim:, :] = jnp.ones((ones, slots + fresh), jnp.bfloat16)
    vals[:dim, slots:] = jnp.transpose(fv_ref[...])
    left = (valid - 1) % chunk + 1
    bias[...] = jnp.where(lax.broadcasted_iota(jnp.int32, bias.shape, 0) < left, 0.0, NEG)
    for copy in copies[:blocks]:
        copy.wait()
    for first in range(0, slots, block_slots):
        vals[:dim, first : first + block_slots] = jnp.transpose(loaded[first : first + block_slots, :])
    for copy in copies[blocks:]:
        copy.wait()

    def fold_max(scores, best):
        part = jnp.max(scores.reshape(-1, 8, tile), axis=0)
        return part if best is None else jnp.maximum(best, part)

    def score_chunk(t, j, count, s_ref, best):
        q = q_ref[pl.ds(t * span, span)].reshape(tile, dim)
        at = slice(j * chunk, (j + 1) * chunk) if j < count else slice(slots, slots + fresh)
        left_side = keys[at, :] if j < count else fk_ref[...]
        scores = lax.dot_general(left_side, q, (((1,), (1,)), ((), ())), preferred_element_type=jnp.float32)
        if j == count - 1:
            mask = bias[...]
            scores = scores + jnp.concatenate([mask] * (tile // mask.shape[1]), axis=1)
        elif j == count:
            token = (t * tile + lax.broadcasted_iota(jnp.int32, (1, tile), 1)) // group_size
            unit = lax.broadcasted_iota(jnp.int32, (fresh, 1), 0)
            scores = jnp.where(unit <= token + fresh_shift, scores, NEG)
        s_ref[at, :] = scores
        return fold_max(scores, best)

    def value_chunk(j, count, s_ref, top, acc):
        at = slice(j * chunk, (j + 1) * chunk) if j < count else slice(slots, slots + fresh)
        weights = jnp.exp2((s_ref[at, :] - top) * scale).astype(jnp.bfloat16)
        part = jnp.dot(vals[:, at], weights, preferred_element_type=jnp.float32)
        return part if acc is None else acc + part

    def finish(t, top, acc):
        total = acc[dim : dim + 1, :]
        out = acc[:dim, :] / total
        level = top * scale + jnp.log2(total)
        high = level.astype(jnp.bfloat16).astype(jnp.float32)
        mid = (level - high).astype(jnp.bfloat16).astype(jnp.float32)
        low = level - high - mid
        which = lax.broadcasted_iota(jnp.int32, (STAT_ROWS, tile), 0)
        stats = jnp.where(which == 0, high, jnp.where(which == 1, mid, low)).astype(jnp.bfloat16)
        for first in range(0, tile, dim):
            flat = jnp.transpose(out[:, first : first + dim]).astype(jnp.bfloat16)
            width = min(per_source, dim)
            for part in range(dim // width):
                source = t * span + (first + part * width) // per_source
                inside = (first + part * width) % per_source
                out_ref[source, inside : inside + width, :] = flat[part * width : (part + 1) * width, :]
                out_ref[source, per_source:, inside : inside + width] = stats[
                    :, first + part * width : first + (part + 1) * width
                ]

    def stage(t_next, s_next, m_next, t_now, s_now, m_now, count):
        best = None
        acc = None
        if t_now is not None:
            top = jnp.max(m_now[...], axis=0, keepdims=True)
        for j in range(count + 1):
            if t_next is not None:
                best = score_chunk(t_next, j, count, s_next, best)
            if t_now is not None:
                acc = value_chunk(j, count, s_now, top, acc)
        if t_next is not None:
            m_next[...] = best
        if t_now is not None:
            finish(t_now, top, acc)

    for count in range(slots // chunk + 1):

        @pl.when((valid > (count - 1) * chunk) & (valid <= count * chunk))
        def _(count=count):
            stage(0, s0, m0, None, None, None, count)

            def pair(i, carry):
                stage(2 * i + 1, s1, m1, 2 * i, s0, m0, count)
                stage(jnp.minimum(2 * i + 2, tiles - 1), s0, m0, 2 * i + 1, s1, m1, count)
                return carry

            lax.fori_loop(0, tiles // 2, pair, 0)

    result = pltpu.make_async_copy(out_ref, out_hbm, out_sem)
    result.start()
    result.wait()


def attend(length, place, head_q, kv_blocks, fresh, row_start, row_count, group_size):
    sources, _, dim = head_q.shape
    slots = len(kv_blocks) * kv_blocks[0].shape[1]
    rows = sources * row_count
    units = fresh[0].shape[0]
    tile = min(256, rows // 2)
    chunk = min(1024, slots)
    grant = 8 * tile * (slots + units) + 8 * slots * dim + 8 * rows * dim + SMALL_VMEM
    return pl.pallas_call(
        functools.partial(
            attend_kernel, blocks=len(kv_blocks), tile=tile, group_size=group_size, row_start=row_start
        ),
        in_specs=[SMEM_SPEC] * 2 + [HBM_SPEC] * (1 + len(kv_blocks)) + [VMEM_SPEC] * 2,
        out_specs=HBM_SPEC,
        scratch_shapes=[
            pltpu.VMEM((sources, row_count, dim), jnp.bfloat16),
            pltpu.VMEM((sources, row_count + STAT_ROWS, dim), jnp.bfloat16),
            pltpu.VMEM((slots, dim), jnp.bfloat16),
            pltpu.VMEM((slots, dim), jnp.bfloat16),
            pltpu.VMEM((dim + 16, slots + units), jnp.bfloat16),
            pltpu.VMEM((chunk, min(dim, tile)), jnp.float32),
            pltpu.VMEM((slots + units, tile), jnp.float32),
            pltpu.VMEM((slots + units, tile), jnp.float32),
            pltpu.VMEM((8, tile), jnp.float32),
            pltpu.VMEM((8, tile), jnp.float32),
            pltpu.SemaphoreType.DMA((len(kv_blocks), 2)),
            pltpu.SemaphoreType.DMA,
            pltpu.SemaphoreType.DMA,
        ],
        out_shape=jax.ShapeDtypeStruct((sources, row_count + STAT_ROWS, dim), jnp.bfloat16),
        compiler_params=pltpu.CompilerParams(vmem_limit_bytes=grant),
        cost_estimate=pl.CostEstimate(
            flops=4 * rows * slots * dim,
            bytes_accessed=4 * slots * dim + 4 * rows * dim,
            transcendentals=rows * slots,
        ),
    )(length, place, head_q, *kv_blocks, *fresh)


def merge_kernel(part_ref, *refs, group_size):
    out_ref = refs[-1]
    spread, heads, _, dim = part_ref.shape
    local_rows = out_ref.shape[1]
    per_source = local_rows * group_size
    levels = []
    for b in range(spread):
        stats = [
            part_ref[b, h, per_source : per_source + STAT_ROWS, :].astype(jnp.float32) for h in range(heads)
        ]
        levels.append(jnp.concatenate([x[0:1] + x[1:2] + x[2:3] for x in stats], axis=0))
    top = functools.reduce(jnp.maximum, levels)
    weights = [jnp.exp2(level - top) for level in levels]
    total = functools.reduce(jnp.add, weights)
    weights = [jnp.transpose(w / total) for w in weights]
    for h in range(heads):
        mixed = functools.reduce(
            jnp.add,
            [
                w[:per_source, h : h + 1] * part_ref[b, h, :per_source, :].astype(jnp.float32)
                for b, w in enumerate(weights)
            ],
        ).astype(jnp.bfloat16)
        out_ref[0, :, h * group_size : (h + 1) * group_size, :] = mixed.reshape(local_rows, group_size, dim)


def merge(parts, request, requests, local_rows, group_size, earlier):
    heads, dim = parts.shape[1], parts.shape[3]
    rest = [] if earlier is None else [earlier]
    return pl.pallas_call(
        functools.partial(merge_kernel, group_size=group_size),
        grid=(1,),
        in_specs=[pl.BlockSpec(parts.shape, lambda i: (0, 0, 0, 0))]
        + [pl.BlockSpec(memory_space=pl.ANY) for _ in rest],
        out_specs=pl.BlockSpec((1, local_rows, heads * group_size, dim), lambda i: (request, 0, 0, 0)),
        out_shape=jax.ShapeDtypeStruct((requests, local_rows, heads * group_size, dim), jnp.bfloat16),
        input_output_aliases={1: 0} if rest else {},
        compiler_params=pltpu.CompilerParams(vmem_limit_bytes=SMALL_VMEM),
    )(parts, *rest)


def pack_kernel(q_ref, fresh_ref, out_ref):
    requests, local_rows, heads, dim = q_ref.shape
    kv_heads = fresh_ref.shape[0]
    group_size = heads // kv_heads
    rows = requests * local_rows * group_size
    for d in range(out_ref.shape[0]):
        head = d % kv_heads
        out_ref[d, :rows, :] = q_ref[:, :, head * group_size : (head + 1) * group_size, :].reshape(rows, dim)
        out_ref[d, rows:, :] = fresh_ref[head]


def pack(queries, fresh, devices):
    requests, local_rows, heads, dim = queries.shape
    rows = requests * local_rows * (heads // fresh.shape[0]) + fresh.shape[1]
    return pl.pallas_call(
        pack_kernel,
        in_specs=[VMEM_SPEC, VMEM_SPEC],
        out_specs=VMEM_SPEC,
        out_shape=jax.ShapeDtypeStruct((devices, rows, dim), jnp.bfloat16),
        compiler_params=pltpu.CompilerParams(vmem_limit_bytes=SMALL_VMEM),
    )(queries, fresh)


def split_kernel(own_ref, k_hbm, v_hbm, *refs, request):
    loaded, held, sems = refs[-3:]
    copies = [
        pltpu.make_async_copy(hbm.at[request], loaded.at[i], sems.at[i]) for i, hbm in enumerate((k_hbm, v_hbm))
    ]
    for copy in copies:
        copy.start()
    for i, copy in enumerate(copies):
        copy.wait()
        held[:, i] = jnp.swapaxes(loaded[i], 0, 1)
    for k, out_ref in enumerate(refs[:-3]):
        out_ref[...] = held[own_ref[0] ^ k]


def split_heads(own, cache_k, cache_v, request, grant):
    _, slots, kv_heads, dim = cache_k.shape
    return pl.pallas_call(
        functools.partial(split_kernel, request=request),
        in_specs=[SMEM_SPEC, HBM_SPEC, HBM_SPEC],
        out_specs=[VMEM_SPEC] * kv_heads,
        out_shape=[jax.ShapeDtypeStruct((2, slots, dim), jnp.bfloat16)] * kv_heads,
        scratch_shapes=[
            pltpu.VMEM((2, slots, kv_heads, dim), jnp.bfloat16),
            pltpu.VMEM((kv_heads, 2, slots, dim), jnp.bfloat16),
            pltpu.SemaphoreType.DMA((2,)),
        ],
        compiler_params=pltpu.CompilerParams(vmem_limit_bytes=grant),
    )(own, cache_k, cache_v)


def attention(queries, new_k, new_v, cache_k, cache_v, cache_len):
    requests, local_rows, heads, head_dim = queries.shape
    kv_heads = cache_k.shape[2]
    group_size = heads // kv_heads
    devices_seq = lax.axis_size("seq")
    seq_index = lax.axis_index("seq")
    spread = devices_seq // kv_heads
    block = seq_index // kv_heads
    own = (seq_index % kv_heads).astype(jnp.int32)
    per_source = local_rows * group_size

    fresh = jnp.transpose(jnp.stack([new_k, new_v]), (3, 0, 1, 2, 4)).reshape(
        kv_heads, 2 * requests * local_rows, head_dim
    )
    head_q = lax.all_to_all(
        pack(queries, fresh, devices_seq), "seq", split_axis=0, concat_axis=0, tiled=True
    )
    head_fresh = head_q[:, requests * per_source :, :].reshape(
        devices_seq, 2, requests, local_rows, head_dim
    )
    head_fresh = jnp.transpose(head_fresh, (1, 2, 0, 3, 4)).reshape(
        2, requests, devices_seq * local_rows, head_dim
    )

    kv_blocks = []
    for r in range(requests):
        parts = split_heads(own[None], cache_k, cache_v, r, LARGE_VMEM if r == 0 else 2 * SMALL_VMEM)
        moved = [parts[0]]
        for k in range(1, kv_heads):
            moved.append(lax.ppermute(parts[k], "seq", [(i, i ^ k) for i in range(devices_seq)]))
        kv_blocks.append(moved)

    place = jnp.stack([own, block]).astype(jnp.int32)
    out = None
    for r in range(requests):
        part = attend(
            cache_len[r : r + 1],
            place,
            head_q,
            kv_blocks[r],
            (head_fresh[0, r], head_fresh[1, r]),
            r * per_source,
            per_source,
            group_size,
        )
        part = lax.all_to_all(part, "seq", split_axis=0, concat_axis=0, tiled=True)
        part = part.reshape(spread, kv_heads, per_source + STAT_ROWS, head_dim)
        out = merge(part, r, requests, local_rows, group_size, out)
    return out


def solution(mesh):
    in_specs = (
        P("groups", "seq", None, None),
        P("groups", "seq", None, None),
        P("groups", "seq", None, None),
        P("groups", "seq", None, None),
        P("groups", "seq", None, None),
        P("groups"),
    )
    out_specs = P("groups", "seq", None, None)
    return jax.shard_map(attention, mesh=mesh, in_specs=in_specs, out_specs=out_specs, check_vma=False)
```

```python
import functools
import math

import jax
import jax.numpy as jnp
from jax import lax
from jax.experimental import pallas as pl
from jax.experimental.pallas import tpu as pltpu
from jax.sharding import PartitionSpec as P


NEG = -1e30
STAT_ROWS = 8
SMALL_VMEM = 12 * 2**20
LARGE_VMEM = 56 * 2**20


VMEM_SPEC = pl.BlockSpec(memory_space=pltpu.VMEM)
HBM_SPEC = pl.BlockSpec(memory_space=pltpu.HBM)
SMEM_SPEC = pl.BlockSpec(memory_space=pltpu.SMEM)


def attend_kernel(*refs, order, blocks, tile, group_size, row_start, with_fresh, with_state, final):
    refs = list(refs)
    length_ref, place_ref, q_hbm = refs.pop(0), refs.pop(0), refs.pop(0)
    kv_refs = [refs.pop(0) for _ in order]
    if with_fresh:
        fk_ref, fv_ref = refs.pop(0), refs.pop(0)
    if with_state:
        acc_in, top_in = refs.pop(0), refs.pop(0)
    if final:
        out_hbm = refs.pop(0)
        out_ref, out_sem = refs.pop(), refs.pop()
    else:
        acc_out, top_out = refs.pop(0), refs.pop(0)
    q_ref, keys, loaded, vals, bias, s0, s1, m0, m1, in_sems, q_sem = refs
    per_source, dim = q_ref.shape[1:]
    block_slots = kv_refs[0].shape[1]
    chunk = bias.shape[0]
    slots = len(order) * block_slots
    chunks = slots // chunk
    fresh = fk_ref.shape[0] if with_fresh else 0
    rows = q_ref.shape[0] * per_source
    tiles = rows // tile
    span = tile // per_source
    ones = vals.shape[0] - dim
    scale = math.log2(math.e) / math.sqrt(dim)
    own, device_block = place_ref[0], place_ref[1]
    valid = jnp.clip(length_ref[0] - device_block * blocks * block_slots, 0, blocks * block_slots)
    fresh_shift = jnp.where(device_block == q_ref.shape[0] // blocks - 1, 0, -rows)

    held = sorted({k // 2 for k in order})
    absent = [c for c in range(blocks // 2) if c not in held]

    def rank_of(index):
        rank = index
        for c in absent:
            rank = rank - jnp.where((own // 2) ^ c < index, 1, 0)
        return rank

    value_copies = []
    copies = []
    for i, k in enumerate(order):
        first = rank_of((own // 2) ^ (k // 2)) * chunk + ((own % 2) ^ (k % 2)) * block_slots
        at = pl.ds(pl.multiple_of(first, block_slots), block_slots)
        value_copies.append(pltpu.make_async_copy(kv_refs[i].at[1], loaded.at[at, :], in_sems.at[i, 1]))
        copies.append(pltpu.make_async_copy(kv_refs[i].at[0], keys.at[at, :], in_sems.at[i, 0]))
    copies.append(pltpu.make_async_copy(q_hbm.at[:, row_start : row_start + per_source, :], q_ref, q_sem))
    for copy in value_copies + copies:
        copy.start()

    filled = jnp.int32(0)
    last_valid = jnp.int32(0)
    for c in held:
        left = valid - ((own // 2) ^ c) * chunk
        filled = filled + jnp.where(left > 0, 1, 0)
        last_valid = jnp.where((left > 0) & (left < chunk), left, last_valid)
    last_valid = jnp.where(last_valid == 0, chunk, last_valid)

    vals[dim:, :] = jnp.ones((ones, slots + fresh), jnp.bfloat16)
    if with_fresh:
        vals[:dim, slots:] = jnp.transpose(fv_ref[...])
    bias[...] = jnp.where(lax.broadcasted_iota(jnp.int32, bias.shape, 0) < last_valid, 0.0, NEG)
    for copy in value_copies:
        copy.wait()
    for first in range(0, slots, block_slots):
        vals[:dim, first : first + block_slots] = jnp.transpose(loaded[first : first + block_slots, :])
    for copy in copies:
        copy.wait()

    def fold_max(scores, best):
        part = jnp.max(scores.reshape(-1, 8, tile), axis=0)
        return part if best is None else jnp.maximum(best, part)

    def score_chunk(t, j, count, s_ref, best):
        q = q_ref[pl.ds(t * span, span)].reshape(tile, dim)
        at = slice(j * chunk, (j + 1) * chunk) if j < count else slice(slots, slots + fresh)
        left_side = keys[at, :] if j < count else fk_ref[...]
        scores = lax.dot_general(left_side, q, (((1,), (1,)), ((), ())), preferred_element_type=jnp.float32)
        if j == count - 1:
            mask = bias[...]
            scores = scores + jnp.concatenate([mask] * (tile // mask.shape[1]), axis=1)
        elif j == count:
            token = (t * tile + lax.broadcasted_iota(jnp.int32, (1, tile), 1)) // group_size
            unit = lax.broadcasted_iota(jnp.int32, (fresh, 1), 0)
            scores = jnp.where(unit <= token + fresh_shift, scores, NEG)
        s_ref[at, :] = scores
        return fold_max(scores, best)

    def value_chunk(j, count, s_ref, top, acc):
        at = slice(j * chunk, (j + 1) * chunk) if j < count else slice(slots, slots + fresh)
        weights = jnp.exp2((s_ref[at, :] - top) * scale).astype(jnp.bfloat16)
        part = jnp.dot(vals[:, at], weights, preferred_element_type=jnp.float32)
        return part if acc is None else acc + part

    def finish(t, top, acc):
        total = acc[dim : dim + 1, :]
        out = acc[:dim, :] / total
        level = top * scale + jnp.log2(total)
        high = level.astype(jnp.bfloat16).astype(jnp.float32)
        mid = (level - high).astype(jnp.bfloat16).astype(jnp.float32)
        low = level - high - mid
        which = lax.broadcasted_iota(jnp.int32, (STAT_ROWS, tile), 0)
        stats = jnp.where(which == 0, high, jnp.where(which == 1, mid, low)).astype(jnp.bfloat16)
        for first in range(0, tile, dim):
            flat = jnp.transpose(out[:, first : first + dim]).astype(jnp.bfloat16)
            width = min(per_source, dim)
            for part in range(dim // width):
                source = t * span + (first + part * width) // per_source
                inside = (first + part * width) % per_source
                out_ref[source, inside : inside + width, :] = flat[part * width : (part + 1) * width, :]
                out_ref[source, per_source:, inside : inside + width] = stats[
                    :, first + part * width : first + (part + 1) * width
                ]

    def stage(t_next, s_next, m_next, t_now, s_now, m_now, count):
        pieces = count + (1 if with_fresh else 0)
        best = None
        acc = None
        if t_now is not None:
            at = pl.ds(pl.multiple_of(t_now * tile, tile), tile)
            top = jnp.max(m_now[...], axis=0, keepdims=True) if pieces else None
            if with_state:
                before = top_in[:, at][:1]
                top = before if top is None else jnp.maximum(top, before)
                acc = acc_in[:, at] * jnp.exp2((before - top) * scale)
        for j in range(pieces):
            if t_next is not None:
                best = score_chunk(t_next, j, count, s_next, best)
            if t_now is not None:
                acc = value_chunk(j, count, s_now, top, acc)
        if t_next is not None and pieces:
            m_next[...] = best
        if t_now is not None:
            if final:
                finish(t_now, top, acc)
            else:
                acc_out[:, at] = acc
                top_out[:, at] = jnp.broadcast_to(top, (8, tile))

    for count in range(chunks + 1):

        @pl.when(filled == count)
        def _(count=count):
            stage(0, s0, m0, None, None, None, count)

            def pair(i, carry):
                stage(2 * i + 1, s1, m1, 2 * i, s0, m0, count)
                stage(jnp.minimum(2 * i + 2, tiles - 1), s0, m0, 2 * i + 1, s1, m1, count)
                return carry

            lax.fori_loop(0, tiles // 2, pair, 0)

    if final:
        result = pltpu.make_async_copy(out_ref, out_hbm, out_sem)
        result.start()
        result.wait()


def attend(length, place, head_q, kv_blocks, order, fresh, state, final, row_start, row_count, group_size):
    sources, _, dim = head_q.shape
    slots = len(order) * kv_blocks[0].shape[1]
    rows = sources * row_count
    units = 0 if fresh is None else fresh[0].shape[0]
    tile = min(256, rows // 2)
    chunk = 2 * kv_blocks[0].shape[1]
    depth = dim + 16
    operands = [length, place, head_q] + [kv_blocks[k] for k in order]
    in_specs = [SMEM_SPEC] * 2 + [HBM_SPEC] * (1 + len(order))
    scratch = [
        pltpu.VMEM((sources, row_count, dim), jnp.bfloat16),
        pltpu.VMEM((slots, dim), jnp.bfloat16),
        pltpu.VMEM((slots, dim), jnp.bfloat16),
        pltpu.VMEM((depth, slots + units), jnp.bfloat16),
        pltpu.VMEM((chunk, min(dim, tile)), jnp.float32),
        pltpu.VMEM((slots + units, tile), jnp.float32),
        pltpu.VMEM((slots + units, tile), jnp.float32),
        pltpu.VMEM((8, tile), jnp.float32),
        pltpu.VMEM((8, tile), jnp.float32),
        pltpu.SemaphoreType.DMA((len(order), 2)),
        pltpu.SemaphoreType.DMA,
    ]
    if fresh is not None:
        operands += list(fresh)
        in_specs += [VMEM_SPEC] * 2
    if state is not None:
        operands += list(state)
        in_specs += [VMEM_SPEC] * 2
    if final:
        out_shape = jax.ShapeDtypeStruct((sources, row_count + STAT_ROWS, dim), jnp.bfloat16)
        out_specs = HBM_SPEC
        scratch += [pltpu.SemaphoreType.DMA, pltpu.VMEM(out_shape.shape, jnp.bfloat16)]
    else:
        out_shape = [
            jax.ShapeDtypeStruct((depth, rows), jnp.float32),
            jax.ShapeDtypeStruct((8, rows), jnp.float32),
        ]
        out_specs = [VMEM_SPEC] * 2
    grant = 8 * tile * (slots + units) + 8 * slots * dim + 12 * rows * dim + SMALL_VMEM
    return pl.pallas_call(
        functools.partial(
            attend_kernel,
            order=order,
            blocks=len(kv_blocks),
            tile=tile,
            group_size=group_size,
            row_start=row_start,
            with_fresh=fresh is not None,
            with_state=state is not None,
            final=final,
        ),
        in_specs=in_specs,
        out_specs=out_specs,
        scratch_shapes=scratch,
        out_shape=out_shape,
        compiler_params=pltpu.CompilerParams(vmem_limit_bytes=grant),
        cost_estimate=pl.CostEstimate(
            flops=4 * rows * slots * dim,
            bytes_accessed=4 * slots * dim + 4 * rows * dim,
            transcendentals=rows * slots,
        ),
    )(*operands)


def merge_kernel(part_ref, *refs, group_size):
    out_ref = refs[-1]
    spread, heads, _, dim = part_ref.shape
    local_rows = out_ref.shape[1]
    per_source = local_rows * group_size
    levels = []
    for b in range(spread):
        stats = [
            part_ref[b, h, per_source : per_source + STAT_ROWS, :].astype(jnp.float32) for h in range(heads)
        ]
        levels.append(jnp.concatenate([x[0:1] + x[1:2] + x[2:3] for x in stats], axis=0))
    top = functools.reduce(jnp.maximum, levels)
    weights = [jnp.exp2(level - top) for level in levels]
    total = functools.reduce(jnp.add, weights)
    weights = [jnp.transpose(w / total) for w in weights]
    for h in range(heads):
        mixed = functools.reduce(
            jnp.add,
            [
                w[:per_source, h : h + 1] * part_ref[b, h, :per_source, :].astype(jnp.float32)
                for b, w in enumerate(weights)
            ],
        ).astype(jnp.bfloat16)
        out_ref[0, :, h * group_size : (h + 1) * group_size, :] = mixed.reshape(local_rows, group_size, dim)


def merge(parts, request, requests, local_rows, group_size, earlier):
    heads, dim = parts.shape[1], parts.shape[3]
    rest = [] if earlier is None else [earlier]
    return pl.pallas_call(
        functools.partial(merge_kernel, group_size=group_size),
        grid=(1,),
        in_specs=[pl.BlockSpec(parts.shape, lambda i: (0, 0, 0, 0))]
        + [pl.BlockSpec(memory_space=pl.ANY) for _ in rest],
        out_specs=pl.BlockSpec((1, local_rows, heads * group_size, dim), lambda i: (request, 0, 0, 0)),
        out_shape=jax.ShapeDtypeStruct((requests, local_rows, heads * group_size, dim), jnp.bfloat16),
        input_output_aliases={1: 0} if rest else {},
        compiler_params=pltpu.CompilerParams(vmem_limit_bytes=SMALL_VMEM),
    )(parts, *rest)


def pack_kernel(q_ref, fresh_ref, out_ref):
    requests, local_rows, heads, dim = q_ref.shape
    kv_heads = fresh_ref.shape[0]
    group_size = heads // kv_heads
    rows = requests * local_rows * group_size
    for d in range(out_ref.shape[0]):
        head = d % kv_heads
        out_ref[d, :rows, :] = q_ref[:, :, head * group_size : (head + 1) * group_size, :].reshape(rows, dim)
        out_ref[d, rows:, :] = fresh_ref[head]


def pack(queries, fresh, devices):
    requests, local_rows, heads, dim = queries.shape
    rows = requests * local_rows * (heads // fresh.shape[0]) + fresh.shape[1]
    return pl.pallas_call(
        pack_kernel,
        in_specs=[VMEM_SPEC, VMEM_SPEC],
        out_specs=VMEM_SPEC,
        out_shape=jax.ShapeDtypeStruct((devices, rows, dim), jnp.bfloat16),
        compiler_params=pltpu.CompilerParams(vmem_limit_bytes=SMALL_VMEM),
    )(queries, fresh)


def split_kernel(own_ref, k_hbm, v_hbm, *refs, request):
    loaded, held, sems = refs[-3:]
    copies = [
        pltpu.make_async_copy(hbm.at[request], loaded.at[i], sems.at[i]) for i, hbm in enumerate((k_hbm, v_hbm))
    ]
    for copy in copies:
        copy.start()
    for i, copy in enumerate(copies):
        copy.wait()
        held[:, i] = jnp.swapaxes(loaded[i], 0, 1)
    for k, out_ref in enumerate(refs[:-3]):
        out_ref[...] = held[own_ref[0] ^ k]


def split_heads(own, cache_k, cache_v, request, grant):
    _, slots, kv_heads, dim = cache_k.shape
    return pl.pallas_call(
        functools.partial(split_kernel, request=request),
        in_specs=[SMEM_SPEC, HBM_SPEC, HBM_SPEC],
        out_specs=[VMEM_SPEC] * kv_heads,
        out_shape=[jax.ShapeDtypeStruct((2, slots, dim), jnp.bfloat16)] * kv_heads,
        scratch_shapes=[
            pltpu.VMEM((2, slots, kv_heads, dim), jnp.bfloat16),
            pltpu.VMEM((kv_heads, 2, slots, dim), jnp.bfloat16),
            pltpu.SemaphoreType.DMA((2,)),
        ],
        compiler_params=pltpu.CompilerParams(vmem_limit_bytes=grant),
    )(own, cache_k, cache_v)


def attention(queries, new_k, new_v, cache_k, cache_v, cache_len):
    requests, local_rows, heads, head_dim = queries.shape
    kv_heads = cache_k.shape[2]
    group_size = heads // kv_heads
    devices_seq = lax.axis_size("seq")
    seq_index = lax.axis_index("seq")
    spread = devices_seq // kv_heads
    block = seq_index // kv_heads
    own = (seq_index % kv_heads).astype(jnp.int32)
    per_source = local_rows * group_size

    fresh = jnp.transpose(jnp.stack([new_k, new_v]), (3, 0, 1, 2, 4)).reshape(
        kv_heads, 2 * requests * local_rows, head_dim
    )
    head_q = lax.all_to_all(
        pack(queries, fresh, devices_seq), "seq", split_axis=0, concat_axis=0, tiled=True
    )
    head_fresh = head_q[:, requests * per_source :, :].reshape(
        devices_seq, 2, requests, local_rows, head_dim
    )
    head_fresh = jnp.transpose(head_fresh, (1, 2, 0, 3, 4)).reshape(
        2, requests, devices_seq * local_rows, head_dim
    )

    kv_blocks = []
    for r in range(requests):
        parts = split_heads(own[None], cache_k, cache_v, r, LARGE_VMEM if r == 0 else 2 * SMALL_VMEM)
        moved = [parts[0]]
        for k in range(1, kv_heads):
            moved.append(lax.ppermute(parts[k], "seq", [(i, i ^ k) for i in range(devices_seq)]))
        kv_blocks.append(moved)

    early = kv_heads - 2
    place = jnp.stack([own, block]).astype(jnp.int32)
    out = None
    for r in range(requests):
        rows = (r * per_source, per_source, group_size)
        common = (cache_len[r : r + 1], place, head_q, kv_blocks[r])
        state = attend(*common, tuple(range(early)), (head_fresh[0, r], head_fresh[1, r]), None, False, *rows)
        part = attend(*common, tuple(range(early, kv_heads)), None, state, True, *rows)
        part = lax.all_to_all(part, "seq", split_axis=0, concat_axis=0, tiled=True)
        part = part.reshape(spread, kv_heads, per_source + STAT_ROWS, head_dim)
        out = merge(part, r, requests, local_rows, group_size, out)
    return out


def solution(mesh):
    in_specs = (
        P("groups", "seq", None, None),
        P("groups", "seq", None, None),
        P("groups", "seq", None, None),
        P("groups", "seq", None, None),
        P("groups", "seq", None, None),
        P("groups"),
    )
    out_specs = P("groups", "seq", None, None)
    return jax.shard_map(attention, mesh=mesh, in_specs=in_specs, out_specs=out_specs, check_vma=False)
```

```python
import functools
import math

import jax
import jax.numpy as jnp
from jax import lax
from jax.experimental import pallas as pl
from jax.experimental.pallas import tpu as pltpu
from jax.sharding import PartitionSpec as P


NEG = -1e30
STAT_ROWS = 8
SMALL_VMEM = 12 * 2**20
LARGE_VMEM = 56 * 2**20


VMEM_SPEC = pl.BlockSpec(memory_space=pltpu.VMEM)
HBM_SPEC = pl.BlockSpec(memory_space=pltpu.HBM)
SMEM_SPEC = pl.BlockSpec(memory_space=pltpu.SMEM)


def attend_kernel(*refs, order, blocks, tile, group_size, row_start, with_fresh, with_state, final):
    refs = list(refs)
    length_ref, place_ref, q_hbm = refs.pop(0), refs.pop(0), refs.pop(0)
    kv_refs = [refs.pop(0) for _ in order]
    if with_fresh:
        fk_ref, fv_ref = refs.pop(0), refs.pop(0)
    if with_state:
        acc_in, top_in = refs.pop(0), refs.pop(0)
    if final:
        out_hbm = refs.pop(0)
        out_ref, out_sem = refs.pop(), refs.pop()
    else:
        acc_out, top_out = refs.pop(0), refs.pop(0)
    q_ref, keys, loaded, vals, bias, s0, s1, m0, m1, in_sems, q_sem = refs
    per_source, dim = q_ref.shape[1:]
    block_slots = kv_refs[0].shape[1]
    chunk = bias.shape[0]
    slots = len(order) * block_slots
    chunks = slots // chunk
    fresh = fk_ref.shape[0] if with_fresh else 0
    rows = q_ref.shape[0] * per_source
    tiles = rows // tile
    span = tile // per_source
    ones = vals.shape[0] - dim
    scale = math.log2(math.e) / math.sqrt(dim)
    own, device_block = place_ref[0], place_ref[1]
    valid = jnp.clip(length_ref[0] - device_block * blocks * block_slots, 0, blocks * block_slots)
    fresh_shift = jnp.where(device_block == q_ref.shape[0] // blocks - 1, 0, -rows)

    held = sorted({k // 2 for k in order})
    absent = [c for c in range(blocks // 2) if c not in held]

    def rank_of(index):
        rank = index
        for c in absent:
            rank = rank - jnp.where((own // 2) ^ c < index, 1, 0)
        return rank

    value_copies = []
    copies = []
    for i, k in enumerate(order):
        first = rank_of((own // 2) ^ (k // 2)) * chunk + ((own % 2) ^ (k % 2)) * block_slots
        at = pl.ds(pl.multiple_of(first, block_slots), block_slots)
        value_copies.append(pltpu.make_async_copy(kv_refs[i].at[1], loaded.at[at, :], in_sems.at[i, 1]))
        copies.append(pltpu.make_async_copy(kv_refs[i].at[0], keys.at[at, :], in_sems.at[i, 0]))
    copies.append(pltpu.make_async_copy(q_hbm.at[:, row_start : row_start + per_source, :], q_ref, q_sem))
    for copy in value_copies + copies:
        copy.start()

    filled = jnp.int32(0)
    last_valid = jnp.int32(0)
    for c in held:
        left = valid - ((own // 2) ^ c) * chunk
        filled = filled + jnp.where(left > 0, 1, 0)
        last_valid = jnp.where((left > 0) & (left < chunk), left, last_valid)
    last_valid = jnp.where(last_valid == 0, chunk, last_valid)

    vals[dim:, :] = jnp.ones((ones, slots + fresh), jnp.bfloat16)
    if with_fresh:
        vals[:dim, slots:] = jnp.transpose(fv_ref[...])
    bias[...] = jnp.where(lax.broadcasted_iota(jnp.int32, bias.shape, 0) < last_valid, 0.0, NEG)
    for copy in copies + value_copies:
        copy.wait()

    def turn_values(count):
        for first in range(0, count * chunk, block_slots):
            vals[:dim, first : first + block_slots] = jnp.transpose(loaded[first : first + block_slots, :])

    def fold_max(scores, best):
        part = jnp.max(scores.reshape(-1, 8, tile), axis=0)
        return part if best is None else jnp.maximum(best, part)

    def score_chunk(t, j, count, s_ref, best):
        q = q_ref[pl.ds(t * span, span)].reshape(tile, dim)
        at = slice(j * chunk, (j + 1) * chunk) if j < count else slice(slots, slots + fresh)
        left_side = keys[at, :] if j < count else fk_ref[...]
        scores = lax.dot_general(left_side, q, (((1,), (1,)), ((), ())), preferred_element_type=jnp.float32)
        if j == count - 1:
            mask = bias[...]
            scores = scores + jnp.concatenate([mask] * (tile // mask.shape[1]), axis=1)
        elif j == count:
            token = (t * tile + lax.broadcasted_iota(jnp.int32, (1, tile), 1)) // group_size
            unit = lax.broadcasted_iota(jnp.int32, (fresh, 1), 0)
            scores = jnp.where(unit <= token + fresh_shift, scores, NEG)
        s_ref[at, :] = scores
        return fold_max(scores, best)

    def value_chunk(j, count, s_ref, top, acc):
        at = slice(j * chunk, (j + 1) * chunk) if j < count else slice(slots, slots + fresh)
        weights = jnp.exp2((s_ref[at, :] - top) * scale).astype(jnp.bfloat16)
        part = jnp.dot(vals[:, at], weights, preferred_element_type=jnp.float32)
        return part if acc is None else acc + part

    def finish(t, top, acc):
        total = acc[dim : dim + 1, :]
        out = (acc[:dim, :] * (1.0 / total)).astype(jnp.bfloat16)
        level = top * scale + jnp.log2(total)
        high = level.astype(jnp.bfloat16).astype(jnp.float32)
        mid = (level - high).astype(jnp.bfloat16).astype(jnp.float32)
        low = level - high - mid
        which = lax.broadcasted_iota(jnp.int32, (STAT_ROWS, tile), 0)
        stats = jnp.where(which == 0, high, jnp.where(which == 1, mid, low)).astype(jnp.bfloat16)
        for first in range(0, tile, dim):
            flat = jnp.transpose(out[:, first : first + dim])
            width = min(per_source, dim)
            for part in range(dim // width):
                source = t * span + (first + part * width) // per_source
                inside = (first + part * width) % per_source
                out_ref[source, inside : inside + width, :] = flat[part * width : (part + 1) * width, :]
                out_ref[source, per_source:, inside : inside + width] = stats[
                    :, first + part * width : first + (part + 1) * width
                ]

    def stage(t_next, s_next, m_next, t_now, s_now, m_now, count):
        pieces = count + (1 if with_fresh else 0)
        best = None
        acc = None
        if t_now is not None:
            at = pl.ds(pl.multiple_of(t_now * tile, tile), tile)
            top = jnp.max(m_now[...], axis=0, keepdims=True) if pieces else None
            if with_state:
                before = top_in[:, at][:1]
                top = before if top is None else jnp.maximum(top, before)
                acc = acc_in[:, at] * jnp.exp2((before - top) * scale)
        for j in range(pieces):
            if t_next is not None:
                best = score_chunk(t_next, j, count, s_next, best)
            if t_now is not None:
                acc = value_chunk(j, count, s_now, top, acc)
        if t_next is not None and pieces:
            m_next[...] = best
        if t_now is not None:
            if final:
                finish(t_now, top, acc)
            else:
                acc_out[:, at] = acc
                top_out[:, at] = jnp.broadcast_to(top, (8, tile))

    for count in range(chunks + 1):

        @pl.when(filled == count)
        def _(count=count):
            stage(0, s0, m0, None, None, None, count)
            turn_values(count)

            def pair(i, carry):
                stage(2 * i + 1, s1, m1, 2 * i, s0, m0, count)
                stage(jnp.minimum(2 * i + 2, tiles - 1), s0, m0, 2 * i + 1, s1, m1, count)
                return carry

            lax.fori_loop(0, tiles // 2, pair, 0)

    if final:
        result = pltpu.make_async_copy(out_ref, out_hbm, out_sem)
        result.start()
        result.wait()


def attend(length, place, head_q, kv_blocks, order, fresh, state, final, row_start, row_count, group_size):
    sources, _, dim = head_q.shape
    slots = len(order) * kv_blocks[0].shape[1]
    rows = sources * row_count
    units = 0 if fresh is None else fresh[0].shape[0]
    tile = min(256, rows // 2)
    chunk = 2 * kv_blocks[0].shape[1]
    depth = dim + 16
    operands = [length, place, head_q] + [kv_blocks[k] for k in order]
    in_specs = [SMEM_SPEC] * 2 + [HBM_SPEC] * (1 + len(order))
    scratch = [
        pltpu.VMEM((sources, row_count, dim), jnp.bfloat16),
        pltpu.VMEM((slots, dim), jnp.bfloat16),
        pltpu.VMEM((slots, dim), jnp.bfloat16),
        pltpu.VMEM((depth, slots + units), jnp.bfloat16),
        pltpu.VMEM((chunk, min(dim, tile)), jnp.float32),
        pltpu.VMEM((slots + units, tile), jnp.float32),
        pltpu.VMEM((slots + units, tile), jnp.float32),
        pltpu.VMEM((8, tile), jnp.float32),
        pltpu.VMEM((8, tile), jnp.float32),
        pltpu.SemaphoreType.DMA((len(order), 2)),
        pltpu.SemaphoreType.DMA,
    ]
    if fresh is not None:
        operands += list(fresh)
        in_specs += [VMEM_SPEC] * 2
    if state is not None:
        operands += list(state)
        in_specs += [VMEM_SPEC] * 2
    if final:
        out_shape = jax.ShapeDtypeStruct((sources, row_count + STAT_ROWS, dim), jnp.bfloat16)
        out_specs = HBM_SPEC
        scratch += [pltpu.SemaphoreType.DMA, pltpu.VMEM(out_shape.shape, jnp.bfloat16)]
    else:
        out_shape = [
            jax.ShapeDtypeStruct((depth, rows), jnp.float32),
            jax.ShapeDtypeStruct((8, rows), jnp.float32),
        ]
        out_specs = [VMEM_SPEC] * 2
    grant = 8 * tile * (slots + units) + 8 * slots * dim + 12 * rows * dim + SMALL_VMEM
    return pl.pallas_call(
        functools.partial(
            attend_kernel,
            order=order,
            blocks=len(kv_blocks),
            tile=tile,
            group_size=group_size,
            row_start=row_start,
            with_fresh=fresh is not None,
            with_state=state is not None,
            final=final,
        ),
        in_specs=in_specs,
        out_specs=out_specs,
        scratch_shapes=scratch,
        out_shape=out_shape,
        compiler_params=pltpu.CompilerParams(vmem_limit_bytes=grant),
        cost_estimate=pl.CostEstimate(
            flops=4 * rows * slots * dim,
            bytes_accessed=4 * slots * dim + 4 * rows * dim,
            transcendentals=rows * slots,
        ),
    )(*operands)


def merge_kernel(part_ref, *refs, group_size):
    out_ref = refs[-1]
    spread, heads, _, dim = part_ref.shape
    local_rows = out_ref.shape[1]
    per_source = local_rows * group_size
    levels = []
    for b in range(spread):
        stats = [
            part_ref[b, h, per_source : per_source + STAT_ROWS, :].astype(jnp.float32) for h in range(heads)
        ]
        levels.append(jnp.concatenate([x[0:1] + x[1:2] + x[2:3] for x in stats], axis=0))
    top = functools.reduce(jnp.maximum, levels)
    weights = [jnp.exp2(level - top) for level in levels]
    total = functools.reduce(jnp.add, weights)
    weights = [jnp.transpose(w / total) for w in weights]
    for h in range(heads):
        mixed = functools.reduce(
            jnp.add,
            [
                w[:per_source, h : h + 1] * part_ref[b, h, :per_source, :].astype(jnp.float32)
                for b, w in enumerate(weights)
            ],
        ).astype(jnp.bfloat16)
        out_ref[0, :, h * group_size : (h + 1) * group_size, :] = mixed.reshape(local_rows, group_size, dim)


def merge(parts, request, requests, local_rows, group_size, earlier):
    heads, dim = parts.shape[1], parts.shape[3]
    rest = [] if earlier is None else [earlier]
    return pl.pallas_call(
        functools.partial(merge_kernel, group_size=group_size),
        grid=(1,),
        in_specs=[pl.BlockSpec(parts.shape, lambda i: (0, 0, 0, 0))]
        + [pl.BlockSpec(memory_space=pl.ANY) for _ in rest],
        out_specs=pl.BlockSpec((1, local_rows, heads * group_size, dim), lambda i: (request, 0, 0, 0)),
        out_shape=jax.ShapeDtypeStruct((requests, local_rows, heads * group_size, dim), jnp.bfloat16),
        input_output_aliases={1: 0} if rest else {},
        compiler_params=pltpu.CompilerParams(vmem_limit_bytes=SMALL_VMEM),
    )(parts, *rest)


def pack_kernel(q_ref, fresh_ref, out_ref):
    requests, local_rows, heads, dim = q_ref.shape
    kv_heads = fresh_ref.shape[0]
    group_size = heads // kv_heads
    rows = requests * local_rows * group_size
    for d in range(out_ref.shape[0]):
        head = d % kv_heads
        out_ref[d, :rows, :] = q_ref[:, :, head * group_size : (head + 1) * group_size, :].reshape(rows, dim)
        out_ref[d, rows:, :] = fresh_ref[head]


def pack(queries, fresh, devices):
    requests, local_rows, heads, dim = queries.shape
    rows = requests * local_rows * (heads // fresh.shape[0]) + fresh.shape[1]
    return pl.pallas_call(
        pack_kernel,
        in_specs=[VMEM_SPEC, VMEM_SPEC],
        out_specs=VMEM_SPEC,
        out_shape=jax.ShapeDtypeStruct((devices, rows, dim), jnp.bfloat16),
        compiler_params=pltpu.CompilerParams(vmem_limit_bytes=SMALL_VMEM),
    )(queries, fresh)


def split_kernel(own_ref, k_hbm, v_hbm, *refs, request):
    loaded, held, sems = refs[-3:]
    copies = [
        pltpu.make_async_copy(hbm.at[request], loaded.at[i], sems.at[i]) for i, hbm in enumerate((k_hbm, v_hbm))
    ]
    for copy in copies:
        copy.start()
    for i, copy in enumerate(copies):
        copy.wait()
        held[:, i] = jnp.swapaxes(loaded[i], 0, 1)
    for k, out_ref in enumerate(refs[:-3]):
        out_ref[...] = held[own_ref[0] ^ k]


def split_heads(own, cache_k, cache_v, request, grant):
    _, slots, kv_heads, dim = cache_k.shape
    return pl.pallas_call(
        functools.partial(split_kernel, request=request),
        in_specs=[SMEM_SPEC, HBM_SPEC, HBM_SPEC],
        out_specs=[VMEM_SPEC] * kv_heads,
        out_shape=[jax.ShapeDtypeStruct((2, slots, dim), jnp.bfloat16)] * kv_heads,
        scratch_shapes=[
            pltpu.VMEM((2, slots, kv_heads, dim), jnp.bfloat16),
            pltpu.VMEM((kv_heads, 2, slots, dim), jnp.bfloat16),
            pltpu.SemaphoreType.DMA((2,)),
        ],
        compiler_params=pltpu.CompilerParams(vmem_limit_bytes=grant),
    )(own, cache_k, cache_v)


def attention(queries, new_k, new_v, cache_k, cache_v, cache_len):
    requests, local_rows, heads, head_dim = queries.shape
    kv_heads = cache_k.shape[2]
    group_size = heads // kv_heads
    devices_seq = lax.axis_size("seq")
    seq_index = lax.axis_index("seq")
    spread = devices_seq // kv_heads
    block = seq_index // kv_heads
    own = (seq_index % kv_heads).astype(jnp.int32)
    per_source = local_rows * group_size

    fresh = jnp.transpose(jnp.stack([new_k, new_v]), (3, 0, 1, 2, 4)).reshape(
        kv_heads, 2 * requests * local_rows, head_dim
    )
    head_q = lax.all_to_all(
        pack(queries, fresh, devices_seq), "seq", split_axis=0, concat_axis=0, tiled=True
    )
    head_fresh = head_q[:, requests * per_source :, :].reshape(
        devices_seq, 2, requests, local_rows, head_dim
    )
    head_fresh = jnp.transpose(head_fresh, (1, 2, 0, 3, 4)).reshape(
        2, requests, devices_seq * local_rows, head_dim
    )

    kv_blocks = []
    for r in range(requests):
        parts = split_heads(own[None], cache_k, cache_v, r, LARGE_VMEM if r == 0 else 2 * SMALL_VMEM)
        moved = [parts[0]]
        for k in range(1, kv_heads):
            moved.append(lax.ppermute(parts[k], "seq", [(i, i ^ k) for i in range(devices_seq)]))
        kv_blocks.append(moved)

    place = jnp.stack([own, block]).astype(jnp.int32)
    out = None
    for r in range(requests):
        rows = (r * per_source, per_source, group_size)
        common = (cache_len[r : r + 1], place, head_q, kv_blocks[r])
        fresh_r = (head_fresh[0, r], head_fresh[1, r])
        part = attend(*common, tuple(range(kv_heads)), fresh_r, None, True, *rows)
        part = lax.all_to_all(part, "seq", split_axis=0, concat_axis=0, tiled=True)
        part = part.reshape(spread, kv_heads, per_source + STAT_ROWS, head_dim)
        out = merge(part, r, requests, local_rows, group_size, out)
    return out


def solution(mesh):
    in_specs = (
        P("groups", "seq", None, None),
        P("groups", "seq", None, None),
        P("groups", "seq", None, None),
        P("groups", "seq", None, None),
        P("groups", "seq", None, None),
        P("groups"),
    )
    out_specs = P("groups", "seq", None, None)
    return jax.shard_map(attention, mesh=mesh, in_specs=in_specs, out_specs=out_specs, check_vma=False)
```

```python
import functools
import math

import jax
import jax.numpy as jnp
from jax import lax
from jax.experimental import pallas as pl
from jax.experimental.pallas import tpu as pltpu
from jax.sharding import PartitionSpec as P


NEG = -1e30
STAT_ROWS = 8
SMALL_VMEM = 12 * 2**20
LARGE_VMEM = 56 * 2**20


VMEM_SPEC = pl.BlockSpec(memory_space=pltpu.VMEM)
HBM_SPEC = pl.BlockSpec(memory_space=pltpu.HBM)
SMEM_SPEC = pl.BlockSpec(memory_space=pltpu.SMEM)


def attend_kernel(*refs, order, blocks, tile, group_size, row_start, with_fresh, with_state, final):
    refs = list(refs)
    length_ref, place_ref, q_hbm = refs.pop(0), refs.pop(0), refs.pop(0)
    kv_refs = [refs.pop(0) for _ in order]
    if with_fresh:
        fk_ref, fv_ref = refs.pop(0), refs.pop(0)
    if with_state:
        acc_in, top_in = refs.pop(0), refs.pop(0)
    if final:
        out_hbm = refs.pop(0)
        out_ref, out_sem = refs.pop(), refs.pop()
    else:
        acc_out, top_out = refs.pop(0), refs.pop(0)
    q_ref, keys, loaded, vals, bias, s0, s1, m0, m1, in_sems, q_sem = refs
    per_source, dim = q_ref.shape[1:]
    block_slots = kv_refs[0].shape[1]
    chunk = bias.shape[0]
    slots = len(order) * block_slots
    chunks = slots // chunk
    fresh = fk_ref.shape[0] if with_fresh else 0
    rows = q_ref.shape[0] * per_source
    tiles = rows // tile
    span = tile // per_source
    ones = vals.shape[0] - dim
    scale = math.log2(math.e) / math.sqrt(dim)
    own, device_block = place_ref[0], place_ref[1]
    valid = jnp.clip(length_ref[0] - device_block * blocks * block_slots, 0, blocks * block_slots)
    fresh_shift = jnp.where(device_block == q_ref.shape[0] // blocks - 1, 0, -rows)

    held = sorted({k // 2 for k in order})
    absent = [c for c in range(blocks // 2) if c not in held]

    def rank_of(index):
        rank = index
        for c in absent:
            rank = rank - jnp.where((own // 2) ^ c < index, 1, 0)
        return rank

    value_copies = []
    copies = []
    for i, k in enumerate(order):
        first = rank_of((own // 2) ^ (k // 2)) * chunk + ((own % 2) ^ (k % 2)) * block_slots
        at = pl.ds(pl.multiple_of(first, block_slots), block_slots)
        value_copies.append(pltpu.make_async_copy(kv_refs[i].at[1], loaded.at[at, :], in_sems.at[i, 1]))
        copies.append(pltpu.make_async_copy(kv_refs[i].at[0], keys.at[at, :], in_sems.at[i, 0]))
    copies.append(pltpu.make_async_copy(q_hbm.at[:, row_start : row_start + per_source, :], q_ref, q_sem))
    for copy in value_copies + copies:
        copy.start()

    filled = jnp.int32(0)
    last_valid = jnp.int32(0)
    for c in held:
        left = valid - ((own // 2) ^ c) * chunk
        filled = filled + jnp.where(left > 0, 1, 0)
        last_valid = jnp.where((left > 0) & (left < chunk), left, last_valid)
    last_valid = jnp.where(last_valid == 0, chunk, last_valid)

    vals[dim:, :] = jnp.ones((ones, slots + fresh), jnp.bfloat16)
    if with_fresh:
        vals[:dim, slots:] = jnp.transpose(fv_ref[...])
    bias[...] = jnp.where(lax.broadcasted_iota(jnp.int32, bias.shape, 0) < last_valid, 0.0, NEG)
    for copy in copies + value_copies:
        copy.wait()

    def turn_values(count):
        for first in range(0, count * chunk, block_slots):
            vals[:dim, first : first + block_slots] = jnp.transpose(loaded[first : first + block_slots, :])

    def fold_max(scores, best):
        part = jnp.max(scores.reshape(-1, 8, tile), axis=0)
        return part if best is None else jnp.maximum(best, part)

    def score_chunk(t, j, count, s_ref, best):
        q = q_ref[pl.ds(t * span, span)].reshape(tile, dim)
        at = slice(j * chunk, (j + 1) * chunk) if j < count else slice(slots, slots + fresh)
        left_side = keys[at, :] if j < count else fk_ref[...]
        scores = lax.dot_general(left_side, q, (((1,), (1,)), ((), ())), preferred_element_type=jnp.float32)
        if j == count - 1:
            mask = bias[...]
            scores = scores + jnp.concatenate([mask] * (tile // mask.shape[1]), axis=1)
        elif j == count:
            token = (t * tile + lax.broadcasted_iota(jnp.int32, (1, tile), 1)) // group_size
            unit = lax.broadcasted_iota(jnp.int32, (fresh, 1), 0)
            scores = jnp.where(unit <= token + fresh_shift, scores, NEG)
        s_ref[at, :] = scores
        return fold_max(scores, best)

    def value_chunk(j, count, s_ref, top, acc):
        at = slice(j * chunk, (j + 1) * chunk) if j < count else slice(slots, slots + fresh)
        weights = jnp.exp2((s_ref[at, :] - top) * scale).astype(jnp.bfloat16)
        part = jnp.dot(vals[:, at], weights, preferred_element_type=jnp.float32)
        return part if acc is None else acc + part

    def finish(t, top, acc):
        total = acc[dim : dim + 1, :]
        out = (acc[:dim, :] * (1.0 / total)).astype(jnp.bfloat16)
        level = top * scale + jnp.log2(total)
        high = level.astype(jnp.bfloat16).astype(jnp.float32)
        mid = (level - high).astype(jnp.bfloat16).astype(jnp.float32)
        low = level - high - mid
        which = lax.broadcasted_iota(jnp.int32, (STAT_ROWS, tile), 0)
        stats = jnp.where(which == 0, high, jnp.where(which == 1, mid, low)).astype(jnp.bfloat16)
        for first in range(0, tile, dim):
            flat = jnp.transpose(out[:, first : first + dim])
            width = min(per_source, dim)
            for part in range(dim // width):
                source = t * span + (first + part * width) // per_source
                inside = (first + part * width) % per_source
                out_ref[source, inside : inside + width, :] = flat[part * width : (part + 1) * width, :]
                out_ref[source, per_source:, inside : inside + width] = stats[
                    :, first + part * width : first + (part + 1) * width
                ]

    def stage(t_next, s_next, m_next, t_now, s_now, m_now, count):
        pieces = count + (1 if with_fresh else 0)
        best = None
        acc = None
        if t_now is not None:
            at = pl.ds(pl.multiple_of(t_now * tile, tile), tile)
            top = jnp.max(m_now[...], axis=0, keepdims=True) if pieces else None
            if with_state:
                before = top_in[:, at][:1]
                top = before if top is None else jnp.maximum(top, before)
                acc = acc_in[:, at] * jnp.exp2((before - top) * scale)
        for j in range(pieces):
            if t_next is not None:
                best = score_chunk(t_next, j, count, s_next, best)
            if t_now is not None:
                acc = value_chunk(j, count, s_now, top, acc)
        if t_next is not None and pieces:
            m_next[...] = best
        if t_now is not None:
            if final:
                finish(t_now, top, acc)
            else:
                acc_out[:, at] = acc
                top_out[:, at] = jnp.broadcast_to(top, (8, tile))

    for count in range(chunks + 1):

        @pl.when(filled == count)
        def _(count=count):
            stage(0, s0, m0, None, None, None, count)
            turn_values(count)

            def pair(i, carry):
                stage(2 * i + 1, s1, m1, 2 * i, s0, m0, count)
                stage(jnp.minimum(2 * i + 2, tiles - 1), s0, m0, 2 * i + 1, s1, m1, count)
                return carry

            lax.fori_loop(0, tiles // 2, pair, 0)

    if final:
        result = pltpu.make_async_copy(out_ref, out_hbm, out_sem)
        result.start()
        result.wait()


def attend(length, place, head_q, kv_blocks, order, fresh, state, final, row_start, row_count, group_size):
    sources, _, dim = head_q.shape
    slots = len(order) * kv_blocks[0].shape[1]
    rows = sources * row_count
    units = 0 if fresh is None else fresh[0].shape[0]
    tile = min(256, rows // 2)
    chunk = 2 * kv_blocks[0].shape[1]
    depth = dim + 16
    operands = [length, place, head_q] + [kv_blocks[k] for k in order]
    in_specs = [SMEM_SPEC] * 2 + [HBM_SPEC] * (1 + len(order))
    scratch = [
        pltpu.VMEM((sources, row_count, dim), jnp.bfloat16),
        pltpu.VMEM((slots, dim), jnp.bfloat16),
        pltpu.VMEM((slots, dim), jnp.bfloat16),
        pltpu.VMEM((depth, slots + units), jnp.bfloat16),
        pltpu.VMEM((chunk, min(dim, tile)), jnp.float32),
        pltpu.VMEM((slots + units, tile), jnp.float32),
        pltpu.VMEM((slots + units, tile), jnp.float32),
        pltpu.VMEM((8, tile), jnp.float32),
        pltpu.VMEM((8, tile), jnp.float32),
        pltpu.SemaphoreType.DMA((len(order), 2)),
        pltpu.SemaphoreType.DMA,
    ]
    if fresh is not None:
        operands += list(fresh)
        in_specs += [VMEM_SPEC] * 2
    if state is not None:
        operands += list(state)
        in_specs += [VMEM_SPEC] * 2
    if final:
        out_shape = jax.ShapeDtypeStruct((sources, row_count + STAT_ROWS, dim), jnp.bfloat16)
        out_specs = HBM_SPEC
        scratch += [pltpu.SemaphoreType.DMA, pltpu.VMEM(out_shape.shape, jnp.bfloat16)]
    else:
        out_shape = [
            jax.ShapeDtypeStruct((depth, rows), jnp.float32),
            jax.ShapeDtypeStruct((8, rows), jnp.float32),
        ]
        out_specs = [VMEM_SPEC] * 2
    grant = 8 * tile * (slots + units) + 8 * slots * dim + 12 * rows * dim + SMALL_VMEM
    return pl.pallas_call(
        functools.partial(
            attend_kernel,
            order=order,
            blocks=len(kv_blocks),
            tile=tile,
            group_size=group_size,
            row_start=row_start,
            with_fresh=fresh is not None,
            with_state=state is not None,
            final=final,
        ),
        in_specs=in_specs,
        out_specs=out_specs,
        scratch_shapes=scratch,
        out_shape=out_shape,
        compiler_params=pltpu.CompilerParams(vmem_limit_bytes=grant),
        cost_estimate=pl.CostEstimate(
            flops=4 * rows * slots * dim,
            bytes_accessed=4 * slots * dim + 4 * rows * dim,
            transcendentals=rows * slots,
        ),
    )(*operands)


def merge_kernel(part_ref, *refs, group_size):
    out_ref = refs[-1]
    spread, heads, _, dim = part_ref.shape
    local_rows = out_ref.shape[1]
    per_source = local_rows * group_size
    levels = []
    for b in range(spread):
        stats = [
            part_ref[b, h, per_source : per_source + STAT_ROWS, :].astype(jnp.float32) for h in range(heads)
        ]
        levels.append(jnp.concatenate([x[0:1] + x[1:2] + x[2:3] for x in stats], axis=0))
    top = functools.reduce(jnp.maximum, levels)
    weights = [jnp.exp2(level - top) for level in levels]
    total = functools.reduce(jnp.add, weights)
    weights = [jnp.transpose(w / total) for w in weights]
    for h in range(heads):
        mixed = functools.reduce(
            jnp.add,
            [
                w[:per_source, h : h + 1] * part_ref[b, h, :per_source, :].astype(jnp.float32)
                for b, w in enumerate(weights)
            ],
        ).astype(jnp.bfloat16)
        out_ref[0, :, h * group_size : (h + 1) * group_size, :] = mixed.reshape(local_rows, group_size, dim)


def merge(parts, request, requests, local_rows, group_size, earlier):
    heads, dim = parts.shape[1], parts.shape[3]
    rest = [] if earlier is None else [earlier]
    return pl.pallas_call(
        functools.partial(merge_kernel, group_size=group_size),
        grid=(1,),
        in_specs=[pl.BlockSpec(parts.shape, lambda i: (0, 0, 0, 0))]
        + [pl.BlockSpec(memory_space=pl.ANY) for _ in rest],
        out_specs=pl.BlockSpec((1, local_rows, heads * group_size, dim), lambda i: (request, 0, 0, 0)),
        out_shape=jax.ShapeDtypeStruct((requests, local_rows, heads * group_size, dim), jnp.bfloat16),
        input_output_aliases={1: 0} if rest else {},
        compiler_params=pltpu.CompilerParams(vmem_limit_bytes=SMALL_VMEM),
    )(parts, *rest)


def pack_kernel(q_ref, fresh_ref, out_ref):
    requests, local_rows, heads, dim = q_ref.shape
    kv_heads = fresh_ref.shape[0]
    group_size = heads // kv_heads
    rows = requests * local_rows * group_size
    for d in range(out_ref.shape[0]):
        head = d % kv_heads
        out_ref[d, :rows, :] = q_ref[:, :, head * group_size : (head + 1) * group_size, :].reshape(rows, dim)
        out_ref[d, rows:, :] = fresh_ref[head]


def pack(queries, fresh, devices):
    requests, local_rows, heads, dim = queries.shape
    rows = requests * local_rows * (heads // fresh.shape[0]) + fresh.shape[1]
    return pl.pallas_call(
        pack_kernel,
        in_specs=[VMEM_SPEC, VMEM_SPEC],
        out_specs=VMEM_SPEC,
        out_shape=jax.ShapeDtypeStruct((devices, rows, dim), jnp.bfloat16),
        compiler_params=pltpu.CompilerParams(vmem_limit_bytes=SMALL_VMEM),
    )(queries, fresh)


def split_kernel(own_ref, k_hbm, v_hbm, *refs, request):
    loaded, held, sems = refs[-3:]
    copies = [
        pltpu.make_async_copy(hbm.at[request], loaded.at[i], sems.at[i]) for i, hbm in enumerate((k_hbm, v_hbm))
    ]
    for copy in copies:
        copy.start()
    for i, copy in enumerate(copies):
        copy.wait()
        held[:, i] = jnp.swapaxes(loaded[i], 0, 1)
    for k, out_ref in enumerate(refs[:-3]):
        out_ref[...] = held[own_ref[0] ^ k]


def split_heads(own, cache_k, cache_v, request, grant):
    _, slots, kv_heads, dim = cache_k.shape
    return pl.pallas_call(
        functools.partial(split_kernel, request=request),
        in_specs=[SMEM_SPEC, HBM_SPEC, HBM_SPEC],
        out_specs=[VMEM_SPEC] * kv_heads,
        out_shape=[jax.ShapeDtypeStruct((2, slots, dim), jnp.bfloat16)] * kv_heads,
        scratch_shapes=[
            pltpu.VMEM((2, slots, kv_heads, dim), jnp.bfloat16),
            pltpu.VMEM((kv_heads, 2, slots, dim), jnp.bfloat16),
            pltpu.SemaphoreType.DMA((2,)),
        ],
        compiler_params=pltpu.CompilerParams(vmem_limit_bytes=grant),
    )(own, cache_k, cache_v)


def attention(queries, new_k, new_v, cache_k, cache_v, cache_len):
    requests, local_rows, heads, head_dim = queries.shape
    kv_heads = cache_k.shape[2]
    group_size = heads // kv_heads
    devices_seq = lax.axis_size("seq")
    seq_index = lax.axis_index("seq")
    spread = devices_seq // kv_heads
    block = seq_index // kv_heads
    own = (seq_index % kv_heads).astype(jnp.int32)
    per_source = local_rows * group_size

    fresh = jnp.transpose(jnp.stack([new_k, new_v]), (3, 0, 1, 2, 4)).reshape(
        kv_heads, 2 * requests * local_rows, head_dim
    )
    head_q = lax.all_to_all(
        pack(queries, fresh, devices_seq), "seq", split_axis=0, concat_axis=0, tiled=True
    )
    head_fresh = head_q[:, requests * per_source :, :].reshape(
        devices_seq, 2, requests, local_rows, head_dim
    )
    head_fresh = jnp.transpose(head_fresh, (1, 2, 0, 3, 4)).reshape(
        2, requests, devices_seq * local_rows, head_dim
    )

    kv_blocks = []
    for r in range(requests):
        parts = split_heads(own[None], cache_k, cache_v, r, LARGE_VMEM if r == 0 else 2 * SMALL_VMEM)
        moved = [parts[0]]
        for k in range(1, kv_heads):
            moved.append(lax.ppermute(parts[k], "seq", [(i, i ^ k) for i in range(devices_seq)]))
        kv_blocks.append(moved)

    place = jnp.stack([own, block]).astype(jnp.int32)
    out = None
    for r in range(requests):
        rows = (r * per_source, per_source, group_size)
        common = (cache_len[r : r + 1], place, head_q, kv_blocks[r])
        fresh_r = (head_fresh[0, r], head_fresh[1, r])
        state, first = None, 0
        if r == requests - 1:
            first = kv_heads - 2
            state = attend(*common, tuple(range(first)), fresh_r, None, False, *rows)
            fresh_r = None
        part = attend(*common, tuple(range(first, kv_heads)), fresh_r, state, True, *rows)
        part = lax.all_to_all(part, "seq", split_axis=0, concat_axis=0, tiled=True)
        part = part.reshape(spread, kv_heads, per_source + STAT_ROWS, head_dim)
        out = merge(part, r, requests, local_rows, group_size, out)
    return out


def solution(mesh):
    in_specs = (
        P("groups", "seq", None, None),
        P("groups", "seq", None, None),
        P("groups", "seq", None, None),
        P("groups", "seq", None, None),
        P("groups", "seq", None, None),
        P("groups"),
    )
    out_specs = P("groups", "seq", None, None)
    return jax.shard_map(attention, mesh=mesh, in_specs=in_specs, out_specs=out_specs, check_vma=False)
```

```python
import functools
import math

import jax
import jax.numpy as jnp
from jax import lax
from jax.experimental import pallas as pl
from jax.experimental.pallas import tpu as pltpu
from jax.sharding import PartitionSpec as P


NEG = -1e30
STAT_ROWS = 8
SMALL_VMEM = 12 * 2**20
LARGE_VMEM = 56 * 2**20


VMEM_SPEC = pl.BlockSpec(memory_space=pltpu.VMEM)
HBM_SPEC = pl.BlockSpec(memory_space=pltpu.HBM)
SMEM_SPEC = pl.BlockSpec(memory_space=pltpu.SMEM)


def attend_kernel(*refs, order, blocks, tile, group_size, row_start, with_fresh, with_state, final):
    refs = list(refs)
    length_ref, place_ref, q_hbm = refs.pop(0), refs.pop(0), refs.pop(0)
    kv_refs = [refs.pop(0) for _ in order]
    if with_fresh:
        fk_ref, fv_ref = refs.pop(0), refs.pop(0)
    if with_state:
        acc_in, top_in = refs.pop(0), refs.pop(0)
    if final:
        out_hbm = refs.pop(0)
        out_ref, out_sem = refs.pop(), refs.pop()
    else:
        acc_out, top_out = refs.pop(0), refs.pop(0)
    q_ref, keys, loaded, vals, bias, s0, s1, m0, m1, in_sems, q_sem = refs
    per_source, dim = q_ref.shape[1:]
    block_slots = kv_refs[0].shape[1]
    chunk = bias.shape[0]
    slots = len(order) * block_slots
    chunks = slots // chunk
    fresh = fk_ref.shape[0] if with_fresh else 0
    rows = q_ref.shape[0] * per_source
    tiles = rows // tile
    span = tile // per_source
    ones = vals.shape[0] - dim
    scale = math.log2(math.e) / math.sqrt(dim)
    own, device_block = place_ref[0], place_ref[1]
    valid = jnp.clip(length_ref[0] - device_block * blocks * block_slots, 0, blocks * block_slots)
    fresh_shift = jnp.where(device_block == q_ref.shape[0] // blocks - 1, 0, -rows)

    held = sorted({k // 2 for k in order})
    absent = [c for c in range(blocks // 2) if c not in held]

    def rank_of(index):
        rank = index
        for c in absent:
            rank = rank - jnp.where((own // 2) ^ c < index, 1, 0)
        return rank

    value_copies = []
    copies = []
    for i, k in enumerate(order):
        first = rank_of((own // 2) ^ (k // 2)) * chunk + ((own % 2) ^ (k % 2)) * block_slots
        at = pl.ds(pl.multiple_of(first, block_slots), block_slots)
        value_copies.append(pltpu.make_async_copy(kv_refs[i].at[1], loaded.at[at, :], in_sems.at[i, 1]))
        copies.append(pltpu.make_async_copy(kv_refs[i].at[0], keys.at[at, :], in_sems.at[i, 0]))
    copies.append(pltpu.make_async_copy(q_hbm.at[:, row_start : row_start + per_source, :], q_ref, q_sem))
    for copy in value_copies + copies:
        copy.start()

    filled = jnp.int32(0)
    last_valid = jnp.int32(0)
    for c in held:
        left = valid - ((own // 2) ^ c) * chunk
        filled = filled + jnp.where(left > 0, 1, 0)
        last_valid = jnp.where((left > 0) & (left < chunk), left, last_valid)
    last_valid = jnp.where(last_valid == 0, chunk, last_valid)

    vals[dim:, :] = jnp.ones((ones, slots + fresh), jnp.bfloat16)
    if with_fresh:
        vals[:dim, slots:] = jnp.transpose(fv_ref[...])
    bias[...] = jnp.where(lax.broadcasted_iota(jnp.int32, bias.shape, 0) < last_valid, 0.0, NEG)
    for copy in copies + value_copies:
        copy.wait()

    def turn_values(count):
        for first in range(0, count * chunk, block_slots):
            vals[:dim, first : first + block_slots] = jnp.transpose(loaded[first : first + block_slots, :])

    def fold_max(scores, best):
        part = jnp.max(scores.reshape(-1, 8, tile), axis=0)
        return part if best is None else jnp.maximum(best, part)

    def score_chunk(t, j, count, s_ref, best):
        q = q_ref[pl.ds(t * span, span)].reshape(tile, dim)
        at = slice(j * chunk, (j + 1) * chunk) if j < count else slice(slots, slots + fresh)
        left_side = keys[at, :] if j < count else fk_ref[...]
        scores = lax.dot_general(left_side, q, (((1,), (1,)), ((), ())), preferred_element_type=jnp.float32)
        if j == count - 1:
            mask = bias[...]
            scores = scores + jnp.concatenate([mask] * (tile // mask.shape[1]), axis=1)
        elif j == count:
            token = (t * tile + lax.broadcasted_iota(jnp.int32, (1, tile), 1)) // group_size
            unit = lax.broadcasted_iota(jnp.int32, (fresh, 1), 0)
            scores = jnp.where(unit <= token + fresh_shift, scores, NEG)
        s_ref[at, :] = scores
        return fold_max(scores, best)

    def value_chunk(j, count, s_ref, top, acc):
        at = slice(j * chunk, (j + 1) * chunk) if j < count else slice(slots, slots + fresh)
        weights = jnp.exp2((s_ref[at, :] - top) * scale).astype(jnp.bfloat16)
        part = jnp.dot(vals[:, at], weights, preferred_element_type=jnp.float32)
        return part if acc is None else acc + part

    def finish(t, top, acc):
        total = acc[dim : dim + 1, :]
        out = (acc[:dim, :] * (1.0 / total)).astype(jnp.bfloat16)
        level = top * scale + jnp.log2(total)
        high = level.astype(jnp.bfloat16).astype(jnp.float32)
        mid = (level - high).astype(jnp.bfloat16).astype(jnp.float32)
        low = level - high - mid
        which = lax.broadcasted_iota(jnp.int32, (STAT_ROWS, tile), 0)
        stats = jnp.where(which == 0, high, jnp.where(which == 1, mid, low)).astype(jnp.bfloat16)
        for first in range(0, tile, dim):
            flat = jnp.transpose(out[:, first : first + dim])
            width = min(per_source, dim)
            for part in range(dim // width):
                source = t * span + (first + part * width) // per_source
                inside = (first + part * width) % per_source
                out_ref[source, inside : inside + width, :] = flat[part * width : (part + 1) * width, :]
                out_ref[source, per_source:, inside : inside + width] = stats[
                    :, first + part * width : first + (part + 1) * width
                ]

    def stage(t_next, s_next, m_next, t_now, s_now, m_now, count):
        pieces = count + (1 if with_fresh else 0)
        best = None
        acc = None
        if t_now is not None:
            at = pl.ds(pl.multiple_of(t_now * tile, tile), tile)
            top = jnp.max(m_now[...], axis=0, keepdims=True) if pieces else None
            if with_state:
                before = top_in[:, at][:1]
                top = before if top is None else jnp.maximum(top, before)
                acc = acc_in[:, at] * jnp.exp2((before - top) * scale)
        for j in range(pieces):
            if t_next is not None:
                best = score_chunk(t_next, j, count, s_next, best)
            if t_now is not None:
                acc = value_chunk(j, count, s_now, top, acc)
        if t_next is not None and pieces:
            m_next[...] = best
        if t_now is not None:
            if final:
                finish(t_now, top, acc)
            else:
                acc_out[:, at] = acc
                top_out[:, at] = jnp.broadcast_to(top, (8, tile))

    for count in range(chunks + 1):

        @pl.when(filled == count)
        def _(count=count):
            stage(0, s0, m0, None, None, None, count)
            turn_values(count)

            def pair(i, carry):
                stage(2 * i + 1, s1, m1, 2 * i, s0, m0, count)
                stage(2 * i + 2, s0, m0, 2 * i + 1, s1, m1, count)
                return carry

            lax.fori_loop(0, tiles // 2 - 1, pair, 0)
            last = jnp.int32(tiles - 1)
            stage(last, s1, m1, last - 1, s0, m0, count)
            stage(None, None, None, last, s1, m1, count)

    if final:
        result = pltpu.make_async_copy(out_ref, out_hbm, out_sem)
        result.start()
        result.wait()


def attend(length, place, head_q, kv_blocks, order, fresh, state, final, row_start, row_count, group_size):
    sources, _, dim = head_q.shape
    slots = len(order) * kv_blocks[0].shape[1]
    rows = sources * row_count
    units = 0 if fresh is None else fresh[0].shape[0]
    tile = min(256, rows // 2)
    chunk = 2 * kv_blocks[0].shape[1]
    depth = dim + 16
    operands = [length, place, head_q] + [kv_blocks[k] for k in order]
    in_specs = [SMEM_SPEC] * 2 + [HBM_SPEC] * (1 + len(order))
    scratch = [
        pltpu.VMEM((sources, row_count, dim), jnp.bfloat16),
        pltpu.VMEM((slots, dim), jnp.bfloat16),
        pltpu.VMEM((slots, dim), jnp.bfloat16),
        pltpu.VMEM((depth, slots + units), jnp.bfloat16),
        pltpu.VMEM((chunk, min(dim, tile)), jnp.float32),
        pltpu.VMEM((slots + units, tile), jnp.float32),
        pltpu.VMEM((slots + units, tile), jnp.float32),
        pltpu.VMEM((8, tile), jnp.float32),
        pltpu.VMEM((8, tile), jnp.float32),
        pltpu.SemaphoreType.DMA((len(order), 2)),
        pltpu.SemaphoreType.DMA,
    ]
    if fresh is not None:
        operands += list(fresh)
        in_specs += [VMEM_SPEC] * 2
    if state is not None:
        operands += list(state)
        in_specs += [VMEM_SPEC] * 2
    if final:
        out_shape = jax.ShapeDtypeStruct((sources, row_count + STAT_ROWS, dim), jnp.bfloat16)
        out_specs = HBM_SPEC
        scratch += [pltpu.SemaphoreType.DMA, pltpu.VMEM(out_shape.shape, jnp.bfloat16)]
    else:
        out_shape = [
            jax.ShapeDtypeStruct((depth, rows), jnp.float32),
            jax.ShapeDtypeStruct((8, rows), jnp.float32),
        ]
        out_specs = [VMEM_SPEC] * 2
    grant = 8 * tile * (slots + units) + 8 * slots * dim + 12 * rows * dim + SMALL_VMEM
    return pl.pallas_call(
        functools.partial(
            attend_kernel,
            order=order,
            blocks=len(kv_blocks),
            tile=tile,
            group_size=group_size,
            row_start=row_start,
            with_fresh=fresh is not None,
            with_state=state is not None,
            final=final,
        ),
        in_specs=in_specs,
        out_specs=out_specs,
        scratch_shapes=scratch,
        out_shape=out_shape,
        compiler_params=pltpu.CompilerParams(vmem_limit_bytes=grant),
        cost_estimate=pl.CostEstimate(
            flops=4 * rows * slots * dim,
            bytes_accessed=4 * slots * dim + 4 * rows * dim,
            transcendentals=rows * slots,
        ),
    )(*operands)


def merge_kernel(part_ref, *refs, group_size):
    out_ref = refs[-1]
    spread, heads, _, dim = part_ref.shape
    local_rows = out_ref.shape[1]
    per_source = local_rows * group_size
    levels = []
    for b in range(spread):
        stats = [
            part_ref[b, h, per_source : per_source + STAT_ROWS, :].astype(jnp.float32) for h in range(heads)
        ]
        levels.append(jnp.concatenate([x[0:1] + x[1:2] + x[2:3] for x in stats], axis=0))
    top = functools.reduce(jnp.maximum, levels)
    weights = [jnp.exp2(level - top) for level in levels]
    total = functools.reduce(jnp.add, weights)
    weights = [jnp.transpose(w / total) for w in weights]
    for h in range(heads):
        mixed = functools.reduce(
            jnp.add,
            [
                w[:per_source, h : h + 1] * part_ref[b, h, :per_source, :].astype(jnp.float32)
                for b, w in enumerate(weights)
            ],
        ).astype(jnp.bfloat16)
        out_ref[0, :, h * group_size : (h + 1) * group_size, :] = mixed.reshape(local_rows, group_size, dim)


def merge(parts, request, requests, local_rows, group_size, earlier):
    heads, dim = parts.shape[1], parts.shape[3]
    rest = [] if earlier is None else [earlier]
    return pl.pallas_call(
        functools.partial(merge_kernel, group_size=group_size),
        grid=(1,),
        in_specs=[pl.BlockSpec(parts.shape, lambda i: (0, 0, 0, 0))]
        + [pl.BlockSpec(memory_space=pl.ANY) for _ in rest],
        out_specs=pl.BlockSpec((1, local_rows, heads * group_size, dim), lambda i: (request, 0, 0, 0)),
        out_shape=jax.ShapeDtypeStruct((requests, local_rows, heads * group_size, dim), jnp.bfloat16),
        input_output_aliases={1: 0} if rest else {},
        compiler_params=pltpu.CompilerParams(vmem_limit_bytes=SMALL_VMEM),
    )(parts, *rest)


def pack_kernel(q_ref, k_ref, v_ref, out_ref):
    requests, local_rows, heads, dim = q_ref.shape
    kv_heads = k_ref.shape[2]
    group_size = heads // kv_heads
    rows = requests * local_rows * group_size
    units = requests * local_rows
    fresh = [jnp.swapaxes(ref[...].reshape(units, kv_heads, dim), 0, 1) for ref in (k_ref, v_ref)]
    for d in range(out_ref.shape[0]):
        head = d % kv_heads
        out_ref[d, :rows, :] = q_ref[:, :, head * group_size : (head + 1) * group_size, :].reshape(rows, dim)
        out_ref[d, rows : rows + units, :] = fresh[0][head]
        out_ref[d, rows + units :, :] = fresh[1][head]


def pack(queries, new_k, new_v, devices):
    requests, local_rows, heads, dim = queries.shape
    kv_heads = new_k.shape[2]
    rows = requests * local_rows * (heads // kv_heads + 2)
    return pl.pallas_call(
        pack_kernel,
        in_specs=[VMEM_SPEC] * 3,
        out_specs=VMEM_SPEC,
        out_shape=jax.ShapeDtypeStruct((devices, rows, dim), jnp.bfloat16),
        compiler_params=pltpu.CompilerParams(vmem_limit_bytes=SMALL_VMEM),
    )(queries, new_k, new_v)


def split_kernel(own_ref, k_hbm, v_hbm, *refs, request):
    loaded, held, sems = refs[-3:]
    copies = [
        pltpu.make_async_copy(hbm.at[request], loaded.at[i], sems.at[i]) for i, hbm in enumerate((k_hbm, v_hbm))
    ]
    for copy in copies:
        copy.start()
    for i, copy in enumerate(copies):
        copy.wait()
        held[:, i] = jnp.swapaxes(loaded[i], 0, 1)
    for k, out_ref in enumerate(refs[:-3]):
        out_ref[...] = held[own_ref[0] ^ k]


def split_heads(own, cache_k, cache_v, request, grant):
    _, slots, kv_heads, dim = cache_k.shape
    return pl.pallas_call(
        functools.partial(split_kernel, request=request),
        in_specs=[SMEM_SPEC, HBM_SPEC, HBM_SPEC],
        out_specs=[VMEM_SPEC] * kv_heads,
        out_shape=[jax.ShapeDtypeStruct((2, slots, dim), jnp.bfloat16)] * kv_heads,
        scratch_shapes=[
            pltpu.VMEM((2, slots, kv_heads, dim), jnp.bfloat16),
            pltpu.VMEM((kv_heads, 2, slots, dim), jnp.bfloat16),
            pltpu.SemaphoreType.DMA((2,)),
        ],
        compiler_params=pltpu.CompilerParams(vmem_limit_bytes=grant),
    )(own, cache_k, cache_v)


def attention(queries, new_k, new_v, cache_k, cache_v, cache_len):
    requests, local_rows, heads, head_dim = queries.shape
    kv_heads = cache_k.shape[2]
    group_size = heads // kv_heads
    devices_seq = lax.axis_size("seq")
    seq_index = lax.axis_index("seq")
    spread = devices_seq // kv_heads
    block = seq_index // kv_heads
    own = (seq_index % kv_heads).astype(jnp.int32)
    per_source = local_rows * group_size

    head_q = lax.all_to_all(pack(queries, new_k, new_v, devices_seq), "seq", split_axis=0, concat_axis=0, tiled=True)
    head_fresh = head_q[:, requests * per_source :, :].reshape(
        devices_seq, 2, requests, local_rows, head_dim
    )
    head_fresh = jnp.transpose(head_fresh, (1, 2, 0, 3, 4)).reshape(
        2, requests, devices_seq * local_rows, head_dim
    )

    kv_blocks = []
    for r in range(requests):
        parts = split_heads(own[None], cache_k, cache_v, r, LARGE_VMEM if r == 0 else 2 * SMALL_VMEM)
        moved = [parts[0]]
        for k in range(1, kv_heads):
            moved.append(lax.ppermute(parts[k], "seq", [(i, i ^ k) for i in range(devices_seq)]))
        kv_blocks.append(moved)

    place = jnp.stack([own, block]).astype(jnp.int32)
    out = None
    for r in range(requests):
        rows = (r * per_source, per_source, group_size)
        common = (cache_len[r : r + 1], place, head_q, kv_blocks[r])
        fresh_r = (head_fresh[0, r], head_fresh[1, r])
        first = kv_heads - 2
        state = attend(*common, tuple(range(first)), fresh_r, None, False, *rows)
        part = attend(*common, tuple(range(first, kv_heads)), None, state, True, *rows)
        part = lax.all_to_all(part, "seq", split_axis=0, concat_axis=0, tiled=True)
        part = part.reshape(spread, kv_heads, per_source + STAT_ROWS, head_dim)
        out = merge(part, r, requests, local_rows, group_size, out)
    return out


def solution(mesh):
    in_specs = (
        P("groups", "seq", None, None),
        P("groups", "seq", None, None),
        P("groups", "seq", None, None),
        P("groups", "seq", None, None),
        P("groups", "seq", None, None),
        P("groups"),
    )
    out_specs = P("groups", "seq", None, None)
    return jax.shard_map(attention, mesh=mesh, in_specs=in_specs, out_specs=out_specs, check_vma=False)
```

```python
import functools
import math

import jax
import jax.numpy as jnp
from jax import lax
from jax.experimental import pallas as pl
from jax.experimental.pallas import tpu as pltpu
from jax.sharding import PartitionSpec as P


NEG = -1e30
STAT_ROWS = 8
SMALL_VMEM = 12 * 2**20
LARGE_VMEM = 56 * 2**20


VMEM_SPEC = pl.BlockSpec(memory_space=pltpu.VMEM)
HBM_SPEC = pl.BlockSpec(memory_space=pltpu.HBM)
SMEM_SPEC = pl.BlockSpec(memory_space=pltpu.SMEM)


def attend_kernel(*refs, order, blocks, tile, group_size, row_start, with_fresh, with_state, final):
    refs = list(refs)
    length_ref, place_ref, q_hbm = refs.pop(0), refs.pop(0), refs.pop(0)
    kv_refs = [refs.pop(0) for _ in order]
    if with_fresh:
        fk_ref, fv_ref = refs.pop(0), refs.pop(0)
    if with_state:
        acc_in, top_in = refs.pop(0), refs.pop(0)
    if final:
        out_hbm = refs.pop(0)
        out_ref, out_sem = refs.pop(), refs.pop()
    else:
        acc_out, top_out = refs.pop(0), refs.pop(0)
    q_ref, keys, loaded, vals, bias, s0, s1, m0, m1, in_sems, q_sem = refs
    per_source, dim = q_ref.shape[1:]
    block_slots = kv_refs[0].shape[1]
    chunk = bias.shape[0]
    slots = len(order) * block_slots
    chunks = slots // chunk
    fresh = fk_ref.shape[0] if with_fresh else 0
    rows = q_ref.shape[0] * per_source
    tiles = rows // tile
    span = tile // per_source
    ones = vals.shape[0] - dim
    scale = math.log2(math.e) / math.sqrt(dim)
    own, device_block = place_ref[0], place_ref[1]
    valid = jnp.clip(length_ref[0] - device_block * blocks * block_slots, 0, blocks * block_slots)
    fresh_shift = jnp.where(device_block == q_ref.shape[0] // blocks - 1, 0, -rows)

    held = sorted({k // 2 for k in order})
    absent = [c for c in range(blocks // 2) if c not in held]

    def rank_of(index):
        rank = index
        for c in absent:
            rank = rank - jnp.where((own // 2) ^ c < index, 1, 0)
        return rank

    value_copies = []
    copies = []
    for i, k in enumerate(order):
        first = rank_of((own // 2) ^ (k // 2)) * chunk + ((own % 2) ^ (k % 2)) * block_slots
        at = pl.ds(pl.multiple_of(first, block_slots), block_slots)
        value_copies.append(pltpu.make_async_copy(kv_refs[i].at[1], loaded.at[at, :], in_sems.at[i, 1]))
        copies.append(pltpu.make_async_copy(kv_refs[i].at[0], keys.at[at, :], in_sems.at[i, 0]))
    copies.append(pltpu.make_async_copy(q_hbm.at[:, row_start : row_start + per_source, :], q_ref, q_sem))
    for copy in value_copies + copies:
        copy.start()

    filled = jnp.int32(0)
    last_valid = jnp.int32(0)
    for c in held:
        left = valid - ((own // 2) ^ c) * chunk
        filled = filled + jnp.where(left > 0, 1, 0)
        last_valid = jnp.where((left > 0) & (left < chunk), left, last_valid)
    last_valid = jnp.where(last_valid == 0, chunk, last_valid)

    vals[dim:, :] = jnp.ones((ones, slots + fresh), jnp.bfloat16)
    if with_fresh:
        vals[:dim, slots:] = jnp.transpose(fv_ref[...])
    bias[...] = jnp.where(lax.broadcasted_iota(jnp.int32, bias.shape, 0) < last_valid, 0.0, NEG)
    for copy in copies + value_copies:
        copy.wait()

    def turn_values(count):
        for first in range(0, count * chunk, block_slots):
            vals[:dim, first : first + block_slots] = jnp.transpose(loaded[first : first + block_slots, :])

    def fold_max(scores, best):
        part = jnp.max(scores.reshape(-1, 8, tile), axis=0)
        return part if best is None else jnp.maximum(best, part)

    def score_chunk(t, j, count, s_ref, best):
        q = q_ref[pl.ds(t * span, span)].reshape(tile, dim)
        at = slice(j * chunk, (j + 1) * chunk) if j < count else slice(slots, slots + fresh)
        left_side = keys[at, :] if j < count else fk_ref[...]
        scores = lax.dot_general(left_side, q, (((1,), (1,)), ((), ())), preferred_element_type=jnp.float32)
        if j == count - 1:
            mask = bias[...]
            scores = scores + jnp.concatenate([mask] * (tile // mask.shape[1]), axis=1)
        elif j == count:
            token = (t * tile + lax.broadcasted_iota(jnp.int32, (1, tile), 1)) // group_size
            unit = lax.broadcasted_iota(jnp.int32, (fresh, 1), 0)
            scores = jnp.where(unit <= token + fresh_shift, scores, NEG)
        s_ref[at, :] = scores
        return fold_max(scores, best)

    def value_chunk(j, count, s_ref, top, acc):
        at = slice(j * chunk, (j + 1) * chunk) if j < count else slice(slots, slots + fresh)
        weights = jnp.exp2((s_ref[at, :] - top) * scale).astype(jnp.bfloat16)
        part = jnp.dot(vals[:, at], weights, preferred_element_type=jnp.float32)
        return part if acc is None else acc + part

    def finish(t, top, acc):
        total = acc[dim : dim + 1, :]
        out = (acc[:dim, :] * (1.0 / total)).astype(jnp.bfloat16)
        level = top * scale + jnp.log2(total)
        high = level.astype(jnp.bfloat16).astype(jnp.float32)
        mid = (level - high).astype(jnp.bfloat16).astype(jnp.float32)
        low = level - high - mid
        which = lax.broadcasted_iota(jnp.int32, (STAT_ROWS, tile), 0)
        stats = jnp.where(which == 0, high, jnp.where(which == 1, mid, low)).astype(jnp.bfloat16)
        for first in range(0, tile, dim):
            flat = jnp.transpose(out[:, first : first + dim])
            width = min(per_source, dim)
            for part in range(dim // width):
                source = t * span + (first + part * width) // per_source
                inside = (first + part * width) % per_source
                out_ref[source, inside : inside + width, :] = flat[part * width : (part + 1) * width, :]
                out_ref[source, per_source:, inside : inside + width] = stats[
                    :, first + part * width : first + (part + 1) * width
                ]

    def stage(t_next, s_next, m_next, t_now, s_now, m_now, count):
        pieces = count + (1 if with_fresh else 0)
        best = None
        acc = None
        if t_now is not None:
            at = pl.ds(pl.multiple_of(t_now * tile, tile), tile)
            top = jnp.max(m_now[...], axis=0, keepdims=True) if pieces else None
            if with_state:
                before = top_in[:, at][:1]
                top = before if top is None else jnp.maximum(top, before)
                acc = acc_in[:, at] * jnp.exp2((before - top) * scale)
        for j in range(pieces):
            if t_next is not None:
                best = score_chunk(t_next, j, count, s_next, best)
            if t_now is not None:
                acc = value_chunk(j, count, s_now, top, acc)
        if t_next is not None and pieces:
            m_next[...] = best
        if t_now is not None:
            if final:
                finish(t_now, top, acc)
            else:
                acc_out[:, at] = acc
                top_out[:, at] = jnp.broadcast_to(top, (8, tile))

    for count in range(chunks + 1):

        @pl.when(filled == count)
        def _(count=count):
            stage(0, s0, m0, None, None, None, count)
            turn_values(count)

            def pair(i, carry):
                stage(2 * i + 1, s1, m1, 2 * i, s0, m0, count)
                stage(2 * i + 2, s0, m0, 2 * i + 1, s1, m1, count)
                return carry

            lax.fori_loop(0, tiles // 2 - 1, pair, 0)
            last = jnp.int32(tiles - 1)
            stage(last, s1, m1, last - 1, s0, m0, count)
            stage(None, None, None, last, s1, m1, count)

    if final:
        result = pltpu.make_async_copy(out_ref, out_hbm, out_sem)
        result.start()
        result.wait()


def attend(length, place, head_q, kv_blocks, order, fresh, state, final, row_start, row_count, group_size):
    sources, _, dim = head_q.shape
    slots = len(order) * kv_blocks[0].shape[1]
    rows = sources * row_count
    units = 0 if fresh is None else fresh[0].shape[0]
    tile = min(256, rows // 2)
    chunk = 2 * kv_blocks[0].shape[1]
    depth = dim + 16
    operands = [length, place, head_q] + [kv_blocks[k] for k in order]
    in_specs = [SMEM_SPEC] * 2 + [HBM_SPEC] * (1 + len(order))
    scratch = [
        pltpu.VMEM((sources, row_count, dim), jnp.bfloat16),
        pltpu.VMEM((slots, dim), jnp.bfloat16),
        pltpu.VMEM((slots, dim), jnp.bfloat16),
        pltpu.VMEM((depth, slots + units), jnp.bfloat16),
        pltpu.VMEM((chunk, min(dim, tile)), jnp.float32),
        pltpu.VMEM((slots + units, tile), jnp.float32),
        pltpu.VMEM((slots + units, tile), jnp.float32),
        pltpu.VMEM((8, tile), jnp.float32),
        pltpu.VMEM((8, tile), jnp.float32),
        pltpu.SemaphoreType.DMA((len(order), 2)),
        pltpu.SemaphoreType.DMA,
    ]
    if fresh is not None:
        operands += list(fresh)
        in_specs += [VMEM_SPEC] * 2
    if state is not None:
        operands += list(state)
        in_specs += [VMEM_SPEC] * 2
    if final:
        out_shape = jax.ShapeDtypeStruct((sources, row_count + STAT_ROWS, dim), jnp.bfloat16)
        out_specs = HBM_SPEC
        scratch += [pltpu.SemaphoreType.DMA, pltpu.VMEM(out_shape.shape, jnp.bfloat16)]
    else:
        out_shape = [
            jax.ShapeDtypeStruct((depth, rows), jnp.float32),
            jax.ShapeDtypeStruct((8, rows), jnp.float32),
        ]
        out_specs = [VMEM_SPEC] * 2
    grant = 8 * tile * (slots + units) + 8 * slots * dim + 12 * rows * dim + SMALL_VMEM
    return pl.pallas_call(
        functools.partial(
            attend_kernel,
            order=order,
            blocks=len(kv_blocks),
            tile=tile,
            group_size=group_size,
            row_start=row_start,
            with_fresh=fresh is not None,
            with_state=state is not None,
            final=final,
        ),
        in_specs=in_specs,
        out_specs=out_specs,
        scratch_shapes=scratch,
        out_shape=out_shape,
        compiler_params=pltpu.CompilerParams(vmem_limit_bytes=grant),
        cost_estimate=pl.CostEstimate(
            flops=4 * rows * slots * dim,
            bytes_accessed=4 * slots * dim + 4 * rows * dim,
            transcendentals=rows * slots,
        ),
    )(*operands)


def merge_kernel(part_ref, *refs, group_size):
    out_ref = refs[-1]
    spread, heads, _, dim = part_ref.shape
    local_rows = out_ref.shape[1]
    per_source = local_rows * group_size
    levels = []
    for b in range(spread):
        stats = [
            part_ref[b, h, per_source : per_source + STAT_ROWS, :].astype(jnp.float32) for h in range(heads)
        ]
        levels.append(jnp.concatenate([x[0:1] + x[1:2] + x[2:3] for x in stats], axis=0))
    top = functools.reduce(jnp.maximum, levels)
    weights = [jnp.exp2(level - top) for level in levels]
    total = functools.reduce(jnp.add, weights)
    weights = [jnp.transpose(w / total) for w in weights]
    for h in range(heads):
        mixed = functools.reduce(
            jnp.add,
            [
                w[:per_source, h : h + 1] * part_ref[b, h, :per_source, :].astype(jnp.float32)
                for b, w in enumerate(weights)
            ],
        ).astype(jnp.bfloat16)
        out_ref[0, :, h * group_size : (h + 1) * group_size, :] = mixed.reshape(local_rows, group_size, dim)


def merge(parts, request, requests, local_rows, group_size, earlier):
    heads, dim = parts.shape[1], parts.shape[3]
    rest = [] if earlier is None else [earlier]
    return pl.pallas_call(
        functools.partial(merge_kernel, group_size=group_size),
        grid=(1,),
        in_specs=[pl.BlockSpec(parts.shape, lambda i: (0, 0, 0, 0))]
        + [pl.BlockSpec(memory_space=pl.ANY) for _ in rest],
        out_specs=pl.BlockSpec((1, local_rows, heads * group_size, dim), lambda i: (request, 0, 0, 0)),
        out_shape=jax.ShapeDtypeStruct((requests, local_rows, heads * group_size, dim), jnp.bfloat16),
        input_output_aliases={1: 0} if rest else {},
        compiler_params=pltpu.CompilerParams(vmem_limit_bytes=SMALL_VMEM),
    )(parts, *rest)


def pack_kernel(q_ref, k_ref, v_ref, out_ref):
    requests, local_rows, heads, dim = q_ref.shape
    kv_heads = k_ref.shape[2]
    group_size = heads // kv_heads
    rows = requests * local_rows * group_size
    units = requests * local_rows
    fresh = [jnp.swapaxes(ref[...].reshape(units, kv_heads, dim), 0, 1) for ref in (k_ref, v_ref)]
    for d in range(out_ref.shape[0]):
        head = d % kv_heads
        out_ref[d, :rows, :] = q_ref[:, :, head * group_size : (head + 1) * group_size, :].reshape(rows, dim)
        out_ref[d, rows : rows + units, :] = fresh[0][head]
        out_ref[d, rows + units :, :] = fresh[1][head]


def pack(queries, new_k, new_v, devices):
    requests, local_rows, heads, dim = queries.shape
    kv_heads = new_k.shape[2]
    rows = requests * local_rows * (heads // kv_heads + 2)
    return pl.pallas_call(
        pack_kernel,
        in_specs=[VMEM_SPEC] * 3,
        out_specs=VMEM_SPEC,
        out_shape=jax.ShapeDtypeStruct((devices, rows, dim), jnp.bfloat16),
        compiler_params=pltpu.CompilerParams(vmem_limit_bytes=SMALL_VMEM),
    )(queries, new_k, new_v)


def split_kernel(own_ref, k_hbm, v_hbm, *refs, request):
    loaded, held, sems = refs[-3:]
    copies = [
        pltpu.make_async_copy(hbm.at[request], loaded.at[i], sems.at[i]) for i, hbm in enumerate((k_hbm, v_hbm))
    ]
    for copy in copies:
        copy.start()
    for i, copy in enumerate(copies):
        copy.wait()
        held[:, i] = jnp.swapaxes(loaded[i], 0, 1)
    for k, out_ref in enumerate(refs[:-3]):
        out_ref[...] = held[own_ref[0] ^ k]


def split_heads(own, cache_k, cache_v, request, grant):
    _, slots, kv_heads, dim = cache_k.shape
    return pl.pallas_call(
        functools.partial(split_kernel, request=request),
        in_specs=[SMEM_SPEC, HBM_SPEC, HBM_SPEC],
        out_specs=[VMEM_SPEC] * kv_heads,
        out_shape=[jax.ShapeDtypeStruct((2, slots, dim), jnp.bfloat16)] * kv_heads,
        scratch_shapes=[
            pltpu.VMEM((2, slots, kv_heads, dim), jnp.bfloat16),
            pltpu.VMEM((kv_heads, 2, slots, dim), jnp.bfloat16),
            pltpu.SemaphoreType.DMA((2,)),
        ],
        compiler_params=pltpu.CompilerParams(vmem_limit_bytes=grant),
    )(own, cache_k, cache_v)


def attention(queries, new_k, new_v, cache_k, cache_v, cache_len):
    requests, local_rows, heads, head_dim = queries.shape
    kv_heads = cache_k.shape[2]
    group_size = heads // kv_heads
    devices_seq = lax.axis_size("seq")
    seq_index = lax.axis_index("seq")
    spread = devices_seq // kv_heads
    block = seq_index // kv_heads
    own = (seq_index % kv_heads).astype(jnp.int32)
    per_source = local_rows * group_size

    head_q = lax.all_to_all(pack(queries, new_k, new_v, devices_seq), "seq", split_axis=0, concat_axis=0, tiled=True)
    head_fresh = head_q[:, requests * per_source :, :].reshape(
        devices_seq, 2, requests, local_rows, head_dim
    )
    head_fresh = jnp.transpose(head_fresh, (1, 2, 0, 3, 4)).reshape(
        2, requests, devices_seq * local_rows, head_dim
    )

    kv_blocks = []
    for r in range(requests):
        parts = split_heads(own[None], cache_k, cache_v, r, LARGE_VMEM if r == 0 else 2 * SMALL_VMEM)
        moved = [parts[0]]
        for k in range(1, kv_heads):
            moved.append(lax.ppermute(parts[k], "seq", [(i, i ^ k) for i in range(devices_seq)]))
        kv_blocks.append(moved)

    place = jnp.stack([own, block]).astype(jnp.int32)
    out = None
    for r in range(requests):
        rows = (r * per_source, per_source, group_size)
        common = (cache_len[r : r + 1], place, head_q, kv_blocks[r])
        fresh_r = (head_fresh[0, r], head_fresh[1, r])
        state, first = None, 0
        part = attend(*common, tuple(range(first, kv_heads)), fresh_r, state, True, *rows)
        part = lax.all_to_all(part, "seq", split_axis=0, concat_axis=0, tiled=True)
        part = part.reshape(spread, kv_heads, per_source + STAT_ROWS, head_dim)
        out = merge(part, r, requests, local_rows, group_size, out)
    return out


def solution(mesh):
    in_specs = (
        P("groups", "seq", None, None),
        P("groups", "seq", None, None),
        P("groups", "seq", None, None),
        P("groups", "seq", None, None),
        P("groups", "seq", None, None),
        P("groups"),
    )
    out_specs = P("groups", "seq", None, None)
    return jax.shard_map(attention, mesh=mesh, in_specs=in_specs, out_specs=out_specs, check_vma=False)
```
